256 devices in a mesh: tile: 128 (over z, x_lo, y, core), ch: 2 (over x_hi).
Axes of the slice: x: 4 (x_hi: 2, x_lo: 2; x = x_hi * 2 + x_lo), y: 4, z: 8, core: 2. Of those that a mesh axis runs over, the one named last changes fastest.
Arguments:
- features: bfloat16 [128, 32, 32, 384], P('tile', None, None, 'ch'), may hold values from -6 to 6
- weight: bfloat16 [3, 3, 384, 384], replicated, may hold values from -0.109375 to 0.109375
- cotangent: bfloat16 [128, 32, 32, 384], P('tile', None, None, 'ch'), may hold values from -6 to 6
- edge_tiles: int32 [128, 4], replicated, may hold values from 0 to 127, as said below
- edge_turns: int32 [128, 4], replicated, may hold values from 0 to 3
- corner_tiles: int32 [128, 4], replicated, may hold values from 0 to 127, as said below
- corner_turns: int32 [128, 4], replicated, may hold values from 0 to 3
Outputs:
- output: bfloat16 [128, 32, 32, 384], P('tile', None, None, 'ch')
- grad_features: bfloat16 [128, 32, 32, 384], P('tile', None, None, 'ch')
- grad_weight: float32 [3, 3, 384, 384], P(None, None, 'ch')
The draws below stay inside these ranges and needn't reach their ends.
Inputs may be any that keep to these rules, and one draw needn't show every extreme that they name: (edge_tiles[t, e] - t) mod 128 lies in 1 .. 4 or in 124 .. 127; both distances 4 and -4 occur. (corner_tiles[t, c] - t) mod 128 lies in 1 .. 4 or in 124 .. 127; both distances 4 and -4 occur.
All inputs are finite; a program needn't handle non-finite values.
Results may differ from the reference program's by a relative error of at most 0.0029.
Values may be sent and summed in bfloat16 or wider, within the bound.
A program may use at most 64 MiB of HBM per device.

```python
import math
import jax
import jax.numpy as jnp
import numpy as np
from jax import lax

C = 384
S = 32
SPAN = 4
TILES = 128


def draw_near(key, salt):
    base_key = jax.random.fold_in(key, salt)
    distance = jax.random.randint(base_key, (TILES, 4), 1, SPAN + 1)
    direction = jax.random.randint(jax.random.fold_in(base_key, 7), (TILES, 4), 0, 2) * 2 - 1
    offset = distance * direction
    offset = offset.at[0, 0].set(SPAN).at[0, 1].set(-SPAN)
    return jnp.mod(jnp.arange(TILES, dtype=jnp.int32)[:, None] + offset, TILES).astype(jnp.int32)


def draw_edge_tiles(key, part):
    return draw_near(key, 11)


def draw_corner_tiles(key, part):
    return draw_near(key, 23)


def touch_ends(values, key, least, largest):
    longest = values.shape.index(max(values.shape))
    spots = []
    for shift in (0, 1):
        where = [jax.random.randint(jax.random.fold_in(key, axis), (), 0, length) for axis, length in enumerate(values.shape)]
        where[longest] = (where[longest] + shift) % values.shape[longest]
        spots.append(tuple(where))
    return values.at[spots[0]].set(least).at[spots[1]].set(largest)


def shard_levels(rng, extent, cuts, least, top_value):
    loudness = 1.0
    for position, blocks in cuts:
        steps = jax.random.uniform(jax.random.fold_in(jax.random.fold_in(rng, 6), position), (blocks,), jnp.float32, least / len(cuts), top_value / len(cuts))
        loudness = loudness * jnp.repeat(jnp.exp(steps), extent[position] // blocks).reshape((-1,) + (1,) * (len(extent) - 1 - position))
    return loudness


def noise(stream_key, dims, scale, limit, cuts=(), kind=jnp.bfloat16):
    entries = jax.random.normal(stream_key, dims, jnp.float32) * scale
    if len(cuts) > 0:
        entries = shard_levels(stream_key, dims, cuts, -0.22, 0.18) * entries
    return jnp.clip(entries, min=-limit, max=limit).astype(kind)


def setup_inputs(seed: int = 0) -> dict:
    key_list = jax.random.split(jax.random.key(seed), 8)
    return {
        "features": noise(key_list[0], (TILES, S, S, C), 1.0, 6.0, ((0, 128), (3, 2))),
        "weight": noise(key_list[1], (3, 3, C, C), (9 * C) ** -0.5, 0.109375),
        "cotangent": noise(key_list[2], (TILES, S, S, C), 1.0, 6.0, ((0, 128), (3, 2))),
        "edge_tiles": draw_edge_tiles(jax.random.fold_in(key_list[7], 71), 0),
        "edge_turns": touch_ends(jax.random.randint(key_list[4], (TILES, 4), 0, 4), jax.random.fold_in(key_list[4], 1), 0, 3).astype(jnp.int32),
        "corner_tiles": draw_corner_tiles(jax.random.fold_in(key_list[7], 71), 0),
        "corner_turns": touch_ends(jax.random.randint(key_list[6], (TILES, 4), 0, 4), jax.random.fold_in(key_list[6], 1), 0, 3).astype(jnp.int32),
    }


def turn_tables():
    labels = [[3 * row + col for col in range(3)] for row in range(3)]

    def turn_once(block):
        return [[block[col][2 - row] for col in range(3)] for row in range(3)]

    def sides_of(block):
        return [list(block[0]), [block[row][2] for row in range(3)], list(block[2]), [block[row][0] for row in range(3)]]

    def corners_of(block):
        return [block[0][0], block[0][2], block[2][2], block[2][0]]
    base_sides = sides_of(labels)
    base_corners = corners_of(labels)
    edge_table = np.zeros((4, 4), np.int32)
    corner_table = np.zeros((4, 4), np.int32)
    for border in range(4):
        turned = labels
        for quarter in range(4):
            wanted = sides_of(turned)[(border + 2) % 4]
            for side_index in range(4):
                if base_sides[side_index] == wanted:
                    edge_table[border, quarter] = side_index
                if base_sides[side_index][::-1] == wanted:
                    edge_table[border, quarter] = side_index + 4
            corner_cell = corners_of(turned)[(border + 2) % 4]
            for corner_index in range(4):
                if base_corners[corner_index] == corner_cell:
                    corner_table[border, quarter] = corner_index
            turned = turn_once(turned)
    return (edge_table, corner_table)

def rounded(values):
    return lax.optimization_barrier(values.astype(jnp.bfloat16)).astype(jnp.float32)

def reference(features, weight, cotangent, edge_tiles, edge_turns, corner_tiles, corner_turns):
    edge_table, corner_table = turn_tables()
    tile_count, side_len, _, chan_count = features.shape
    sides = jnp.stack([features[:, 0], features[:, :, -1], features[:, -1], features[:, :, 0]], axis=1)
    sides_both = jnp.concatenate([sides, sides[:, :, ::-1]], axis=1)
    corners = jnp.stack([features[:, 0, 0], features[:, 0, -1], features[:, -1, -1], features[:, -1, 0]], axis=1)
    edge_slots = [jnp.asarray(edge_table[border])[edge_turns[:, border]] for border in range(4)]
    corner_slots = [jnp.asarray(corner_table[border])[corner_turns[:, border]] for border in range(4)]
    halos = [sides_both[edge_tiles[:, border], edge_slots[border]] for border in range(4)]
    corner_halos = [corners[corner_tiles[:, border], corner_slots[border]] for border in range(4)]
    padded = jnp.pad(features, ((0, 0), (1, 1), (1, 1), (0, 0)))
    padded = padded.at[:, 0, 1:-1].set(halos[0]).at[:, 1:-1, -1].set(halos[1])
    padded = padded.at[:, -1, 1:-1].set(halos[2]).at[:, 1:-1, 0].set(halos[3])
    padded = padded.at[:, 0, 0].set(corner_halos[0]).at[:, 0, -1].set(corner_halos[1])
    padded = padded.at[:, -1, -1].set(corner_halos[2]).at[:, -1, 0].set(corner_halos[3])
    rows = tile_count * side_len * side_len
    cot_rows = cotangent.reshape(rows, chan_count)
    output = jnp.zeros((rows, chan_count), jnp.float32)
    grad_padded = jnp.zeros(padded.shape, jnp.float32)
    grads = []
    for row_off in range(3):
        for col_off in range(3):
            window = padded[:, row_off:row_off + side_len, col_off:col_off + side_len].reshape(rows, chan_count)
            output = output + jnp.dot(window, weight[row_off, col_off], preferred_element_type=jnp.float32)
            back = jnp.dot(cot_rows, weight[row_off, col_off].T, preferred_element_type=jnp.float32)
            grad_padded = grad_padded.at[:, row_off:row_off + side_len, col_off:col_off + side_len].add(back.reshape(tile_count, side_len, side_len, chan_count))
            grads.append(jnp.dot(window.T, cot_rows, preferred_element_type=jnp.float32))
    grad_weight = jnp.stack(grads).reshape(3, 3, chan_count, chan_count) * (1.0 / math.sqrt(rows))
    pieces = [grad_padded[:, 0, 1:-1], grad_padded[:, 1:-1, -1], grad_padded[:, -1, 1:-1], grad_padded[:, 1:-1, 0]]
    corner_pieces = [grad_padded[:, 0, 0], grad_padded[:, 0, -1], grad_padded[:, -1, -1], grad_padded[:, -1, 0]]
    collected = jnp.zeros((tile_count, 8, side_len, chan_count), jnp.float32)
    corner_sums = jnp.zeros((tile_count, 4, chan_count), jnp.float32)
    for border in range(4):
        collected = collected.at[edge_tiles[:, border], edge_slots[border]].add(rounded(pieces[border]))
        corner_sums = corner_sums.at[corner_tiles[:, border], corner_slots[border]].add(rounded(corner_pieces[border]))
    side_sums = collected[:, :4] + collected[:, 4:, ::-1]
    interior = grad_padded[:, 1:-1, 1:-1]
    interior = interior.at[:, 0].add(side_sums[:, 0]).at[:, :, -1].add(side_sums[:, 1])
    interior = interior.at[:, -1].add(side_sums[:, 2]).at[:, :, 0].add(side_sums[:, 3])
    interior = interior.at[:, 0, 0].add(corner_sums[:, 0]).at[:, 0, -1].add(corner_sums[:, 1])
    interior = interior.at[:, -1, -1].add(corner_sums[:, 2]).at[:, -1, 0].add(corner_sums[:, 3])
    output = output.reshape(features.shape).astype(jnp.bfloat16)
    return (output, interior.astype(jnp.bfloat16), grad_weight)
```

```python
import math

import jax
import jax.numpy as jnp
import numpy as np
from jax import lax
from jax.experimental import pallas as pl
from jax.experimental.pallas import tpu as pltpu
from jax.sharding import PartitionSpec as P

MESH = pl.DeviceIdType.MESH
SPAN = 4
OFFSETS = [-4, -3, -2, -1, 1, 2, 3, 4]
S = 32
ROWS = S * S
UNIT = 16
VM = pltpu.VMEM
BF = jnp.bfloat16
F32 = jnp.float32


def turn_tables():
    labels = [[3 * row + col for col in range(3)] for row in range(3)]

    def turn_once(block):
        return [[block[col][2 - row] for col in range(3)] for row in range(3)]

    def sides_of(block):
        return [
            list(block[0]),
            [block[row][2] for row in range(3)],
            list(block[2]),
            [block[row][0] for row in range(3)],
        ]

    def corners_of(block):
        return [block[0][0], block[0][2], block[2][2], block[2][0]]

    base_sides = sides_of(labels)
    base_corners = corners_of(labels)
    edge_table = np.zeros((4, 4), np.int32)
    corner_table = np.zeros((4, 4), np.int32)
    for border in range(4):
        turned = labels
        for quarter in range(4):
            wanted = sides_of(turned)[(border + 2) % 4]
            for side_index in range(4):
                if base_sides[side_index] == wanted:
                    edge_table[border, quarter] = side_index
                if base_sides[side_index][::-1] == wanted:
                    edge_table[border, quarter] = side_index + 4
            corner_cell = corners_of(turned)[(border + 2) % 4]
            for corner_index in range(4):
                if base_corners[corner_index] == corner_cell:
                    corner_table[border, quarter] = corner_index
            turned = turn_once(turned)
    return (edge_table, corner_table)


EDGE_TABLE, CORNER_TABLE = turn_tables()


def lookup(table, border, turn):
    row = [int(v) for v in table[border]]
    value = jnp.int32(row[0])
    for quarter in range(1, 4):
        value = jnp.where(turn == quarter, jnp.int32(row[quarter]), value)
    return value


def slot_of(offset):
    return offset + SPAN if offset < 0 else offset + SPAN - 1


def wrap(index, size):
    return lax.rem(index + size, jnp.int32(size))


def coords():
    tile = lax.axis_index("tile")
    ch = lax.axis_index("ch")
    core = lax.rem(tile, 2)
    y = lax.rem(tile // 2, 4)
    xl = lax.rem(tile // 8, 2)
    z = tile // 16
    return tile, ch, core, y, xl, z


def dev(tile, ch):
    return {"tile": tile, "ch": ch}


def x_neighbours(tile, ch, xl):
    beside = tile + 8 - 16 * xl
    return dev(beside, ch), dev(beside, 1 - ch)


def remote(src, dst, send, recv, where):
    return pltpu.make_async_remote_copy(
        src_ref=src, dst_ref=dst, send_sem=send, recv_sem=recv, device_id=where, device_id_type=MESH
    )


class Swap:
    def __init__(self, src, dst, relay, sems, tile, ch, xl):
        self.n = relay.shape[1]
        near, far = x_neighbours(tile, ch, xl)
        self.first, self.second = [], []
        for i in range(self.n):
            for path in range(2):
                hop1, hop2 = (near, far) if path == 0 else (far, near)
                j = path * self.n + i
                self.first.append(remote(src.at[j], relay.at[path, i], sems.at[0, j], sems.at[1, j], hop1))
                self.second.append(remote(relay.at[path, i], dst.at[j], sems.at[2, j], sems.at[3, j], hop2))

    def start(self):
        for copy in self.first:
            copy.start()

    def relay(self):
        for one, two in zip(self.first, self.second):
            one.wait_recv()
            two.start()

    def finish(self):
        for one, two in zip(self.first, self.second):
            one.wait_send()
            two.wait()


def barrier(devices):
    sem = pltpu.get_barrier_semaphore()
    for where in devices:
        pl.semaphore_signal(sem, inc=1, device_id=where, device_id_type=MESH)
    pl.semaphore_wait(sem, len(devices))


def near_copies(src, dst, sems, tile, ch, tiles):
    copies = []
    for offset in OFFSETS:
        k = slot_of(-offset)
        copies.append(
            remote(src, dst.at[k], sems.at[0, k], sems.at[1, k], dev(wrap(tile + offset, tiles), ch))
        )
    return copies


def exchange_kernel(sides, cot, all_sides, cot_other, relay, near_sems, swap_sems):
    tiles = 128
    tile, ch, core, y, xl, z = coords()
    near, far = x_neighbours(tile, ch, xl)
    barrier([dev(wrap(tile + o, tiles), ch) for o in OFFSETS] + [near, far])
    swap = Swap(cot, cot_other, relay, swap_sems, tile, ch, xl)
    copies = near_copies(sides, all_sides, near_sems, tile, ch, tiles)
    swap.start()
    for copy in copies:
        copy.start()
    swap.relay()
    for copy in copies:
        copy.wait()
    swap.finish()


def iota2(shape, dim):
    return lax.broadcasted_iota(jnp.int32, shape, dim)


def flipper(rev):
    ii = iota2((S, S), 0)
    target = jnp.where(rev == 1, S - 1 - ii, ii)
    return jnp.where(iota2((S, S), 1) == target, 1.0, 0.0).astype(BF)


def source_slot(target, tile, tiles):
    away = wrap(target - tile, tiles)
    return jnp.where(away > tiles // 2, away - tiles + SPAN, away + SPAN - 1)


def spread_columns(buf, row, x, left, right):
    io = iota2(x.shape, 0)
    buf[0, row] = jnp.where(io == 0, left, pltpu.roll(x, 1, 0)).astype(BF)
    buf[2, row] = jnp.where(io == S - 1, right, pltpu.roll(x, S - 1, 0)).astype(BF)


def compute_kernel(
    edge_tiles, edge_turns, corner_tiles, corner_turns,
    feat, all_sides, cot, cot_other, weight,
    grads, padded, columns, interior, pieces,
    halo, cots, cot_columns,
):
    tiles = 128
    tile, ch, core, y, xl, z = coords()
    C2 = feat.shape[2]
    for border in range(4):
        source = source_slot(edge_tiles[tile, border], tile, tiles)
        slot = lookup(EDGE_TABLE, border, edge_turns[tile, border])
        rev = slot // 4
        halo[border] = jnp.dot(
            flipper(rev), all_sides[source, slot - 4 * rev], preferred_element_type=F32
        )
    columns[0, 1 : S + 1] = halo[3]
    columns[1, 1 : S + 1] = halo[1]
    for corner in range(4):
        source = source_slot(corner_tiles[tile, corner], tile, tiles)
        slot = lookup(CORNER_TABLE, corner, corner_turns[tile, corner])
        side = jnp.where(slot < 2, 0, 2)
        row = jnp.where((slot == 0) | (slot == 3), 0, S - 1)
        cells = all_sides[source, side].astype(F32)
        value = jnp.sum(jnp.where(iota2(cells.shape, 0) == row, cells, 0.0), axis=0, keepdims=True)
        at = 0 if corner < 2 else S + 1
        columns[(0, 1, 1, 0)[corner], at : at + 1] = value
    padded[1, 0] = halo[0].astype(BF)
    padded[1, S + 1] = halo[2].astype(BF)
    padded[1, 1 : S + 1] = feat[...]

    def shift_features(row, carry):
        x = padded[1, row].astype(F32)
        spread_columns(padded, row, x, columns[0, pl.ds(row, 1)], columns[1, pl.ds(row, 1)])
        return carry

    lax.fori_loop(0, S + 2, shift_features, 0)

    zero = jnp.zeros((S, 2 * C2), BF)
    for part in range(3):
        for row in (0, 1, S + 2, S + 3):
            cots[part, row] = zero
    cot_columns[...] = jnp.zeros_like(cot_columns)

    def shift_cots(row, carry):
        own = cot[row].astype(F32)
        other = cot_other[row].astype(F32)
        x = jnp.where(ch == 0, jnp.concatenate([own, other], axis=1), jnp.concatenate([other, own], axis=1))
        cots[1, row + 2] = x.astype(BF)
        nothing = jnp.zeros((1, 2 * C2), F32)
        spread_columns(cots, row + 2, x, nothing, nothing)
        cot_columns[0, pl.ds(row + 2, 1)] = x[0:1]
        cot_columns[1, pl.ds(row + 2, 1)] = x[S - 1 : S]
        return carry

    lax.fori_loop(0, S, shift_cots, 0)

    def weight_grad(tap, carry):
        a, b = tap // 3, lax.rem(tap, 3)
        window = padded[b, pl.ds(a, S)].reshape(ROWS, C2)
        full = cots[1, 2 : S + 2].reshape(ROWS, 2 * C2)
        part = lax.dot_general(window, full, (((0,), (0,)), ((), ())), preferred_element_type=F32)
        at = pl.multiple_of(tap * (C2 // 2), 32)
        grads[0, pl.ds(at, C2 // 2)] = part[: C2 // 2]
        grads[1, pl.ds(at, C2 // 2)] = part[C2 // 2 :]
        return carry

    lax.fori_loop(0, 9, weight_grad, 0)
    tail = grads.shape[1] - 9 * (C2 // 2)
    grads[:, 9 * (C2 // 2) :] = jnp.zeros((2, tail, 2 * C2), F32)

    nt = (((1,), (1,)), ((), ()))
    half = (S + 2) // 2

    def feature_grad(block, carry):
        total = None
        for a in range(3):
            for b in range(3):
                window = cots[2 - b, pl.ds(block * half + 2 - a, half)].reshape(half * S, 2 * C2)
                term = lax.dot_general(window, weight[3 * a + b], nt, preferred_element_type=F32)
                total = term if total is None else total + term
        interior[pl.ds(block * half, half)] = total.reshape(half, S, C2)
        return carry

    lax.fori_loop(0, 2, feature_grad, 0)
    pieces[0] = interior[0].astype(BF)
    pieces[2] = interior[S + 1].astype(BF)
    ends = []
    for side in range(2):
        total = None
        for a in range(3):
            line = cot_columns[side, 2 - a : 2 - a + 40].astype(BF)
            term = lax.dot_general(line, weight[3 * a + 2 * side], nt, preferred_element_type=F32)
            total = term if total is None else total + term
        cot_columns[side, 0:40, 0:C2] = total
        pieces[3 - 2 * side] = cot_columns[side, 1 : S + 1, 0:C2].astype(BF)
        ends.append((total[0:1], total[S + 1 : S + 2]))
    io = iota2((S, C2), 0)
    corner_rows = jnp.zeros((S, C2), F32)
    for corner, value in enumerate((ends[0][0], ends[1][0], ends[1][1], ends[0][1])):
        corner_rows = jnp.where(io == corner, value, corner_rows)
    pieces[4] = corner_rows.astype(BF)


def reduce_kernel(
    scale, grads, padded, pieces,
    gathered, padded_other, all_pieces,
    pair_in, y_out, y_in, acc, x_in, z_out, z_in, relay,
    near_sems, swap_sems, pair_sems, y_sems, x_sems, z_sems, gz_sems, gx_sems, gy_sems, gp_sems,
):
    tiles = 128
    tile, ch, core, y, xl, z = coords()
    near, far = x_neighbours(tile, ch, xl)
    pair = dev(tile + 1 - 2 * core, ch)
    y_at = [lax.rem(y + 1 + j, 4) for j in range(3)]
    y_peer = [dev(tile + 2 * (q - y), ch) for q in y_at]
    z_at = [lax.rem(z + 1 + j, 8) for j in range(7)]
    z_peer = [dev(tile + 16 * (q - z), ch) for q in z_at]
    barrier(
        [dev(wrap(tile + o, tiles), ch) for o in OFFSETS] + [near, far, pair] + y_peer + z_peer
    )
    order = y_at + [y]
    pair_copies = [
        remote(grads.at[1 - core, q], pair_in.at[j], pair_sems.at[0, j], pair_sems.at[1, j], pair)
        for j, q in enumerate(order)
    ]
    for copy in pair_copies:
        copy.start()
    swap = Swap(padded, padded_other, relay, swap_sems, tile, ch, xl)
    swap.start()
    copies = near_copies(pieces, all_pieces, near_sems, tile, ch, tiles)
    y_copies = [
        remote(y_out.at[j], y_in.at[j], y_sems.at[0, j], y_sems.at[1, j], y_peer[j]) for j in range(3)
    ]
    for j in range(4):
        pair_copies[j].wait_recv()
        total = grads[core, order[j]] + pair_in[j]
        if j < 3:
            y_out[j] = total.astype(BF)
            y_copies[j].start()
        else:
            acc[...] = total.reshape(acc.shape)
    swap.relay()
    for copy in copies:
        copy.start()
    for j in range(3):
        y_copies[j].wait_recv()
        acc[...] += y_in[j].astype(F32).reshape(acc.shape)
    x_copy = remote(acc.at[1 - xl], x_in, x_sems.at[0], x_sems.at[1], near)
    x_copy.start()
    z_out[7] = jnp.zeros(z_out.shape[1:], F32)
    x_copy.wait_recv()
    z_out[0:7] = (acc[xl] + x_in[...]).reshape(7, UNIT, acc.shape[2])
    z_copies = [
        remote(z_out.at[z_at[j]], z_in.at[j], z_sems.at[0, j], z_sems.at[1, j], z_peer[j])
        for j in range(7)
    ]
    for copy in z_copies:
        copy.start()
    total = z_out[z]
    for j in range(7):
        z_copies[j].wait_recv()
        total = total + z_in[j]
    gathered[core, y, xl, z] = (total * scale).astype(BF)
    spot = gathered.at[core, y, xl, z]
    gz_copies = [
        remote(spot, spot, gz_sems.at[0, j], gz_sems.at[1, j], z_peer[j]) for j in range(7)
    ]
    for copy in gz_copies:
        copy.start()
    for copy in gz_copies:
        copy.wait_recv()
    spot = gathered.at[core, y, xl]
    gx_copy = remote(spot, spot, gx_sems.at[0], gx_sems.at[1], near)
    gx_copy.start()
    gx_copy.wait_recv()
    spot = gathered.at[core, y]
    gy_copies = [remote(spot, spot, gy_sems.at[0, j], gy_sems.at[1, j], y_peer[j]) for j in range(3)]
    for copy in gy_copies:
        copy.start()
    gp_copies = []
    for j in range(4):
        q = y if j == 0 else lax.rem(y + 4 - j, 4)
        if j > 0:
            gy_copies[j - 1].wait_recv()
        spot = gathered.at[core, q]
        gp_copies.append(remote(spot, spot, gp_sems.at[0, j], gp_sems.at[1, j], pair))
        gp_copies[j].start()
    for copy in copies:
        copy.wait()
    swap.finish()
    for copy in gp_copies:
        copy.wait()
    x_copy.wait_send()
    gx_copy.wait_send()
    for copy in pair_copies + y_copies + z_copies + gz_copies + gy_copies:
        copy.wait_send()


def final_kernel(
    edge_tiles, edge_turns, corner_tiles, corner_turns,
    interior, all_pieces, padded, padded_other, weight,
    output, grad_features,
    sums, corner_sums, shifted,
):
    tiles = 128
    tile, ch, core, y, xl, z = coords()
    C2 = interior.shape[2]
    sums[...] = jnp.zeros_like(sums)
    corner_sums[...] = jnp.zeros_like(corner_sums)
    for offset in OFFSETS:
        k = slot_of(-offset)
        source = wrap(tile - offset, tiles)
        for border in range(4):

            @pl.when(edge_tiles[source, border] == tile)
            def _():
                slot = lookup(EDGE_TABLE, border, edge_turns[source, border])
                rev = slot // 4
                sums[slot - 4 * rev] += jnp.dot(
                    flipper(rev), all_pieces[k, border], preferred_element_type=F32
                )

            @pl.when(corner_tiles[source, border] == tile)
            def _():
                slot = lookup(CORNER_TABLE, border, corner_turns[source, border])
                cells = all_pieces[k, 4].astype(F32)
                value = jnp.sum(
                    jnp.where(iota2(cells.shape, 0) == border, cells, 0.0), axis=0, keepdims=True
                )
                corner_sums[slot] += jnp.broadcast_to(value, (8, C2))

    io = iota2((S, C2), 0)
    for corner in range(4):
        at = 0 if corner in (0, 3) else S - 1
        side = 0 if corner < 2 else 2
        sums[side] += jnp.where(io == at, corner_sums[corner, 0:1], 0.0)

    def add_sides(row, carry):
        x = interior[row + 1]
        x = x + jnp.where(io == 0, sums[3, pl.ds(row, 1)], 0.0)
        x = x + jnp.where(io == S - 1, sums[1, pl.ds(row, 1)], 0.0)
        x = x + jnp.where(row == 0, sums[0], 0.0)
        x = x + jnp.where(row == S - 1, sums[2], 0.0)
        grad_features[row] = x.astype(BF)
        return carry

    lax.fori_loop(0, S, add_sides, 0)

    sums[...] = jnp.zeros_like(sums)
    edge = padded_other[S + 2].astype(F32)
    edge2 = padded_other[S + 3].astype(F32)
    corners = padded_other[S + 4].astype(F32)
    shifted[1] = padded_other[0 : S + 2]

    def shift_features(row, carry):
        x = shifted[1, row].astype(F32)
        hot = iota2((S, C2), 0) == row - 1
        left = jnp.sum(jnp.where(hot, edge, 0.0), axis=0, keepdims=True)
        right = jnp.sum(jnp.where(hot, edge2, 0.0), axis=0, keepdims=True)
        left = left + jnp.where(row == 0, corners[0:1], 0.0) + jnp.where(row == S + 1, corners[3:4], 0.0)
        right = right + jnp.where(row == 0, corners[1:2], 0.0) + jnp.where(row == S + 1, corners[2:3], 0.0)
        spread_columns(shifted, row, x, left, right)
        return carry

    lax.fori_loop(0, S + 2, shift_features, 0)
    half = S // 2

    def convolve(block, carry):
        total = None
        for a in range(3):
            for b in range(3):
                for buf, part in ((padded, 0), (shifted, 1)):
                    window = buf[b, pl.ds(block * half + a, half)].reshape(half * S, C2)
                    term = jnp.dot(window, weight[part, 3 * a + b], preferred_element_type=F32)
                    total = term if total is None else total + term
        output[pl.ds(block * half, half)] = total.reshape(half, S, C2).astype(BF)
        return carry

    lax.fori_loop(0, 2, convolve, 0)


def params(**more):
    return pltpu.CompilerParams(vmem_limit_bytes=60 * 1024 * 1024, **more)


VSPEC = pl.BlockSpec(memory_space=VM)
SSPEC = pl.BlockSpec(memory_space=pltpu.SMEM)
DMA = pltpu.SemaphoreType.DMA


def body(features, weight, cotangent, edge_tiles, edge_turns, corner_tiles, corner_turns):
    field = features[0]
    C2 = field.shape[2]
    C = 2 * C2
    ch = lax.axis_index("ch")
    cot = cotangent[0]
    shape = jax.ShapeDtypeStruct
    sides = jnp.stack([field[0], field[:, -1], field[-1], field[:, 0]])

    all_sides, cot_other = pl.pallas_call(
        exchange_kernel,
        name="exchange",
        out_shape=(shape((8, 4, S, C2), BF), shape((8, ROWS // 8, C2), BF)),
        in_specs=[VSPEC] * 2,
        out_specs=(VSPEC,) * 2,
        scratch_shapes=[VM((2, 4, ROWS // 8, C2), BF), DMA((2, 8)), DMA((4, 8))],
        compiler_params=params(collective_id=0, has_side_effects=True),
    )(sides, cot.reshape(8, ROWS // 8, C2))

    taps = weight.reshape(9, C, C)
    weight_rows = lax.dynamic_slice_in_dim(taps, ch * C2, C2, 1)
    out_columns = lax.dynamic_slice_in_dim(taps, ch * C2, C2, 2)
    out_columns = jnp.stack(
        [
            lax.dynamic_slice_in_dim(out_columns, ch * C2, C2, 1),
            lax.dynamic_slice_in_dim(out_columns, (1 - ch) * C2, C2, 1),
        ]
    )
    tables = (edge_tiles, edge_turns, corner_tiles, corner_turns)
    grads, padded, columns, interior, pieces = pl.pallas_call(
        compute_kernel,
        name="compute",
        out_shape=(
            shape((2, 56 * UNIT, C), F32),
            shape((3, S + 2, S, C2), BF),
            shape((2, 40, C2), F32),
            shape((S + 2, S, C2), F32),
            shape((5, S, C2), BF),
        ),
        in_specs=[SSPEC] * 4 + [VSPEC] * 5,
        out_specs=(VSPEC,) * 5,
        scratch_shapes=[VM((4, S, C2), F32), VM((3, S + 4, S, C), BF), VM((2, 48, C), F32)],
        compiler_params=params(),
    )(*tables, field, all_sides, cot, cot_other.reshape(S, S, C2), weight_rows)

    lines = columns[:, 1 : S + 1].astype(BF)
    ends = jnp.concatenate([columns[:, 0], columns[::-1, S + 1]]).astype(BF)
    ends = jnp.pad(ends, ((0, S - 4), (0, 0)))[None]
    sent = jnp.concatenate([padded[1], lines, ends, jnp.zeros((3, S, C2), BF)]).reshape(8, 5, S, C2)

    gathered, padded_other, all_pieces = pl.pallas_call(
        lambda *refs: reduce_kernel(1.0 / math.sqrt(128 * ROWS), *refs),
        name="reduce",
        out_shape=(
            shape((2, 4, 2, 8, UNIT, C), BF),
            shape((8, 5, S, C2), BF),
            shape((8, 5, S, C2), BF),
        ),
        in_specs=[VSPEC] * 3,
        out_specs=(VSPEC,) * 3,
        scratch_shapes=[
            VM((4, 14 * UNIT, C), F32),
            VM((3, 14 * UNIT, C), BF),
            VM((3, 14 * UNIT, C), BF),
            VM((2, 7 * UNIT, C), F32),
            VM((7 * UNIT, C), F32),
            VM((8, UNIT, C), F32),
            VM((7, UNIT, C), F32),
            VM((2, 4, 5, S, C2), BF),
            DMA((2, 8)),
            DMA((4, 8)),
            DMA((2, 4)),
            DMA((2, 3)),
            DMA((2,)),
            DMA((2, 7)),
            DMA((2, 7)),
            DMA((2,)),
            DMA((2, 3)),
            DMA((2, 4)),
        ],
        compiler_params=params(collective_id=1, has_side_effects=True),
    )(grads.reshape(2, 4, 14 * UNIT, C), sent, pieces)

    output, grad_features = pl.pallas_call(
        final_kernel,
        name="final",
        out_shape=(shape((S, S, C2), BF), shape((S, S, C2), BF)),
        in_specs=[SSPEC] * 4 + [VSPEC] * 5,
        out_specs=(VSPEC,) * 2,
        scratch_shapes=[VM((4, S, C2), F32), VM((4, 8, C2), F32), VM((3, S + 2, S, C2), BF)],
        compiler_params=params(),
    )(*tables, interior, all_pieces, padded, padded_other.reshape(8 * 5, S, C2), out_columns)

    flat = gathered[:, :, :, :7].reshape(2, 56 * UNIT, C)[:, : 9 * (C2 // 2)]
    grad_weight = flat.reshape(2, 9, C2 // 2, C).transpose(1, 0, 2, 3).astype(F32).reshape(3, 3, C2, C)
    return (output[None], grad_features[None], grad_weight)


def solution(mesh):
    return jax.shard_map(
        body,
        mesh=mesh,
        in_specs=(
            P("tile", None, None, "ch"),
            P(),
            P("tile", None, None, "ch"),
            P(),
            P(),
            P(),
            P(),
        ),
        out_specs=(
            P("tile", None, None, "ch"),
            P("tile", None, None, "ch"),
            P(None, None, "ch", None),
        ),
        check_vma=False,
    )
```

```python
import math

import jax
import jax.numpy as jnp
import numpy as np
from jax import lax
from jax.experimental import pallas as pl
from jax.experimental.pallas import tpu as pltpu
from jax.sharding import PartitionSpec as P

MESH = pl.DeviceIdType.MESH
SPAN = 4
OFFSETS = [-4, -3, -2, -1, 1, 2, 3, 4]
S = 32
ROWS = S * S
UNIT = 16
VM = pltpu.VMEM
BF = jnp.bfloat16
F32 = jnp.float32


def turn_tables():
    labels = [[3 * row + col for col in range(3)] for row in range(3)]

    def turn_once(block):
        return [[block[col][2 - row] for col in range(3)] for row in range(3)]

    def sides_of(block):
        return [
            list(block[0]),
            [block[row][2] for row in range(3)],
            list(block[2]),
            [block[row][0] for row in range(3)],
        ]

    def corners_of(block):
        return [block[0][0], block[0][2], block[2][2], block[2][0]]

    base_sides = sides_of(labels)
    base_corners = corners_of(labels)
    edge_table = np.zeros((4, 4), np.int32)
    corner_table = np.zeros((4, 4), np.int32)
    for border in range(4):
        turned = labels
        for quarter in range(4):
            wanted = sides_of(turned)[(border + 2) % 4]
            for side_index in range(4):
                if base_sides[side_index] == wanted:
                    edge_table[border, quarter] = side_index
                if base_sides[side_index][::-1] == wanted:
                    edge_table[border, quarter] = side_index + 4
            corner_cell = corners_of(turned)[(border + 2) % 4]
            for corner_index in range(4):
                if base_corners[corner_index] == corner_cell:
                    corner_table[border, quarter] = corner_index
            turned = turn_once(turned)
    return (edge_table, corner_table)


EDGE_TABLE, CORNER_TABLE = turn_tables()


def lookup(table, border, turn):
    row = [int(v) for v in table[border]]
    value = jnp.int32(row[0])
    for quarter in range(1, 4):
        value = jnp.where(turn == quarter, jnp.int32(row[quarter]), value)
    return value


def slot_of(offset):
    return offset + SPAN if offset < 0 else offset + SPAN - 1


def wrap(index, size):
    return lax.rem(index + size, jnp.int32(size))


def coords():
    tile = lax.axis_index("tile")
    ch = lax.axis_index("ch")
    core = lax.rem(tile, 2)
    y = lax.rem(tile // 2, 4)
    xl = lax.rem(tile // 8, 2)
    z = tile // 16
    return tile, ch, core, y, xl, z


def dev(tile, ch):
    return {"tile": tile, "ch": ch}


def x_neighbours(tile, ch, xl):
    beside = tile + 8 - 16 * xl
    return dev(beside, ch), dev(beside, 1 - ch)


def remote(src, dst, send, recv, where):
    return pltpu.make_async_remote_copy(
        src_ref=src, dst_ref=dst, send_sem=send, recv_sem=recv, device_id=where, device_id_type=MESH
    )


class Swap:
    def __init__(self, src, dst, relay, sems, tile, ch, xl):
        self.n = relay.shape[1]
        near, far = x_neighbours(tile, ch, xl)
        self.first, self.second = [], []
        for i in range(self.n):
            for path in range(2):
                hop1, hop2 = (near, far) if path == 0 else (far, near)
                j = path * self.n + i
                self.first.append(remote(src.at[j], relay.at[path, i], sems.at[0, j], sems.at[1, j], hop1))
                self.second.append(remote(relay.at[path, i], dst.at[j], sems.at[2, j], sems.at[3, j], hop2))

    def start(self):
        for copy in self.first:
            copy.start()

    def relay(self):
        for one, two in zip(self.first, self.second):
            one.wait_recv()
            two.start()

    def finish_sends(self):
        for one, two in zip(self.first, self.second):
            one.wait_send()
            two.wait_send()


def near_copies(src, dst, sems, tile, ch, tiles):
    copies = []
    for offset in OFFSETS:
        k = slot_of(-offset)
        copies.append(
            remote(src, dst.at[k], sems.at[0, k], sems.at[1, k], dev(wrap(tile + offset, tiles), ch))
        )
    return copies


def iota2(shape, dim):
    return lax.broadcasted_iota(jnp.int32, shape, dim)


def source_slot(target, tile, tiles):
    away = wrap(target - tile, tiles)
    return jnp.clip(jnp.where(away > tiles // 2, away - tiles + SPAN, away + SPAN - 1), 0, 2 * SPAN - 1)


def spread_columns(buf, row, lanes, x, left, right):
    io = iota2(x.shape, 0)
    buf[1, row, :, lanes] = x.astype(BF)
    buf[0, row, :, lanes] = jnp.where(io == 0, left, pltpu.roll(x, 1, 0)).astype(BF)
    buf[2, row, :, lanes] = jnp.where(io == S - 1, right, pltpu.roll(x, S - 1, 0)).astype(BF)


def pack(x):
    return jnp.concatenate([x[: S // 2], x[S // 2 :]], axis=1)


def unpack(x):
    c = x.shape[1] // 2
    return jnp.concatenate([x[:, :c], x[:, c:]], axis=0)


def one_hot_rows(rows, target, width):
    return jnp.where(iota2((rows, width), 1) == target, 1.0, 0.0).astype(BF)


TN = (((0,), (0,)), ((), ()))
NT = (((1,), (1,)), ((), ()))


def fused_kernel(
    scale,
    edge_tiles_in, edge_turns_in, corner_tiles_in, corner_turns_in, feat_in, cot_in, weight_in,
    output, grad_features, gathered,
    edge_tiles, edge_turns, corner_tiles, corner_turns,
    feat, cot, weight, rows_weight, out_weight,
    lines, sides, all_sides, cot_packed, cot_other, relay_a,
    padded, columns, cots, cot_columns, grads, interior, pieces, all_pieces,
    packed, packed_other, relay_b, shifted, partial_out, hits, sums,
    pair_in, y_out, y_in, acc, x_in, z_out, z_in,
    load_sems, side_sems, swap_a_sems, swap_b_sems, piece_sems,
    pair_sems, y_sems, x_sems, z_sems, gz_sems, gx_sems, gy_sems, gp_sems,
):
    tiles = 128
    tile, ch, core, y, xl, z = coords()
    C2 = feat.shape[2]
    C = 2 * C2
    near, far = x_neighbours(tile, ch, xl)
    pair = dev(tile + 1 - 2 * core, ch)
    y_at = [lax.rem(y + 1 + j, 4) for j in range(3)]
    y_peer = [dev(tile + 2 * (q - y), ch) for q in y_at]
    z_at = [lax.rem(z + 1 + j, 8) for j in range(7)]
    z_peer = [dev(tile + 16 * (q - z), ch) for q in z_at]
    greeted = (
        [dev(wrap(tile + o, tiles), ch) for o in OFFSETS] + [near, far, pair] + y_peer + z_peer
    )
    ready = pltpu.get_barrier_semaphore()
    for where in greeted:
        pl.semaphore_signal(ready, inc=1, device_id=where, device_id_type=MESH)

    loads = [
        pltpu.make_async_copy(a, b, load_sems.at[i])
        for i, (a, b) in enumerate(
            (
                (feat_in, feat),
                (cot_in, cot),
                (edge_tiles_in, edge_tiles),
                (edge_turns_in, edge_turns),
                (corner_tiles_in, corner_tiles),
                (corner_turns_in, corner_turns),
                (weight_in, weight),
            )
        )
    ]
    for load in loads:
        load.start()

    loads[0].wait()

    def take_columns(row, carry):
        x = feat[row].astype(F32)
        lines[0, pl.ds(row, 1)] = x[0:1]
        lines[1, pl.ds(row, 1)] = x[S - 1 : S]
        return carry

    lax.fori_loop(0, S, take_columns, 0)
    sides[0] = pack(feat[0].astype(F32)).astype(BF)
    sides[1] = pack(lines[1]).astype(BF)
    sides[2] = pack(feat[S - 1].astype(F32)).astype(BF)
    sides[3] = pack(lines[0]).astype(BF)
    loads[1].wait()

    def pack_cot(row, carry):
        at = pl.multiple_of(lax.rem(row, 4) * 16, 16)
        cot_packed[row // 4, pl.ds(at, 16)] = pack(cot[row].astype(F32)).astype(BF)
        return carry

    lax.fori_loop(0, S, pack_cot, 0)
    pl.semaphore_wait(ready, len(greeted))
    swap_a = Swap(cot_packed, cot_other, relay_a, swap_a_sems, tile, ch, xl)
    swap_a.start()
    side_copies = near_copies(sides, all_sides, side_sems, tile, ch, tiles)
    for copy in side_copies:
        copy.start()

    zero = jnp.zeros((S, C), BF)
    for part in range(3):
        for row in (0, 1, S + 2, S + 3):
            cots[part, row] = zero
    cot_columns[...] = jnp.zeros_like(cot_columns)
    nothing = jnp.zeros((1, C2), F32)

    def shift_own(row, carry):
        x = cot[row].astype(F32)
        spread_columns(cots, row + 2, slice(0, C2), x, nothing, nothing)
        cot_columns[0, pl.ds(row + 2, 1), 0:C2] = x[0:1]
        cot_columns[1, pl.ds(row + 2, 1), 0:C2] = x[S - 1 : S]
        return carry

    lax.fori_loop(0, S, shift_own, 0)
    swap_a.relay()

    for i in range(2, 6):
        loads[i].wait()
    for copy in side_copies:
        copy.wait_recv()
    halos = []
    for border in range(4):
        source = source_slot(edge_tiles[tile, border], tile, tiles)
        slot = lookup(EDGE_TABLE, border, edge_turns[tile, border])
        rev = slot // 4
        x = unpack(all_sides[source, slot - 4 * rev].astype(F32)).astype(BF)
        ii = iota2((S, 1), 0)
        hot = one_hot_rows(S, jnp.where(rev == 1, S - 1 - ii, ii), S)
        halos.append(jnp.dot(hot, x, preferred_element_type=F32))
    columns[0, 1 : S + 1] = halos[3]
    columns[1, 1 : S + 1] = halos[1]
    for corner in range(4):
        source = source_slot(corner_tiles[tile, corner], tile, tiles)
        slot = lookup(CORNER_TABLE, corner, corner_turns[tile, corner])
        cells = all_sides[source, jnp.where(slot < 2, 0, 2)].astype(F32)
        first = (slot == 0) | (slot == 3)
        at = 0 if corner < 2 else S + 1
        columns[(0, 1, 1, 0)[corner], at : at + 1] = jnp.where(first, cells[0:1, :C2], cells[15:16, C2:])
    padded[1, 0] = halos[0].astype(BF)
    padded[1, S + 1] = halos[2].astype(BF)
    padded[1, 1 : S + 1] = feat[...]

    def shift_features(row, carry):
        x = padded[1, row].astype(F32)
        spread_columns(
            padded, row, slice(0, C2), x, columns[0, pl.ds(row, 1)], columns[1, pl.ds(row, 1)]
        )
        return carry

    lax.fori_loop(0, S + 2, shift_features, 0)
    for copy in swap_a.second:
        copy.wait_recv()

    def shift_other(row, carry):
        at = pl.multiple_of(lax.rem(row, 4) * 16, 16)
        x = unpack(cot_other[row // 4, pl.ds(at, 16)].astype(F32))
        spread_columns(cots, row + 2, slice(C2, C), x, nothing, nothing)
        cot_columns[0, pl.ds(row + 2, 1), C2:C] = x[0:1]
        cot_columns[1, pl.ds(row + 2, 1), C2:C] = x[S - 1 : S]
        return carry

    lax.fori_loop(0, S, shift_other, 0)

    def weight_grad(tap, carry):
        a, b = tap // 3, lax.rem(tap, 3)
        window = padded[b, pl.ds(a, S)].reshape(ROWS, C2)
        full = cots[1, 2 : S + 2].reshape(ROWS, C)
        part = lax.dot_general(window, full, TN, preferred_element_type=F32)
        at = pl.multiple_of(tap * (C2 // 2), 32)
        grads[0, pl.ds(at, C2 // 2)] = part[: C2 // 2]
        grads[1, pl.ds(at, C2 // 2)] = part[C2 // 2 :]
        return carry

    lax.fori_loop(0, 9, weight_grad, 0)
    tail = grads.shape[1] - 9 * (C2 // 2)
    grads[:, 9 * (C2 // 2) :] = jnp.zeros((2, tail, C), F32)

    chunk = 14 * UNIT
    order = y_at + [y]
    pair_copies = []
    for j, q in enumerate(order):
        src = grads.at[1 - core, pl.ds(pl.multiple_of(q * chunk, chunk), chunk)]
        pair_copies.append(remote(src, pair_in.at[j], pair_sems.at[0, j], pair_sems.at[1, j], pair))
        pair_copies[j].start()

    def pack_padded(row, carry):
        packed[row // 5, lax.rem(row, 5)] = pack(padded[1, row].astype(F32)).astype(BF)
        return carry

    lax.fori_loop(0, S + 2, pack_padded, 0)
    packed[6, 4] = pack(columns[0, 1 : S + 1]).astype(BF)
    packed[7, 0] = pack(columns[1, 1 : S + 1]).astype(BF)
    io = iota2((16, C), 0)
    ends = jnp.zeros((16, C), F32)
    for corner in range(4):
        at = 0 if corner < 2 else S + 1
        value = columns[(0, 1, 1, 0)[corner], at : at + 1]
        ends = jnp.where(io == corner, jnp.concatenate([value, value], axis=1), ends)
    packed[7, 1] = ends.astype(BF)
    for i in range(2, 5):
        packed[7, i] = jnp.zeros((16, C), BF)
    swap_b = Swap(packed, packed_other, relay_b, swap_b_sems, tile, ch, xl)

    y_copies = [
        remote(y_out.at[j], y_in.at[j], y_sems.at[0, j], y_sems.at[1, j], y_peer[j]) for j in range(3)
    ]
    for j in range(4):
        pair_copies[j].wait_recv()
        at = pl.multiple_of(order[j] * chunk, chunk)
        total = grads[core, pl.ds(at, chunk)] + pair_in[j]
        if j < 3:
            y_out[j] = total.astype(BF)
            y_copies[j].start()
        else:
            acc[...] = total.reshape(acc.shape)
    swap_b.start()

    loads[6].wait()

    def turn_weight(tap, carry):
        w = weight[tap, pl.ds(pl.multiple_of(ch * C2, 16), C2)].astype(F32)
        w = jnp.where(ch == 0, w, jnp.concatenate([w[:, C2:], w[:, :C2]], axis=1))
        rows_weight[tap] = w.astype(BF)
        for part in range(2):
            half = jnp.where(part == 0, ch, 1 - ch)
            w = weight[tap, pl.ds(pl.multiple_of(half * C2, 16), C2)].astype(F32)
            out_weight[part, tap] = jnp.where(ch == 0, w[:, :C2], w[:, C2:]).astype(BF)
        return carry

    lax.fori_loop(0, 9, turn_weight, 0)
    half = (S + 2) // 2

    def feature_grad(block, carry):
        total = None
        for a in range(3):
            for b in range(3):
                window = cots[2 - b, pl.ds(block * half + 2 - a, half)].reshape(half * S, C)
                term = lax.dot_general(window, rows_weight[3 * a + b], NT, preferred_element_type=F32)
                total = term if total is None else total + term
        interior[pl.ds(block * half, half)] = total.reshape(half, S, C2)
        return carry

    lax.fori_loop(0, 2, feature_grad, 0)
    pieces[0] = pack(interior[0]).astype(BF)
    pieces[2] = pack(interior[S + 1]).astype(BF)
    tips = []
    for side in range(2):
        total = None
        for a in range(3):
            line = cot_columns[side, 2 - a : 2 - a + 40].astype(BF)
            term = lax.dot_general(line, rows_weight[3 * a + 2 * side], NT, preferred_element_type=F32)
            total = term if total is None else total + term
        cot_columns[side, 0:40, 0:C2] = total
        pieces[3 - 2 * side] = pack(cot_columns[side, 1 : S + 1, 0:C2]).astype(BF)
        tips.append((total[0:1], total[S + 1 : S + 2]))
    io = iota2((16, C), 0)
    ends = jnp.zeros((16, C), F32)
    for corner, value in enumerate((tips[0][0], tips[1][0], tips[1][1], tips[0][1])):
        ends = jnp.where(io == corner, jnp.concatenate([value, value], axis=1), ends)
    pieces[4] = ends.astype(BF)
    piece_copies = near_copies(pieces, all_pieces, piece_sems, tile, ch, tiles)
    for copy in piece_copies:
        copy.start()
    swap_b.relay()

    for j in range(3):
        y_copies[j].wait_recv()
        acc[...] += y_in[j].astype(F32).reshape(acc.shape)
    x_copy = remote(acc.at[1 - xl], x_in, x_sems.at[0], x_sems.at[1], near)
    x_copy.start()
    z_out[7] = jnp.zeros(z_out.shape[1:], F32)
    x_copy.wait_recv()
    z_out[0:7] = (acc[xl] + x_in[...]).reshape(7, UNIT, C)
    z_copies = [
        remote(z_out.at[z_at[j]], z_in.at[j], z_sems.at[0, j], z_sems.at[1, j], z_peer[j])
        for j in range(7)
    ]
    for copy in z_copies:
        copy.start()

    rows = S // 2

    def convolve_own(block, carry):
        total = None
        for a in range(3):
            for b in range(3):
                window = padded[b, pl.ds(block * rows + a, rows)].reshape(rows * S, C2)
                term = jnp.dot(window, out_weight[0, 3 * a + b], preferred_element_type=F32)
                total = term if total is None else total + term
        partial_out[pl.ds(block * rows, rows)] = total.reshape(rows, S, C2)
        return carry

    lax.fori_loop(0, 2, convolve_own, 0)

    total = z_out[z]
    for j in range(7):
        z_copies[j].wait_recv()
        total = total + z_in[j]
    total = total * scale
    total = jnp.where(ch == 0, total, jnp.concatenate([total[:, C2:], total[:, :C2]], axis=1))
    gathered[core, y, xl, z] = total.astype(BF)
    spot = gathered.at[core, y, xl, z]
    gz_copies = [
        remote(spot, spot, gz_sems.at[0, j], gz_sems.at[1, j], z_peer[j]) for j in range(7)
    ]
    for copy in gz_copies:
        copy.start()

    for copy in swap_b.second:
        copy.wait_recv()
    left_line = unpack(packed_other[6, 4].astype(F32))
    right_line = unpack(packed_other[7, 0].astype(F32))
    ends = packed_other[7, 1].astype(F32)
    columns[0, 1 : S + 1] = left_line
    columns[1, 1 : S + 1] = right_line
    for corner in range(4):
        at = 0 if corner < 2 else S + 1
        columns[(0, 1, 1, 0)[corner], at : at + 1] = ends[corner : corner + 1, :C2]

    def shift_partner(row, carry):
        x = unpack(packed_other[row // 5, lax.rem(row, 5)].astype(F32))
        spread_columns(
            shifted, row, slice(0, C2), x, columns[0, pl.ds(row, 1)], columns[1, pl.ds(row, 1)]
        )
        return carry

    lax.fori_loop(0, S + 2, shift_partner, 0)
    for copy in gz_copies:
        copy.wait_recv()
    spot = gathered.at[core, y, xl]
    gx_copy = remote(spot, spot, gx_sems.at[0], gx_sems.at[1], near)
    gx_copy.start()

    for copy in piece_copies:
        copy.wait_recv()
    for offset in OFFSETS:
        k = slot_of(-offset)
        source = wrap(tile - offset, tiles)
        for border in range(4):
            hit = edge_tiles[source, border] == tile
            slot = lookup(EDGE_TABLE, border, edge_turns[source, border])
            rev = slot // 4
            ii = iota2((S, 1), 0)
            target = jnp.where(rev == 1, S - 1 - ii, ii) + (slot - 4 * rev) * S
            hot = one_hot_rows(S, jnp.where(hit, target, -1), 4 * S)
            hits[0, k, border] = hot[:16]
            hits[1, k, border] = hot[16:]
        ii = iota2((16, 1), 0)
        target = jnp.full((16, 1), -1, jnp.int32)
        for corner in range(4):
            hit = corner_tiles[source, corner] == tile
            slot = lookup(CORNER_TABLE, corner, corner_turns[source, corner])
            cell = jnp.where(slot < 2, 0, 2 * S) + jnp.where((slot == 0) | (slot == 3), 0, S - 1)
            target = jnp.where((ii == corner) & hit, cell, target)
        hits[0, k, 4] = one_hot_rows(16, target, 4 * S)
        hits[1, k, 4] = jnp.zeros((16, 4 * S), BF)
    flat = all_pieces[...].reshape(8 * 5 * 16, C)
    parts = [
        lax.dot_general(hits[i].reshape(8 * 5 * 16, 4 * S), flat, TN, preferred_element_type=F32)
        for i in range(2)
    ]
    sums[...] = (parts[0][:, :C2] + parts[1][:, C2:]).reshape(4, S, C2)
    gx_copy.wait_recv()
    spot = gathered.at[core, y]
    gy_copies = [remote(spot, spot, gy_sems.at[0, j], gy_sems.at[1, j], y_peer[j]) for j in range(3)]
    for copy in gy_copies:
        copy.start()
    gp_copies = []
    for j in range(4):
        q = y if j == 0 else lax.rem(y + 4 - j, 4)
        spot = gathered.at[core, q]
        gp_copies.append(remote(spot, spot, gp_sems.at[0, j], gp_sems.at[1, j], pair))
    gp_copies[0].start()

    def add_sides(row, carry):
        io = iota2((S, C2), 0)
        x = interior[row + 1]
        x = x + jnp.where(io == 0, sums[3, pl.ds(row, 1)], 0.0)
        x = x + jnp.where(io == S - 1, sums[1, pl.ds(row, 1)], 0.0)
        x = x + jnp.where(row == 0, sums[0], 0.0)
        x = x + jnp.where(row == S - 1, sums[2], 0.0)
        grad_features[row] = x.astype(BF)
        return carry

    lax.fori_loop(0, S, add_sides, 0)

    def convolve_other(block, carry):
        total = partial_out[pl.ds(block * rows, rows)].reshape(rows * S, C2)
        for a in range(3):
            for b in range(3):
                window = shifted[b, pl.ds(block * rows + a, rows)].reshape(rows * S, C2)
                total = total + jnp.dot(window, out_weight[1, 3 * a + b], preferred_element_type=F32)
        output[pl.ds(block * rows, rows)] = total.reshape(rows, S, C2).astype(BF)
        return carry

    lax.fori_loop(0, 2, convolve_other, 0)

    for j in range(3):
        gy_copies[j].wait_recv()
        gp_copies[j + 1].start()
    swap_a.finish_sends()
    swap_b.finish_sends()
    for copy in gp_copies:
        copy.wait()
    x_copy.wait_send()
    gx_copy.wait_send()
    for copy in side_copies + piece_copies + pair_copies + y_copies + z_copies + gz_copies + gy_copies:
        copy.wait_send()


VSPEC = pl.BlockSpec(memory_space=VM)
ANY = pl.BlockSpec(memory_space=pl.ANY)
DMA = pltpu.SemaphoreType.DMA
SM = pltpu.SMEM


def body(features, weight, cotangent, edge_tiles, edge_turns, corner_tiles, corner_turns):
    field = features[0]
    C2 = field.shape[2]
    C = 2 * C2
    shape = jax.ShapeDtypeStruct
    table = SM((128, 4), jnp.int32)
    output, grad_features, gathered = pl.pallas_call(
        lambda *refs: fused_kernel(1.0 / math.sqrt(128 * ROWS), *refs),
        name="fused",
        out_shape=(
            shape((S, S, C2), BF),
            shape((S, S, C2), BF),
            shape((2, 4, 2, 8, UNIT, C), BF),
        ),
        in_specs=[ANY] * 7,
        out_specs=(VSPEC,) * 3,
        scratch_shapes=[
            table, table, table, table,
            VM((S, S, C2), BF),
            VM((S, S, C2), BF),
            VM((9, C, C), BF),
            VM((9, C2, C), BF),
            VM((2, 9, C2, C2), BF),
            VM((2, S, C2), F32),
            VM((4, 16, C), BF),
            VM((8, 4, 16, C), BF),
            VM((8, 64, C), BF),
            VM((8, 64, C), BF),
            VM((2, 4, 64, C), BF),
            VM((3, S + 2, S, C2), BF),
            VM((2, 40, C2), F32),
            VM((3, S + 4, S, C), BF),
            VM((2, 48, C), F32),
            VM((2, 56 * UNIT, C), F32),
            VM((S + 2, S, C2), F32),
            VM((5, 16, C), BF),
            VM((8, 5, 16, C), BF),
            VM((8, 5, 16, C), BF),
            VM((8, 5, 16, C), BF),
            VM((2, 4, 5, 16, C), BF),
            VM((3, S + 2, S, C2), BF),
            VM((S, S, C2), F32),
            VM((2, 8, 5, 16, 4 * S), BF),
            VM((4, S, C2), F32),
            VM((4, 14 * UNIT, C), F32),
            VM((3, 14 * UNIT, C), BF),
            VM((3, 14 * UNIT, C), BF),
            VM((2, 7 * UNIT, C), F32),
            VM((7 * UNIT, C), F32),
            VM((8, UNIT, C), F32),
            VM((7, UNIT, C), F32),
            DMA((7,)),
            DMA((2, 8)),
            DMA((4, 8)),
            DMA((4, 8)),
            DMA((2, 8)),
            DMA((2, 4)),
            DMA((2, 3)),
            DMA((2,)),
            DMA((2, 7)),
            DMA((2, 7)),
            DMA((2,)),
            DMA((2, 3)),
            DMA((2, 4)),
        ],
        compiler_params=pltpu.CompilerParams(
            vmem_limit_bytes=60 * 1024 * 1024, collective_id=0, has_side_effects=True
        ),
    )(edge_tiles, edge_turns, corner_tiles, corner_turns, field, cotangent[0], weight.reshape(9, C, C))

    flat = gathered[:, :, :, :7].reshape(2, 56 * UNIT, C)[:, : 9 * (C2 // 2)]
    grad_weight = flat.reshape(2, 9, C2 // 2, C).transpose(1, 0, 2, 3).astype(F32).reshape(3, 3, C2, C)
    return (output[None], grad_features[None], grad_weight)


def solution(mesh):
    return jax.shard_map(
        body,
        mesh=mesh,
        in_specs=(
            P("tile", None, None, "ch"),
            P(),
            P("tile", None, None, "ch"),
            P(),
            P(),
            P(),
            P(),
        ),
        out_specs=(
            P("tile", None, None, "ch"),
            P("tile", None, None, "ch"),
            P(None, None, "ch", None),
        ),
        check_vma=False,
    )
```

```python
import math

import jax
import jax.numpy as jnp
import numpy as np
from jax import lax
from jax.experimental import pallas as pl
from jax.experimental.pallas import tpu as pltpu
from jax.sharding import PartitionSpec as P

MESH = pl.DeviceIdType.MESH
SPAN = 4
OFFSETS = [-4, -3, -2, -1, 1, 2, 3, 4]
S = 32
ROWS = S * S
UNIT = 16
VM = pltpu.VMEM
BF = jnp.bfloat16
F32 = jnp.float32


def turn_tables():
    labels = [[3 * row + col for col in range(3)] for row in range(3)]

    def turn_once(block):
        return [[block[col][2 - row] for col in range(3)] for row in range(3)]

    def sides_of(block):
        return [
            list(block[0]),
            [block[row][2] for row in range(3)],
            list(block[2]),
            [block[row][0] for row in range(3)],
        ]

    def corners_of(block):
        return [block[0][0], block[0][2], block[2][2], block[2][0]]

    base_sides = sides_of(labels)
    base_corners = corners_of(labels)
    edge_table = np.zeros((4, 4), np.int32)
    corner_table = np.zeros((4, 4), np.int32)
    for border in range(4):
        turned = labels
        for quarter in range(4):
            wanted = sides_of(turned)[(border + 2) % 4]
            for side_index in range(4):
                if base_sides[side_index] == wanted:
                    edge_table[border, quarter] = side_index
                if base_sides[side_index][::-1] == wanted:
                    edge_table[border, quarter] = side_index + 4
            corner_cell = corners_of(turned)[(border + 2) % 4]
            for corner_index in range(4):
                if base_corners[corner_index] == corner_cell:
                    corner_table[border, quarter] = corner_index
            turned = turn_once(turned)
    return (edge_table, corner_table)


EDGE_TABLE, CORNER_TABLE = turn_tables()


def lookup(table, border, turn):
    row = [int(v) for v in table[border]]
    value = jnp.int32(row[0])
    for quarter in range(1, 4):
        value = jnp.where(turn == quarter, jnp.int32(row[quarter]), value)
    return value


def slot_of(offset):
    return offset + SPAN if offset < 0 else offset + SPAN - 1


def wrap(index, size):
    return lax.rem(index + size, jnp.int32(size))


def coords():
    tile = lax.axis_index("tile")
    ch = lax.axis_index("ch")
    core = lax.rem(tile, 2)
    y = lax.rem(tile // 2, 4)
    xl = lax.rem(tile // 8, 2)
    z = tile // 16
    return tile, ch, core, y, xl, z


def dev(tile, ch):
    return {"tile": tile, "ch": ch}


def x_neighbours(tile, ch, xl):
    beside = tile + 8 - 16 * xl
    return dev(beside, ch), dev(beside, 1 - ch)


def remote(src, dst, send, recv, where):
    return pltpu.make_async_remote_copy(
        src_ref=src, dst_ref=dst, send_sem=send, recv_sem=recv, device_id=where, device_id_type=MESH
    )


class Swap:
    def __init__(self, src, dst, relay, sems, tile, ch, xl):
        self.n = relay.shape[1]
        near, far = x_neighbours(tile, ch, xl)
        self.first, self.second = [], []
        for i in range(self.n):
            for path in range(2):
                hop1, hop2 = (near, far) if path == 0 else (far, near)
                j = path * self.n + i
                self.first.append(remote(src.at[j], relay.at[path, i], sems.at[0, j], sems.at[1, j], hop1))
                self.second.append(remote(relay.at[path, i], dst.at[j], sems.at[2, j], sems.at[3, j], hop2))

    def start(self):
        for copy in self.first:
            copy.start()

    def relay(self):
        for one, two in zip(self.first, self.second):
            one.wait_recv()
            two.start()

    def finish_sends(self):
        for one, two in zip(self.first, self.second):
            one.wait_send()
            two.wait_send()


def near_copies(src, dst, sems, tile, ch, tiles):
    copies = []
    for offset in OFFSETS:
        k = slot_of(-offset)
        copies.append(
            remote(src, dst.at[k], sems.at[0, k], sems.at[1, k], dev(wrap(tile + offset, tiles), ch))
        )
    return copies


def iota2(shape, dim):
    return lax.broadcasted_iota(jnp.int32, shape, dim)


def source_slot(target, tile, tiles):
    away = wrap(target - tile, tiles)
    return jnp.clip(jnp.where(away > tiles // 2, away - tiles + SPAN, away + SPAN - 1), 0, 2 * SPAN - 1)


def spread_columns(buf, row, lanes, x, left, right):
    io = iota2(x.shape, 0)
    buf[1, row, :, lanes] = x.astype(BF)
    buf[0, row, :, lanes] = jnp.where(io == 0, left, pltpu.roll(x, 1, 0)).astype(BF)
    buf[2, row, :, lanes] = jnp.where(io == S - 1, right, pltpu.roll(x, S - 1, 0)).astype(BF)


def pack(x):
    n = x.shape[0] // 2
    return jnp.concatenate([x[:n, :128], x[n:, :128], x[:n, 128:], x[n:, 128:]], axis=1)


def unpack(x):
    low = jnp.concatenate([x[:, :128], x[:, 256:320]], axis=1)
    high = jnp.concatenate([x[:, 128:256], x[:, 320:]], axis=1)
    return jnp.concatenate([low, high], axis=0)


def one_hot_rows(rows, target, width):
    return jnp.where(iota2((rows, width), 1) == target, 1.0, 0.0).astype(BF)


TN = (((0,), (0,)), ((), ()))
NT = (((1,), (1,)), ((), ()))
CHUNK = 14 * UNIT


class Reduce:
    def __init__(self, scale, bufs, sems, place):
        self.grads, self.pair_in, self.y_out, self.y_in, self.acc, self.x_in, self.z_out, self.z_in, self.gathered = bufs
        self.scale = scale
        tile, ch, core, y, xl, z = self.place = place
        self.near, _ = x_neighbours(tile, ch, xl)
        self.pair = dev(tile + 1 - 2 * core, ch)
        self.y_at = [lax.rem(y + 1 + j, 4) for j in range(3)]
        self.y_peer = [dev(tile + 2 * (q - y), ch) for q in self.y_at]
        self.z_at = [lax.rem(z + 1 + j, 8) for j in range(7)]
        self.z_from = [lax.rem(z + 7 - j, 8) for j in range(7)]
        self.z_peer = [dev(tile + 16 * (q - z), ch) for q in self.z_at]
        self.order = self.y_at + [y]
        pair_sems, y_sems, x_sems, z_sems, gz_sems, gx_sems, gy_sems, gp_sems = sems
        self.pair_copies = []
        for j, q in enumerate(self.order):
            part = self.grads.at[1 - core, pl.ds(pl.multiple_of(q * CHUNK, CHUNK), CHUNK)]
            self.pair_copies.append(
                remote(part, self.pair_in.at[j], pair_sems.at[0, j], pair_sems.at[1, j], self.pair)
            )
        self.y_copies = [
            remote(self.y_out.at[j], self.y_in.at[j], y_sems.at[0, j], y_sems.at[1, j], self.y_peer[j])
            for j in range(3)
        ]
        self.x_copy = remote(self.acc.at[1 - xl], self.x_in, x_sems.at[0], x_sems.at[1], self.near)
        own = jnp.minimum(z, 6)
        self.z_copies, self.gz_copies = [], []
        for j in range(7):
            part = self.z_out.at[jnp.minimum(self.z_at[j], 6)]
            self.z_copies.append(remote(part, self.z_in.at[j], z_sems.at[0, j], z_sems.at[1, j], self.z_peer[j]))
            spot = self.gathered.at[core, y, xl, own]
            self.gz_copies.append(remote(spot, spot, gz_sems.at[0, j], gz_sems.at[1, j], self.z_peer[j]))
        spot = self.gathered.at[core, y, xl]
        self.gx_copy = remote(spot, spot, gx_sems.at[0], gx_sems.at[1], self.near)
        self.gy_copies, self.gp_copies = [], []
        for k in range(2):
            half = xl if k == 0 else 1 - xl
            spot = self.gathered.at[core, y, half]
            for j in range(3):
                self.gy_copies.append(
                    remote(spot, spot, gy_sems.at[0, k, j], gy_sems.at[1, k, j], self.y_peer[j])
                )
            for j in range(4):
                q = y if j == 0 else lax.rem(y + 4 - j, 4)
                spot = self.gathered.at[core, q, half]
                self.gp_copies.append(remote(spot, spot, gp_sems.at[0, k, j], gp_sems.at[1, k, j], self.pair))

    def start(self):
        for copy in self.pair_copies:
            copy.start()

    def to_y(self):
        core = self.place[2]
        for j in range(4):
            self.pair_copies[j].wait_recv()
            at = pl.multiple_of(self.order[j] * CHUNK, CHUNK)
            total = self.grads[core, pl.ds(at, CHUNK)] + self.pair_in[j]
            if j < 3:
                self.y_out[j] = total.astype(BF)
                self.y_copies[j].start()
            else:
                self.acc[...] = total.reshape(self.acc.shape)

    def to_x(self):
        for j in range(3):
            self.y_copies[j].wait_recv()
            self.acc[...] += self.y_in[j].astype(F32).reshape(self.acc.shape)
        self.x_copy.start()

    def to_z(self):
        xl, z = self.place[4:]
        self.x_copy.wait_recv()
        self.z_out[...] = (self.acc[xl] + self.x_in[...]).reshape(self.z_out.shape)
        for j in range(7):
            pl.when(self.z_at[j] != 7)(self.z_copies[j].start)

    def to_gz(self):
        tile, ch, core, y, xl, z = self.place

        @pl.when(z != 7)
        def _():
            own = jnp.minimum(z, 6)
            total = self.z_out[own]
            for j in range(7):
                self.z_copies[j].wait_recv()
                total = total + self.z_in[j]
            self.gathered[core, y, xl, own] = (total * self.scale).astype(BF)
            for copy in self.gz_copies:
                copy.start()

    def to_gx(self):
        for j in range(7):
            pl.when(self.z_from[j] != 7)(self.gz_copies[j].wait_recv)
        self.gx_copy.start()
        for copy in self.gy_copies[:3]:
            copy.start()
        self.gp_copies[0].start()

    def to_gy(self):
        self.gx_copy.wait_recv()
        for copy in self.gy_copies[3:]:
            copy.start()
        self.gp_copies[4].start()

    def to_pair(self):
        for k in range(2):
            for j in range(3):
                self.gy_copies[3 * k + j].wait_recv()
                self.gp_copies[4 * k + j + 1].start()

    def finish(self):
        z = self.place[5]
        for copy in self.gp_copies:
            copy.wait()
        for copy in self.pair_copies + self.y_copies + [self.x_copy, self.gx_copy] + self.gy_copies:
            copy.wait_send()
        for j in range(7):
            pl.when(self.z_at[j] != 7)(self.z_copies[j].wait_send)
            pl.when(z != 7)(self.gz_copies[j].wait_send)


def fused_kernel(
    scale,
    edge_tiles_in, edge_turns_in, corner_tiles_in, corner_turns_in, feat_in, cot_in, weight_in,
    output, grad_features, gathered_1, gathered_2,
    edge_tiles, edge_turns, corner_tiles, corner_turns,
    feat, cot, weight, rows_weight, out_weight,
    lines, sides, all_sides, cot_packed, cot_other, relay_a,
    padded, columns, cots, cot_columns, interior, pieces, all_pieces,
    packed, packed_other, relay_b, shifted, partial_out, hits, sums,
    load_sems, side_sems, swap_a_sems, swap_b_sems, piece_sems,
    *streams,
):
    tiles = 128
    place = tile, ch, core, y, xl, z = coords()
    C2 = feat.shape[2]
    C = 2 * C2
    near, far = x_neighbours(tile, ch, xl)
    bufs = len(REDUCE_BUFS)
    sems = len(REDUCE_SEMS)
    first = Reduce(scale, streams[:bufs] + (gathered_1,), streams[bufs : bufs + sems], place)
    streams = streams[bufs + sems :]
    second = Reduce(scale, streams[:bufs] + (gathered_2,), streams[bufs:], place)
    greeted = [dev(wrap(tile + o, tiles), ch) for o in OFFSETS] + [near, far, first.pair]
    greeted = greeted + first.y_peer + first.z_peer
    ready = pltpu.get_barrier_semaphore()
    for where in greeted:
        pl.semaphore_signal(ready, inc=1, device_id=where, device_id_type=MESH)

    own_rows = pl.ds(pl.multiple_of(ch * C2, 64), C2)
    loads = [
        pltpu.make_async_copy(a, b, load_sems.at[i])
        for i, (a, b) in enumerate(
            (
                (feat_in, feat),
                (cot_in, cot),
                (edge_tiles_in, edge_tiles),
                (edge_turns_in, edge_turns),
                (corner_tiles_in, corner_tiles),
                (corner_turns_in, corner_turns),
                (weight_in, weight),
                (weight_in.at[:, own_rows], rows_weight),
            )
        )
    ]
    for load in loads:
        load.start()

    loads[0].wait()

    def take_columns(row, carry):
        x = feat[row].astype(F32)
        lines[0, pl.ds(row, 1)] = x[0:1]
        lines[1, pl.ds(row, 1)] = x[S - 1 : S]
        return carry

    lax.fori_loop(0, S, take_columns, 0, unroll=4)
    sides[0] = pack(feat[0])
    sides[1] = pack(lines[1].astype(BF))
    sides[2] = pack(feat[S - 1])
    sides[3] = pack(lines[0].astype(BF))
    loads[1].wait()

    def pack_cot(row, carry):
        for i in range(4):
            cot_packed[row, 16 * i : 16 * i + 16] = pack(cot[4 * row + i])
        return carry

    lax.fori_loop(0, S // 4, pack_cot, 0)
    pl.semaphore_wait(ready, len(greeted))
    swap_a = Swap(cot_packed, cot_other, relay_a, swap_a_sems, tile, ch, xl)
    swap_a.start()
    side_copies = near_copies(sides, all_sides, side_sems, tile, ch, tiles)
    for copy in side_copies:
        copy.start()

    zero = jnp.zeros((S, C), BF)
    for part in range(3):
        for row in (0, 1, S + 2, S + 3):
            cots[part, row] = zero
    cot_columns[...] = jnp.zeros_like(cot_columns)
    nothing = jnp.zeros((1, C2), F32)

    def fill(read, lanes):
        def shift(row, carry):
            x = read(row).astype(F32)
            spread_columns(cots, row + 2, lanes, x, nothing, nothing)
            cot_columns[0, pl.ds(row + 2, 1), lanes] = x[0:1]
            cot_columns[1, pl.ds(row + 2, 1), lanes] = x[S - 1 : S]
            return carry

        lax.fori_loop(0, S, shift, 0, unroll=4)

    def read_other(row):
        at = pl.multiple_of(lax.rem(row, 4) * 16, 16)
        return unpack(cot_other[row // 4, pl.ds(at, 16)])

    pl.when(ch == 0)(lambda: fill(lambda row: cot[row], slice(0, C2)))
    pl.when(ch == 1)(lambda: fill(lambda row: cot[row], slice(C2, C)))
    swap_a.relay()

    for i in range(2, 6):
        loads[i].wait()
    for copy in side_copies:
        copy.wait_recv()
    halos = []
    for border in range(4):
        source = source_slot(edge_tiles[border, tile], tile, tiles)
        slot = lookup(EDGE_TABLE, border, edge_turns[border, tile])
        rev = slot // 4
        x = unpack(all_sides[source, slot - 4 * rev])
        ii = iota2((S, 1), 0)
        hot = one_hot_rows(S, jnp.where(rev == 1, S - 1 - ii, ii), S)
        halos.append(jnp.dot(hot, x, preferred_element_type=F32))
    columns[0, 1 : S + 1] = halos[3]
    columns[1, 1 : S + 1] = halos[1]
    for corner in range(4):
        source = source_slot(corner_tiles[corner, tile], tile, tiles)
        slot = lookup(CORNER_TABLE, corner, corner_turns[corner, tile])
        cells = unpack(all_sides[source, jnp.where(slot < 2, 0, 2)]).astype(F32)
        start = (slot == 0) | (slot == 3)
        at = 0 if corner < 2 else S + 1
        columns[(0, 1, 1, 0)[corner], at : at + 1] = jnp.where(start, cells[0:1], cells[S - 1 : S])
    padded[1, 0] = halos[0].astype(BF)
    padded[1, S + 1] = halos[2].astype(BF)
    padded[1, 1 : S + 1] = feat[...]

    def shift_features(row, carry):
        packed[row // 5, lax.rem(row, 5)] = pack(padded[1, row])
        x = padded[1, row].astype(F32)
        spread_columns(
            padded, row, slice(0, C2), x, columns[0, pl.ds(row, 1)], columns[1, pl.ds(row, 1)]
        )
        return carry

    lax.fori_loop(0, S + 2, shift_features, 0, unroll=2)
    packed[6, 4] = pack(columns[0, 1 : S + 1].astype(BF))
    packed[7, 0] = pack(columns[1, 1 : S + 1].astype(BF))
    io = iota2((16, C2), 0)
    ends = jnp.zeros((16, C2), F32)
    for corner in range(4):
        at = 0 if corner < 2 else S + 1
        ends = jnp.where(io == corner, columns[(0, 1, 1, 0)[corner], at : at + 1], ends)
    packed[7, 1] = pack(jnp.concatenate([ends, ends], axis=0).astype(BF))
    for i in range(2, 5):
        packed[7, i] = jnp.zeros((16, C), BF)
    swap_b = Swap(packed, packed_other, relay_b, swap_b_sems, tile, ch, xl)
    swap_b.start()

    def weight_grad(stream, at):
        width = stream.grads.shape[2]
        lanes = pl.ds(pl.multiple_of(at, 128), width)
        block = C2 // 2

        def one_tap(tap, carry):
            a, b = tap // 3, lax.rem(tap, 3)
            window = padded[b, pl.ds(a, S)].reshape(ROWS, C2)
            full = cots[1, 2 : S + 2, :, lanes].reshape(ROWS, width)
            part = lax.dot_general(window, full, TN, preferred_element_type=F32)
            for i in range(2):
                index = 2 * tap + i
                half = index // 9
                spot = pl.multiple_of((index - 9 * half) * block, 32)
                stream.grads[half, pl.ds(spot, block)] = part[i * block : (i + 1) * block]
            return carry

        lax.fori_loop(0, 9, one_tap, 0)
        filled = 9 * block
        stream.grads[:, filled:] = jnp.zeros((2, stream.grads.shape[1] - filled, width), F32)

    weight_grad(first, 256 * ch)
    first.start()
    first.to_y()
    for copy in swap_a.second:
        copy.wait_recv()
    pl.when(ch == 0)(lambda: fill(read_other, slice(C2, C)))
    pl.when(ch == 1)(lambda: fill(read_other, slice(0, C2)))
    weight_grad(second, 128 - 128 * ch)
    second.start()
    swap_b.relay()
    second.to_y()
    first.to_x()

    loads[7].wait()
    half = (S + 2) // 2

    def feature_grad(block, carry):
        total = None
        for a in range(3):
            for b in range(3):
                window = cots[2 - b, pl.ds(block * half + 2 - a, half)].reshape(half * S, C)
                term = lax.dot_general(window, rows_weight[3 * a + b], NT, preferred_element_type=F32)
                total = term if total is None else total + term
        interior[pl.ds(block * half, half)] = total.reshape(half, S, C2)
        return carry

    lax.fori_loop(0, 2, feature_grad, 0)
    first.to_z()
    pieces[0] = pack(interior[0].astype(BF))
    pieces[2] = pack(interior[S + 1].astype(BF))
    tips = []
    for side in range(2):
        total = None
        for a in range(3):
            line = cot_columns[side, 2 - a : 2 - a + 40].astype(BF)
            term = lax.dot_general(line, rows_weight[3 * a + 2 * side], NT, preferred_element_type=F32)
            total = term if total is None else total + term
        cot_columns[side, 0:40, 0:C2] = total
        pieces[3 - 2 * side] = pack(cot_columns[side, 1 : S + 1, 0:C2].astype(BF))
        tips.append((total[0:1], total[S + 1 : S + 2]))
    io = iota2((16, C2), 0)
    ends = jnp.zeros((16, C2), F32)
    for corner, value in enumerate((tips[0][0], tips[1][0], tips[1][1], tips[0][1])):
        ends = jnp.where(io == corner, value, ends)
    pieces[4] = pack(jnp.concatenate([ends, ends], axis=0).astype(BF))
    second.to_x()
    piece_copies = near_copies(pieces, all_pieces, piece_sems, tile, ch, tiles)
    for copy in piece_copies:
        copy.start()
    loads[6].wait()

    def pick_weight(tap, carry):
        for part in range(2):
            input_half = ch if part == 0 else 1 - ch
            w = weight[tap, pl.ds(pl.multiple_of(input_half * C2, 64), C2)].astype(F32)
            out_weight[part, tap] = jnp.where(ch == 0, w[:, :C2], w[:, C2:]).astype(BF)
        return carry

    lax.fori_loop(0, 9, pick_weight, 0)
    second.to_z()
    first.to_gz()

    rows = S // 2

    def convolve_own(block, carry):
        total = None
        for a in range(3):
            for b in range(3):
                window = padded[b, pl.ds(block * rows + a, rows)].reshape(rows * S, C2)
                term = jnp.dot(window, out_weight[0, 3 * a + b], preferred_element_type=F32)
                total = term if total is None else total + term
        partial_out[pl.ds(block * rows, rows)] = total.reshape(rows, S, C2)
        return carry

    lax.fori_loop(0, 2, convolve_own, 0)
    first.to_gx()

    for copy in swap_b.second:
        copy.wait_recv()
    columns[0, 1 : S + 1] = unpack(packed_other[6, 4]).astype(F32)
    columns[1, 1 : S + 1] = unpack(packed_other[7, 0]).astype(F32)
    ends = unpack(packed_other[7, 1]).astype(F32)
    for corner in range(4):
        at = 0 if corner < 2 else S + 1
        columns[(0, 1, 1, 0)[corner], at : at + 1] = ends[corner : corner + 1]

    def shift_partner(row, carry):
        x = unpack(packed_other[row // 5, lax.rem(row, 5)]).astype(F32)
        spread_columns(
            shifted, row, slice(0, C2), x, columns[0, pl.ds(row, 1)], columns[1, pl.ds(row, 1)]
        )
        return carry

    lax.fori_loop(0, S + 2, shift_partner, 0, unroll=2)
    second.to_gz()
    first.to_gy()

    for copy in piece_copies:
        copy.wait_recv()
    for offset in OFFSETS:
        k = slot_of(-offset)
        source = wrap(tile - offset, tiles)
        for border in range(4):
            hit = edge_tiles[border, source] == tile
            slot = lookup(EDGE_TABLE, border, edge_turns[border, source])
            rev = slot // 4
            ii = iota2((S, 1), 0)
            target = jnp.where(rev == 1, S - 1 - ii, ii) + (slot - 4 * rev) * S
            hot = one_hot_rows(S, jnp.where(hit, target, -1), 4 * S)
            hits[0, k, border] = hot[:16]
            hits[1, k, border] = hot[16:]
        ii = iota2((16, 1), 0)
        target = jnp.full((16, 1), -1, jnp.int32)
        for corner in range(4):
            hit = corner_tiles[corner, source] == tile
            slot = lookup(CORNER_TABLE, corner, corner_turns[corner, source])
            cell = jnp.where(slot < 2, 0, 2 * S) + jnp.where((slot == 0) | (slot == 3), 0, S - 1)
            target = jnp.where((ii == corner) & hit, cell, target)
        hits[0, k, 4] = one_hot_rows(16, target, 4 * S)
        hits[1, k, 4] = jnp.zeros((16, 4 * S), BF)
    flat = all_pieces[...].reshape(8 * 5 * 16, C)
    parts = [
        lax.dot_general(hits[i].reshape(8 * 5 * 16, 4 * S), flat, TN, preferred_element_type=F32)
        for i in range(2)
    ]
    low = jnp.concatenate([parts[0][:, :128], parts[0][:, 256:320]], axis=1)
    high = jnp.concatenate([parts[1][:, 128:256], parts[1][:, 320:]], axis=1)
    sums[...] = (low + high).reshape(4, S, C2)
    second.to_gx()

    def add_sides(row, carry):
        io = iota2((S, C2), 0)
        x = interior[row + 1]
        x = x + jnp.where(io == 0, sums[3, pl.ds(row, 1)], 0.0)
        x = x + jnp.where(io == S - 1, sums[1, pl.ds(row, 1)], 0.0)
        x = x + jnp.where(row == 0, sums[0], 0.0)
        x = x + jnp.where(row == S - 1, sums[2], 0.0)
        grad_features[0, row] = x.astype(BF)
        return carry

    lax.fori_loop(0, S, add_sides, 0)
    first.to_pair()
    second.to_gy()

    def convolve_other(block, carry):
        total = partial_out[pl.ds(block * rows, rows)].reshape(rows * S, C2)
        for a in range(3):
            for b in range(3):
                window = shifted[b, pl.ds(block * rows + a, rows)].reshape(rows * S, C2)
                total = total + jnp.dot(window, out_weight[1, 3 * a + b], preferred_element_type=F32)
        output[0, pl.ds(block * rows, rows)] = total.reshape(rows, S, C2).astype(BF)
        return carry

    lax.fori_loop(0, 2, convolve_other, 0)
    second.to_pair()
    swap_a.finish_sends()
    swap_b.finish_sends()
    for copy in side_copies + piece_copies:
        copy.wait_send()
    first.finish()
    second.finish()


VSPEC = pl.BlockSpec(memory_space=VM)
ANY = pl.BlockSpec(memory_space=pl.ANY)
DMA = pltpu.SemaphoreType.DMA
SM = pltpu.SMEM
REDUCE_BUFS = [
    ((2, 4 * CHUNK), F32),
    ((4, CHUNK), F32),
    ((3, CHUNK), BF),
    ((3, CHUNK), BF),
    ((2, CHUNK // 2), F32),
    ((CHUNK // 2,), F32),
    ((7, UNIT), F32),
    ((7, UNIT), F32),
]
REDUCE_SEMS = [(2, 4), (2, 3), (2,), (2, 7), (2, 7), (2,), (2, 2, 3), (2, 2, 4)]


def reduce_scratch(width):
    return [VM(lead + (width,), kind) for lead, kind in REDUCE_BUFS] + [DMA(lead) for lead in REDUCE_SEMS]


def body(features, weight, cotangent, edge_tiles, edge_turns, corner_tiles, corner_turns):
    C2 = features.shape[3]
    C = 2 * C2
    shape = jax.ShapeDtypeStruct
    table = SM((4, 128), jnp.int32)
    output, grad_features, own_lanes, more_lanes = pl.pallas_call(
        lambda *refs: fused_kernel(1.0 / math.sqrt(128 * ROWS), *refs),
        name="fused",
        out_shape=(
            shape((1, S, S, C2), BF),
            shape((1, S, S, C2), BF),
            shape((2, 4, 2, 7, UNIT, 128), BF),
            shape((2, 4, 2, 7, UNIT, 256), BF),
        ),
        in_specs=[ANY] * 7,
        out_specs=(VSPEC,) * 4,
        scratch_shapes=[
            table, table, table, table,
            VM((S, S, C2), BF),
            VM((S, S, C2), BF),
            VM((9, C, C), BF),
            VM((9, C2, C), BF),
            VM((2, 9, C2, C2), BF),
            VM((2, S, C2), F32),
            VM((4, 16, C), BF),
            VM((8, 4, 16, C), BF),
            VM((8, 64, C), BF),
            VM((8, 64, C), BF),
            VM((2, 4, 64, C), BF),
            VM((3, S + 2, S, C2), BF),
            VM((2, 40, C2), F32),
            VM((3, S + 4, S, C), BF),
            VM((2, 48, C), F32),
            VM((S + 2, S, C2), F32),
            VM((5, 16, C), BF),
            VM((8, 5, 16, C), BF),
            VM((8, 5, 16, C), BF),
            VM((8, 5, 16, C), BF),
            VM((2, 4, 5, 16, C), BF),
            VM((3, S + 2, S, C2), BF),
            VM((S, S, C2), F32),
            VM((2, 8, 5, 16, 4 * S), BF),
            VM((4, S, C2), F32),
            DMA((8,)),
            DMA((2, 8)),
            DMA((4, 8)),
            DMA((4, 8)),
            DMA((2, 8)),
        ]
        + reduce_scratch(128)
        + reduce_scratch(256),
        compiler_params=pltpu.CompilerParams(
            vmem_limit_bytes=60 * 1024 * 1024, collective_id=0, has_side_effects=True
        ),
    )(
        edge_tiles.T, edge_turns.T, corner_tiles.T, corner_turns.T,
        features[0], cotangent[0], weight.reshape(9, C, C),
    )

    own_lanes = own_lanes.reshape(2, 4 * CHUNK, 128)[:, : 9 * (C2 // 2)]
    more_lanes = more_lanes.reshape(2, 4 * CHUNK, 256)[:, : 9 * (C2 // 2)]
    grad_weight = jnp.where(
        lax.axis_index("ch") == 0,
        jnp.concatenate([own_lanes, more_lanes], axis=2),
        jnp.concatenate([more_lanes, own_lanes], axis=2),
    )
    return (output, grad_features, grad_weight.astype(F32).reshape(3, 3, C2, C))


def solution(mesh):
    return jax.shard_map(
        body,
        mesh=mesh,
        in_specs=(
            P("tile", None, None, "ch"),
            P(),
            P("tile", None, None, "ch"),
            P(),
            P(),
            P(),
            P(),
        ),
        out_specs=(
            P("tile", None, None, "ch"),
            P("tile", None, None, "ch"),
            P(None, None, "ch", None),
        ),
        check_vma=False,
    )
```

```python
import math

import jax
import jax.numpy as jnp
import numpy as np
from jax import lax
from jax.experimental import pallas as pl
from jax.experimental.pallas import tpu as pltpu
from jax.sharding import PartitionSpec as P

MESH = pl.DeviceIdType.MESH
SPAN = 4
OFFSETS = [-4, -3, -2, -1, 1, 2, 3, 4]
S = 32
ROWS = S * S
UNIT = 16
VM = pltpu.VMEM
BF = jnp.bfloat16
F32 = jnp.float32


def turn_tables():
    labels = [[3 * row + col for col in range(3)] for row in range(3)]

    def turn_once(block):
        return [[block[col][2 - row] for col in range(3)] for row in range(3)]

    def sides_of(block):
        return [
            list(block[0]),
            [block[row][2] for row in range(3)],
            list(block[2]),
            [block[row][0] for row in range(3)],
        ]

    def corners_of(block):
        return [block[0][0], block[0][2], block[2][2], block[2][0]]

    base_sides = sides_of(labels)
    base_corners = corners_of(labels)
    edge_table = np.zeros((4, 4), np.int32)
    corner_table = np.zeros((4, 4), np.int32)
    for border in range(4):
        turned = labels
        for quarter in range(4):
            wanted = sides_of(turned)[(border + 2) % 4]
            for side_index in range(4):
                if base_sides[side_index] == wanted:
                    edge_table[border, quarter] = side_index
                if base_sides[side_index][::-1] == wanted:
                    edge_table[border, quarter] = side_index + 4
            corner_cell = corners_of(turned)[(border + 2) % 4]
            for corner_index in range(4):
                if base_corners[corner_index] == corner_cell:
                    corner_table[border, quarter] = corner_index
            turned = turn_once(turned)
    return (edge_table, corner_table)


EDGE_TABLE, CORNER_TABLE = turn_tables()


def lookup(table, border, turn):
    row = [int(v) for v in table[border]]
    value = jnp.int32(row[0])
    for quarter in range(1, 4):
        value = jnp.where(turn == quarter, jnp.int32(row[quarter]), value)
    return value


def slot_of(offset):
    return offset + SPAN if offset < 0 else offset + SPAN - 1


def wrap(index, size):
    return lax.rem(index + size, jnp.int32(size))


def coords():
    tile = lax.axis_index("tile")
    ch = lax.axis_index("ch")
    core = lax.rem(tile, 2)
    y = lax.rem(tile // 2, 4)
    xl = lax.rem(tile // 8, 2)
    z = tile // 16
    return tile, ch, core, y, xl, z


def dev(tile, ch):
    return {"tile": tile, "ch": ch}


def x_neighbours(tile, ch, xl):
    beside = tile + 8 - 16 * xl
    return dev(beside, ch), dev(beside, 1 - ch)


def remote(src, dst, send, recv, where):
    return pltpu.make_async_remote_copy(
        src_ref=src, dst_ref=dst, send_sem=send, recv_sem=recv, device_id=where, device_id_type=MESH
    )


class Swap:
    def __init__(self, src, dst, relay, sems, tile, ch, xl):
        self.n = relay.shape[1]
        near, far = x_neighbours(tile, ch, xl)
        self.first, self.second = [], []
        for i in range(self.n):
            for path in range(2):
                hop1, hop2 = (near, far) if path == 0 else (far, near)
                j = path * self.n + i
                self.first.append(remote(src.at[j], relay.at[path, i], sems.at[0, j], sems.at[1, j], hop1))
                self.second.append(remote(relay.at[path, i], dst.at[j], sems.at[2, j], sems.at[3, j], hop2))

    def start(self):
        for copy in self.first:
            copy.start()

    def relay(self):
        for one, two in zip(self.first, self.second):
            one.wait_recv()
            two.start()

    def finish_sends(self):
        for one, two in zip(self.first, self.second):
            one.wait_send()
            two.wait_send()


def near_copies(src, dst, sems, tile, ch, tiles):
    copies = []
    for offset in OFFSETS:
        k = slot_of(-offset)
        copies.append(
            remote(src, dst.at[k], sems.at[0, k], sems.at[1, k], dev(wrap(tile + offset, tiles), ch))
        )
    return copies


def iota2(shape, dim):
    return lax.broadcasted_iota(jnp.int32, shape, dim)


def source_slot(target, tile, tiles):
    away = wrap(target - tile, tiles)
    return jnp.clip(jnp.where(away > tiles // 2, away - tiles + SPAN, away + SPAN - 1), 0, 2 * SPAN - 1)


def spread_columns(buf, row, lanes, x, left, right):
    io = iota2(x.shape, 0)
    buf[1, row, :, lanes] = x.astype(BF)
    buf[0, row, :, lanes] = jnp.where(io == 0, left, pltpu.roll(x, 1, 0)).astype(BF)
    buf[2, row, :, lanes] = jnp.where(io == S - 1, right, pltpu.roll(x, S - 1, 0)).astype(BF)


def pack(x):
    n = x.shape[0] // 2
    return jnp.concatenate([x[:n, :128], x[n:, :128], x[:n, 128:], x[n:, 128:]], axis=1)


def unpack(x):
    low = jnp.concatenate([x[:, :128], x[:, 256:320]], axis=1)
    high = jnp.concatenate([x[:, 128:256], x[:, 320:]], axis=1)
    return jnp.concatenate([low, high], axis=0)


def one_hot_rows(rows, target, width):
    return jnp.where(iota2((rows, width), 1) == target, 1.0, 0.0).astype(BF)


TN = (((0,), (0,)), ((), ()))
NT = (((1,), (1,)), ((), ()))
CHUNK = 7 * UNIT


class Reduce:
    def __init__(self, scale, bufs, sems, place, z_first):
        self.grads, self.pair_in, self.sent, self.got, self.unit_out, self.unit_in, self.gathered = bufs
        self.scale = scale
        tile, ch, core, y, xl, z = place
        self.core = core
        self.pair = dev(tile + 1 - 2 * core, ch)
        across = (2 * y + xl, lambda g: dev(tile + 2 * (g // 2 - y) + 8 * (lax.rem(g, 2) - xl), ch))
        along = (z, lambda g: dev(tile + 16 * (g - z), ch))
        (spot, outer), (unit, inner) = (along, across) if z_first else (across, along)
        self.spot, self.unit = spot, unit
        self.order = [lax.rem(spot + 1 + j, 8) for j in range(7)] + [spot]
        self.unit_at = [lax.rem(unit + 1 + j, 8) for j in range(7)]
        self.unit_from = [lax.rem(unit + 7 - j, 8) for j in range(7)]
        self.outer_peers = [outer(g) for g in self.order[:7]]
        self.inner_peers = [inner(g) for g in self.unit_at]
        pair_sems, outer_sems, inner_sems, gather_sems, back_sems, last_sems = sems

        def copy(src, dst, pool, j, where):
            return remote(src, dst, pool.at[0, j], pool.at[1, j], where)

        def rows(half, g):
            return self.grads.at[half, pl.ds(pl.multiple_of(g * CHUNK, CHUNK), CHUNK)]

        self.own = jnp.minimum(unit, 6)
        mine = self.gathered.at[core, spot]
        cell = mine.at[self.own]
        seven = range(7)
        self.pair_copies = [
            copy(rows(1 - core, g), self.pair_in.at[j], pair_sems, j, self.pair)
            for j, g in enumerate(self.order)
        ]
        self.copies = [
            copy(self.sent.at[j], self.got.at[j], outer_sems, j, self.outer_peers[j]) for j in seven
        ]
        self.unit_copies = [
            copy(
                self.unit_out.at[jnp.minimum(self.unit_at[j], 6)], self.unit_in.at[j],
                inner_sems, j, self.inner_peers[j],
            )
            for j in seven
        ]
        self.gather = [copy(cell, cell, gather_sems, j, self.inner_peers[j]) for j in seven]
        self.back = [copy(mine, mine, back_sems, j, self.outer_peers[j]) for j in seven]
        self.last = []
        for j in range(8):
            block = self.gathered.at[core, spot if j == 0 else lax.rem(spot + 8 - j, 8)]
            self.last.append(copy(block, block, last_sems, j, self.pair))

    def own_rows(self, g):
        return self.grads[self.core, pl.ds(pl.multiple_of(g * CHUNK, CHUNK), CHUNK)]

    def start(self):
        for copy in self.pair_copies:
            copy.start()

    def to_outer(self):
        for j in range(7):
            self.pair_copies[j].wait_recv()
            self.sent[j] = (self.own_rows(self.order[j]) + self.pair_in[j]).astype(BF)
            self.copies[j].start()

    def to_inner(self):
        self.pair_copies[7].wait_recv()
        total = self.own_rows(self.spot) + self.pair_in[7]
        for j in range(7):
            self.copies[j].wait_recv()
            total = total + self.got[j].astype(F32)
        self.unit_out[...] = total.reshape(self.unit_out.shape)
        for j in range(7):
            pl.when(self.unit_at[j] != 7)(self.unit_copies[j].start)

    def to_gather(self):
        @pl.when(self.unit != 7)
        def _():
            total = self.unit_out[self.own]
            for j in range(7):
                self.unit_copies[j].wait_recv()
                total = total + self.unit_in[j]
            self.gathered[self.core, self.spot, self.own] = (total * self.scale).astype(BF)
            for copy in self.gather:
                copy.start()

    def to_back(self):
        for j in range(7):
            pl.when(self.unit_from[j] != 7)(self.gather[j].wait_recv)
        for copy in self.back:
            copy.start()
        self.last[0].start()

    def to_pair(self):
        for j in range(7):
            self.back[j].wait_recv()
            self.last[j + 1].start()

    def store(self, out, half, lanes):
        width = self.gathered.shape[4]
        filled = 9 * (out.shape[1] // 4)
        for g in range(8):
            rows = min(CHUNK, filled - g * CHUNK)
            block = self.gathered[half, g].astype(F32).reshape(CHUNK, width)
            out[pl.ds(pl.multiple_of(half * filled + g * CHUNK, 16), rows), lanes] = block[:rows]

    def finish_pair(self):
        for copy in self.last:
            copy.wait()

    def finish(self):
        for copy in self.pair_copies + self.copies + self.back:
            copy.wait_send()
        for j in range(7):
            pl.when(self.unit_at[j] != 7)(self.unit_copies[j].wait_send)
            pl.when(self.unit != 7)(self.gather[j].wait_send)


def fused_kernel(
    scale,
    edge_tiles_in, edge_turns_in, corner_tiles_in, corner_turns_in, feat_in, cot_in, weight_in,
    output, grad_features, grad_weight,
    edge_tiles, edge_turns, corner_tiles, corner_turns,
    feat, cot, weight, rows_weight, out_weight,
    lines, sides, all_sides, cot_packed, cot_other, relay_a,
    padded, columns, cots, cot_columns, interior, pieces, all_pieces,
    packed, packed_other, relay_b, shifted, partial_out, hits, sums, turned,
    load_sems, side_sems, swap_a_sems, swap_b_sems, piece_sems,
    *streams,
):
    tiles = 128
    place = tile, ch, core, y, xl, z = coords()
    C2 = feat.shape[2]
    C = 2 * C2
    near, far = x_neighbours(tile, ch, xl)
    bufs = len(REDUCE_BUFS)
    sems = len(REDUCE_SEMS)
    first, second, third = [
        Reduce(
            scale,
            streams[i * (bufs + sems) : i * (bufs + sems) + bufs],
            streams[i * (bufs + sems) + bufs : (i + 1) * (bufs + sems)],
            place,
            i == 2,
        )
        for i in range(3)
    ]
    greeted = [dev(wrap(tile + o, tiles), ch) for o in OFFSETS] + [near, far, first.pair]
    greeted = greeted + first.outer_peers + first.inner_peers
    ready = pltpu.get_barrier_semaphore()
    for where in greeted:
        pl.semaphore_signal(ready, inc=1, device_id=where, device_id_type=MESH)

    own_rows = pl.ds(pl.multiple_of(ch * C2, 64), C2)
    loads = [
        pltpu.make_async_copy(a, b, load_sems.at[i])
        for i, (a, b) in enumerate(
            (
                (feat_in, feat),
                (cot_in, cot),
                (edge_tiles_in, edge_tiles),
                (edge_turns_in, edge_turns),
                (corner_tiles_in, corner_tiles),
                (corner_turns_in, corner_turns),
                (weight_in, weight),
                (weight_in.at[:, own_rows], rows_weight),
            )
        )
    ]
    for load in loads:
        load.start()

    loads[0].wait()

    def take_columns(row, carry):
        x = feat[row].astype(F32)
        lines[0, pl.ds(row, 1)] = x[0:1]
        lines[1, pl.ds(row, 1)] = x[S - 1 : S]
        return carry

    lax.fori_loop(0, S, take_columns, 0, unroll=4)
    sides[0] = pack(feat[0])
    sides[1] = pack(lines[1].astype(BF))
    sides[2] = pack(feat[S - 1])
    sides[3] = pack(lines[0].astype(BF))
    loads[1].wait()

    def pack_cot(row, carry):
        for i in range(4):
            cot_packed[row, 16 * i : 16 * i + 16] = pack(cot[4 * row + i])
        return carry

    lax.fori_loop(0, S // 4, pack_cot, 0)
    pl.semaphore_wait(ready, len(greeted))
    swap_a = Swap(cot_packed, cot_other, relay_a, swap_a_sems, tile, ch, xl)
    swap_a.start()
    side_copies = near_copies(sides, all_sides, side_sems, tile, ch, tiles)
    for copy in side_copies:
        copy.start()

    zero = jnp.zeros((S, C), BF)
    for part in range(3):
        for row in (0, 1, S + 2, S + 3):
            cots[part, row] = zero
    cot_columns[...] = jnp.zeros_like(cot_columns)
    nothing = jnp.zeros((1, C2), F32)

    def fill(read, lanes):
        def shift(row, carry):
            x = read(row).astype(F32)
            spread_columns(cots, row + 2, lanes, x, nothing, nothing)
            cot_columns[0, pl.ds(row + 2, 1), lanes] = x[0:1]
            cot_columns[1, pl.ds(row + 2, 1), lanes] = x[S - 1 : S]
            return carry

        lax.fori_loop(0, S, shift, 0, unroll=8)

    def read_other(row):
        at = pl.multiple_of(lax.rem(row, 4) * 16, 16)
        return unpack(cot_other[row // 4, pl.ds(at, 16)])

    pl.when(ch == 0)(lambda: fill(lambda row: cot[row], slice(0, C2)))
    pl.when(ch == 1)(lambda: fill(lambda row: cot[row], slice(C2, C)))
    swap_a.relay()

    for i in range(2, 6):
        loads[i].wait()
    for copy in side_copies:
        copy.wait_recv()
    halos = []
    for border in range(4):
        source = source_slot(edge_tiles[border, tile], tile, tiles)
        slot = lookup(EDGE_TABLE, border, edge_turns[border, tile])
        rev = slot // 4
        x = unpack(all_sides[source, slot - 4 * rev])
        ii = iota2((S, 1), 0)
        hot = one_hot_rows(S, jnp.where(rev == 1, S - 1 - ii, ii), S)
        halos.append(jnp.dot(hot, x, preferred_element_type=F32))
    columns[0, 1 : S + 1] = halos[3]
    columns[1, 1 : S + 1] = halos[1]
    for corner in range(4):
        source = source_slot(corner_tiles[corner, tile], tile, tiles)
        slot = lookup(CORNER_TABLE, corner, corner_turns[corner, tile])
        cells = unpack(all_sides[source, jnp.where(slot < 2, 0, 2)]).astype(F32)
        start = (slot == 0) | (slot == 3)
        at = 0 if corner < 2 else S + 1
        columns[(0, 1, 1, 0)[corner], at : at + 1] = jnp.where(start, cells[0:1], cells[S - 1 : S])
    padded[1, 0] = halos[0].astype(BF)
    padded[1, S + 1] = halos[2].astype(BF)
    padded[1, 1 : S + 1] = feat[...]

    def shift_features(row, carry):
        x = padded[1, row].astype(F32)
        spread_columns(
            padded, row, slice(0, C2), x, columns[0, pl.ds(row, 1)], columns[1, pl.ds(row, 1)]
        )
        return carry

    lax.fori_loop(0, S + 2, shift_features, 0, unroll=17)
    for b in range(3):
        turned[b * C2 : (b + 1) * C2] = padded[b].reshape((S + 2) * S, C2).T
    filled = 9 * (C2 // 2)

    def weight_grad(parts, lanes):
        width = 128 * len(parts)
        for a in range(3):
            full = cots[1, 2 - a : 2 - a + S + 2, :, lanes].reshape((S + 2) * S, width)
            result = jnp.dot(turned[...], full, preferred_element_type=F32)
            for i, stream in enumerate(parts):
                for half in range(2):
                    low = max(half * filled, 3 * a * C2)
                    high = min((half + 1) * filled, 3 * (a + 1) * C2)
                    if low < high:
                        stream.grads[half, low - half * filled : high - half * filled] = result[
                            low - 3 * a * C2 : high - 3 * a * C2, 128 * i : 128 * (i + 1)
                        ]
        for stream in parts:
            stream.grads[:, filled:] = jnp.zeros((2, 8 * CHUNK - filled, 128), F32)
            stream.start()

    lanes = [pl.ds(pl.multiple_of(at, 128), 128) for at in (256 * ch, 128 - 128 * ch, 256 - 128 * ch)]
    weight_grad([first], lanes[0])
    for copy in swap_a.second:
        copy.wait_recv()
    pl.when(ch == 0)(lambda: fill(read_other, slice(C2, C)))
    pl.when(ch == 1)(lambda: fill(read_other, slice(0, C2)))
    first.to_outer()
    weight_grad([second, third], pl.ds(pl.multiple_of(128 - 128 * ch, 128), 256))
    second.to_outer()
    third.to_outer()

    def pack_padded(row, carry):
        packed[row // 5, lax.rem(row, 5)] = pack(padded[1, row])
        return carry

    lax.fori_loop(0, S + 2, pack_padded, 0, unroll=2)
    packed[6, 4] = pack(columns[0, 1 : S + 1].astype(BF))
    packed[7, 0] = pack(columns[1, 1 : S + 1].astype(BF))
    io = iota2((16, C2), 0)
    ends = jnp.zeros((16, C2), F32)
    for corner in range(4):
        at = 0 if corner < 2 else S + 1
        ends = jnp.where(io == corner, columns[(0, 1, 1, 0)[corner], at : at + 1], ends)
    packed[7, 1] = pack(jnp.concatenate([ends, ends], axis=0).astype(BF))
    for i in range(2, 5):
        packed[7, i] = jnp.zeros((16, C), BF)
    swap_b = Swap(packed, packed_other, relay_b, swap_b_sems, tile, ch, xl)
    swap_b.start()

    loads[7].wait()
    half = (S + 2) // 2

    def feature_grad(block, carry):
        total = None
        for a in range(3):
            for b in range(3):
                window = cots[2 - b, pl.ds(block * half + 2 - a, half)].reshape(half * S, C)
                term = lax.dot_general(window, rows_weight[3 * a + b], NT, preferred_element_type=F32)
                total = term if total is None else total + term
        interior[pl.ds(block * half, half)] = total.reshape(half, S, C2)
        return carry

    lax.fori_loop(0, 2, feature_grad, 0)
    first.to_inner()
    pieces[0] = pack(interior[0].astype(BF))
    pieces[2] = pack(interior[S + 1].astype(BF))
    tips = []
    for side in range(2):
        total = None
        for a in range(3):
            line = cot_columns[side, 2 - a : 2 - a + 40].astype(BF)
            term = lax.dot_general(line, rows_weight[3 * a + 2 * side], NT, preferred_element_type=F32)
            total = term if total is None else total + term
        cot_columns[side, 0:40, 0:C2] = total
        pieces[3 - 2 * side] = pack(cot_columns[side, 1 : S + 1, 0:C2].astype(BF))
        tips.append((total[0:1], total[S + 1 : S + 2]))
    io = iota2((16, C2), 0)
    ends = jnp.zeros((16, C2), F32)
    for corner, value in enumerate((tips[0][0], tips[1][0], tips[1][1], tips[0][1])):
        ends = jnp.where(io == corner, value, ends)
    pieces[4] = pack(jnp.concatenate([ends, ends], axis=0).astype(BF))
    piece_copies = near_copies(pieces, all_pieces, piece_sems, tile, ch, tiles)
    for copy in piece_copies:
        copy.start()
    loads[6].wait()

    def pick_weight(tap, carry):
        for part in range(2):
            input_half = ch if part == 0 else 1 - ch
            w = weight[tap, pl.ds(pl.multiple_of(input_half * C2, 64), C2)].astype(F32)
            out_weight[part, tap] = jnp.where(ch == 0, w[:, :C2], w[:, C2:]).astype(BF)
        return carry

    lax.fori_loop(0, 9, pick_weight, 0)
    second.to_inner()

    rows = S // 2

    def convolve_own(block, carry):
        total = None
        for a in range(3):
            for b in range(3):
                window = padded[b, pl.ds(block * rows + a, rows)].reshape(rows * S, C2)
                term = jnp.dot(window, out_weight[0, 3 * a + b], preferred_element_type=F32)
                total = term if total is None else total + term
        partial_out[pl.ds(block * rows, rows)] = total.reshape(rows, S, C2)
        return carry

    lax.fori_loop(0, 2, convolve_own, 0)
    first.to_gather()
    swap_b.relay()
    third.to_inner()
    second.to_gather()

    for offset in OFFSETS:
        k = slot_of(-offset)
        source = wrap(tile - offset, tiles)
        for border in range(4):
            hit = edge_tiles[border, source] == tile
            slot = lookup(EDGE_TABLE, border, edge_turns[border, source])
            rev = slot // 4
            ii = iota2((S, 1), 0)
            target = jnp.where(rev == 1, S - 1 - ii, ii) + (slot - 4 * rev) * S
            hot = one_hot_rows(S, jnp.where(hit, target, -1), 4 * S)
            hits[0, k, border] = hot[:16]
            hits[1, k, border] = hot[16:]
        ii = iota2((16, 1), 0)
        target = jnp.full((16, 1), -1, jnp.int32)
        for corner in range(4):
            hit = corner_tiles[corner, source] == tile
            slot = lookup(CORNER_TABLE, corner, corner_turns[corner, source])
            cell = jnp.where(slot < 2, 0, 2 * S) + jnp.where((slot == 0) | (slot == 3), 0, S - 1)
            target = jnp.where((ii == corner) & hit, cell, target)
        hits[0, k, 4] = one_hot_rows(16, target, 4 * S)
        hits[1, k, 4] = jnp.zeros((16, 4 * S), BF)

    third.to_gather()
    first.to_back()
    second.to_back()
    third.to_back()

    for copy in swap_b.second:
        copy.wait_recv()
    columns[0, 1 : S + 1] = unpack(packed_other[6, 4]).astype(F32)
    columns[1, 1 : S + 1] = unpack(packed_other[7, 0]).astype(F32)
    ends = unpack(packed_other[7, 1]).astype(F32)
    for corner in range(4):
        at = 0 if corner < 2 else S + 1
        columns[(0, 1, 1, 0)[corner], at : at + 1] = ends[corner : corner + 1]

    def shift_partner(row, carry):
        x = unpack(packed_other[row // 5, lax.rem(row, 5)]).astype(F32)
        spread_columns(
            shifted, row, slice(0, C2), x, columns[0, pl.ds(row, 1)], columns[1, pl.ds(row, 1)]
        )
        return carry

    lax.fori_loop(0, S + 2, shift_partner, 0, unroll=2)
    first.to_pair()
    for copy in piece_copies:
        copy.wait_recv()

    flat = all_pieces[...].reshape(8 * 5 * 16, C)
    parts = [
        lax.dot_general(hits[i].reshape(8 * 5 * 16, 4 * S), flat, TN, preferred_element_type=F32)
        for i in range(2)
    ]
    low = jnp.concatenate([parts[0][:, :128], parts[0][:, 256:320]], axis=1)
    high = jnp.concatenate([parts[1][:, 128:256], parts[1][:, 320:]], axis=1)
    sums[...] = (low + high).reshape(4, S, C2)
    def add_sides(row, carry):
        io = iota2((S, C2), 0)
        x = interior[row + 1]
        x = x + jnp.where(io == 0, sums[3, pl.ds(row, 1)], 0.0)
        x = x + jnp.where(io == S - 1, sums[1, pl.ds(row, 1)], 0.0)
        x = x + jnp.where(row == 0, sums[0], 0.0)
        x = x + jnp.where(row == S - 1, sums[2], 0.0)
        grad_features[0, row] = x.astype(BF)
        return carry

    lax.fori_loop(0, S, add_sides, 0, unroll=2)

    def convolve_other(block, carry):
        total = partial_out[pl.ds(block * rows, rows)].reshape(rows * S, C2)
        for a in range(3):
            for b in range(3):
                window = shifted[b, pl.ds(block * rows + a, rows)].reshape(rows * S, C2)
                total = total + jnp.dot(window, out_weight[1, 3 * a + b], preferred_element_type=F32)
        output[0, pl.ds(block * rows, rows)] = total.reshape(rows, S, C2).astype(BF)
        return carry

    lax.fori_loop(0, 2, convolve_other, 0)
    second.to_pair()
    third.to_pair()
    for stream, spot in zip((first, second, third), lanes):
        stream.store(grad_weight, core, spot)
    for stream, spot in zip((first, second, third), lanes):
        stream.finish_pair()
        stream.store(grad_weight, 1 - core, spot)
    swap_a.finish_sends()
    swap_b.finish_sends()
    for copy in side_copies + piece_copies:
        copy.wait_send()
    for stream in (first, second, third):
        stream.finish()


VSPEC = pl.BlockSpec(memory_space=VM)
ANY = pl.BlockSpec(memory_space=pltpu.HBM)
DMA = pltpu.SemaphoreType.DMA
SM = pltpu.SMEM
REDUCE_BUFS = [
    ((2, 8 * CHUNK), F32),
    ((8, CHUNK), F32),
    ((7, CHUNK), BF),
    ((7, CHUNK), BF),
    ((7, UNIT), F32),
    ((7, UNIT), F32),
    ((2, 8, 7, UNIT), BF),
]
REDUCE_SEMS = [(2, 8), (2, 7), (2, 7), (2, 7), (2, 7), (2, 8)]


def reduce_scratch(width):
    return [VM(lead + (width,), kind) for lead, kind in REDUCE_BUFS] + [DMA(lead) for lead in REDUCE_SEMS]


def body(features, weight, cotangent, edge_tiles, edge_turns, corner_tiles, corner_turns):
    C2 = features.shape[3]
    C = 2 * C2
    shape = jax.ShapeDtypeStruct
    table = SM((4, 128), jnp.int32)
    output, grad_features, grad_weight = pl.pallas_call(
        lambda *refs: fused_kernel(1.0 / math.sqrt(128 * ROWS), *refs),
        name="fused",
        out_shape=(
            shape((1, S, S, C2), BF),
            shape((1, S, S, C2), BF),
            shape((9 * C2, C), F32),
        ),
        in_specs=[ANY] * 7,
        out_specs=(VSPEC,) * 3,
        scratch_shapes=[
            table, table, table, table,
            VM((S, S, C2), BF),
            VM((S, S, C2), BF),
            VM((9, C, C), BF),
            VM((9, C2, C), BF),
            VM((2, 9, C2, C2), BF),
            VM((2, S, C2), F32),
            VM((4, 16, C), BF),
            VM((8, 4, 16, C), BF),
            VM((8, 64, C), BF),
            VM((8, 64, C), BF),
            VM((2, 4, 64, C), BF),
            VM((3, S + 2, S, C2), BF),
            VM((2, 40, C2), F32),
            VM((3, S + 4, S, C), BF),
            VM((2, 48, C), F32),
            VM((S + 2, S, C2), F32),
            VM((5, 16, C), BF),
            VM((8, 5, 16, C), BF),
            VM((8, 5, 16, C), BF),
            VM((8, 5, 16, C), BF),
            VM((2, 4, 5, 16, C), BF),
            VM((3, S + 2, S, C2), BF),
            VM((S, S, C2), F32),
            VM((2, 8, 5, 16, 4 * S), BF),
            VM((4, S, C2), F32),
            VM((3 * C2, (S + 2) * S), BF),
            DMA((8,)),
            DMA((2, 8)),
            DMA((4, 8)),
            DMA((4, 8)),
            DMA((2, 8)),
        ]
        + reduce_scratch(128) * 3,
        compiler_params=pltpu.CompilerParams(
            vmem_limit_bytes=44 * 1024 * 1024, collective_id=0, has_side_effects=True
        ),
    )(
        *[pltpu.with_memory_space_constraint(x.T, pltpu.HBM) for x in (edge_tiles, edge_turns, corner_tiles, corner_turns)],
        *[pltpu.with_memory_space_constraint(x, pltpu.HBM) for x in (features[0], cotangent[0], weight.reshape(9, C, C))],
    )

    return (output, grad_features, grad_weight.reshape(3, 3, C2, C))


def solution(mesh):
    return jax.shard_map(
        body,
        mesh=mesh,
        in_specs=(
            P("tile", None, None, "ch"),
            P(),
            P("tile", None, None, "ch"),
            P(),
            P(),
            P(),
            P(),
        ),
        out_specs=(
            P("tile", None, None, "ch"),
            P("tile", None, None, "ch"),
            P(None, None, "ch", None),
        ),
        check_vma=False,
    )
```

```python
import math

import jax
import jax.numpy as jnp
import numpy as np
from jax import lax
from jax.experimental import pallas as pl
from jax.experimental.pallas import tpu as pltpu
from jax.sharding import PartitionSpec as P

MESH = pl.DeviceIdType.MESH
SPAN = 4
OFFSETS = [-4, -3, -2, -1, 1, 2, 3, 4]
S = 32
ROWS = S * S
UNIT = 16
VM = pltpu.VMEM
BF = jnp.bfloat16
F32 = jnp.float32


def turn_tables():
    labels = [[3 * row + col for col in range(3)] for row in range(3)]

    def turn_once(block):
        return [[block[col][2 - row] for col in range(3)] for row in range(3)]

    def sides_of(block):
        return [
            list(block[0]),
            [block[row][2] for row in range(3)],
            list(block[2]),
            [block[row][0] for row in range(3)],
        ]

    def corners_of(block):
        return [block[0][0], block[0][2], block[2][2], block[2][0]]

    base_sides = sides_of(labels)
    base_corners = corners_of(labels)
    edge_table = np.zeros((4, 4), np.int32)
    corner_table = np.zeros((4, 4), np.int32)
    for border in range(4):
        turned = labels
        for quarter in range(4):
            wanted = sides_of(turned)[(border + 2) % 4]
            for side_index in range(4):
                if base_sides[side_index] == wanted:
                    edge_table[border, quarter] = side_index
                if base_sides[side_index][::-1] == wanted:
                    edge_table[border, quarter] = side_index + 4
            corner_cell = corners_of(turned)[(border + 2) % 4]
            for corner_index in range(4):
                if base_corners[corner_index] == corner_cell:
                    corner_table[border, quarter] = corner_index
            turned = turn_once(turned)
    return (edge_table, corner_table)


EDGE_TABLE, CORNER_TABLE = turn_tables()


def lookup(table, border, turn):
    row = [int(v) for v in table[border]]
    value = jnp.int32(row[0])
    for quarter in range(1, 4):
        value = jnp.where(turn == quarter, jnp.int32(row[quarter]), value)
    return value


def slot_of(offset):
    return offset + SPAN if offset < 0 else offset + SPAN - 1


def wrap(index, size):
    return lax.rem(index + size, jnp.int32(size))


def coords():
    tile = lax.axis_index("tile")
    ch = lax.axis_index("ch")
    core = lax.rem(tile, 2)
    y = lax.rem(tile // 2, 4)
    xl = lax.rem(tile // 8, 2)
    z = tile // 16
    return tile, ch, core, y, xl, z


def dev(tile, ch):
    return {"tile": tile, "ch": ch}


def x_neighbours(tile, ch, xl):
    beside = tile + 8 - 16 * xl
    return dev(beside, ch), dev(beside, 1 - ch)


def remote(src, dst, send, recv, where):
    return pltpu.make_async_remote_copy(
        src_ref=src, dst_ref=dst, send_sem=send, recv_sem=recv, device_id=where, device_id_type=MESH
    )


class Swap:
    def __init__(self, src, dst, relay, sems, tile, ch, xl):
        self.n = relay.shape[1]
        near, far = x_neighbours(tile, ch, xl)
        self.first, self.second = [], []
        for i in range(self.n):
            for path in range(2):
                hop1, hop2 = (near, far) if path == 0 else (far, near)
                j = path * self.n + i
                self.first.append(remote(src.at[j], relay.at[path, i], sems.at[0, j], sems.at[1, j], hop1))
                self.second.append(remote(relay.at[path, i], dst.at[j], sems.at[2, j], sems.at[3, j], hop2))

    def start(self):
        for copy in self.first:
            copy.start()

    def relay(self):
        for one, two in zip(self.first, self.second):
            one.wait_recv()
            two.start()

    def finish_sends(self):
        for one, two in zip(self.first, self.second):
            one.wait_send()
            two.wait_send()


def near_copies(src, dst, sems, tile, ch, tiles):
    copies = []
    for offset in OFFSETS:
        k = slot_of(-offset)
        copies.append(
            remote(src, dst.at[k], sems.at[0, k], sems.at[1, k], dev(wrap(tile + offset, tiles), ch))
        )
    return copies


def iota2(shape, dim):
    return lax.broadcasted_iota(jnp.int32, shape, dim)


def source_slot(target, tile, tiles):
    away = wrap(target - tile, tiles)
    return jnp.clip(jnp.where(away > tiles // 2, away - tiles + SPAN, away + SPAN - 1), 0, 2 * SPAN - 1)


def spread_columns(buf, row, lanes, x, left, right):
    io = iota2(x.shape, 0)
    buf[1, row, :, lanes] = x.astype(BF)
    buf[0, row, :, lanes] = jnp.where(io == 0, left, pltpu.roll(x, 1, 0)).astype(BF)
    buf[2, row, :, lanes] = jnp.where(io == S - 1, right, pltpu.roll(x, S - 1, 0)).astype(BF)


def pack(x):
    n = x.shape[0] // 2
    return jnp.concatenate([x[:n, :128], x[n:, :128], x[:n, 128:], x[n:, 128:]], axis=1)


def unpack(x):
    low = jnp.concatenate([x[:, :128], x[:, 256:320]], axis=1)
    high = jnp.concatenate([x[:, 128:256], x[:, 320:]], axis=1)
    return jnp.concatenate([low, high], axis=0)


def one_hot_rows(rows, target, width):
    return jnp.where(iota2((rows, width), 1) == target, 1.0, 0.0).astype(BF)


TN = (((0,), (0,)), ((), ()))
NT = (((1,), (1,)), ((), ()))
CHUNK = 7 * UNIT


class Reduce:
    def __init__(self, scale, bufs, sems, place, z_first):
        self.grads, self.pair_in, self.sent, self.got, self.unit_out, self.unit_in, self.gathered = bufs
        self.scale = scale
        tile, ch, core, y, xl, z = place
        self.core = core
        self.pair = dev(tile + 1 - 2 * core, ch)
        across = (2 * y + xl, lambda g: dev(tile + 2 * (g // 2 - y) + 8 * (lax.rem(g, 2) - xl), ch))
        along = (z, lambda g: dev(tile + 16 * (g - z), ch))
        (spot, outer), (unit, inner) = (along, across) if z_first else (across, along)
        self.spot, self.unit = spot, unit
        self.order = [lax.rem(spot + 1 + j, 8) for j in range(7)] + [spot]
        self.unit_at = [lax.rem(unit + 1 + j, 8) for j in range(7)]
        self.unit_from = [lax.rem(unit + 7 - j, 8) for j in range(7)]
        self.outer_peers = [outer(g) for g in self.order[:7]]
        self.inner_peers = [inner(g) for g in self.unit_at]
        pair_sems, outer_sems, inner_sems, gather_sems, back_sems, last_sems = sems

        def copy(src, dst, pool, j, where):
            return remote(src, dst, pool.at[0, j], pool.at[1, j], where)

        def rows(half, g):
            return self.grads.at[half, pl.ds(pl.multiple_of(g * CHUNK, CHUNK), CHUNK)]

        self.own = jnp.minimum(unit, 6)
        mine = self.gathered.at[core, spot]
        cell = mine.at[self.own]
        seven = range(7)
        self.pair_copies = [
            copy(rows(1 - core, g), self.pair_in.at[j], pair_sems, j, self.pair)
            for j, g in enumerate(self.order)
        ]
        self.copies = [
            copy(self.sent.at[j], self.got.at[j], outer_sems, j, self.outer_peers[j]) for j in seven
        ]
        self.unit_copies = [
            copy(
                self.unit_out.at[jnp.minimum(self.unit_at[j], 6)], self.unit_in.at[j],
                inner_sems, j, self.inner_peers[j],
            )
            for j in seven
        ]
        self.gather = [copy(cell, cell, gather_sems, j, self.inner_peers[j]) for j in seven]
        self.back = [copy(mine, mine, back_sems, j, self.outer_peers[j]) for j in seven]
        self.last = []
        for j in range(8):
            block = self.gathered.at[core, spot if j == 0 else lax.rem(spot + 8 - j, 8)]
            self.last.append(copy(block, block, last_sems, j, self.pair))

    def own_rows(self, g):
        return self.grads[self.core, pl.ds(pl.multiple_of(g * CHUNK, CHUNK), CHUNK)]

    def start(self, step, begin):
        for g, copy in zip(self.order, self.pair_copies):
            early = g <= 4 if begin == 0 else g >= 3
            pl.when(early if step == 0 else jnp.logical_not(early))(copy.start)

    def to_outer(self):
        for j in range(7):
            self.pair_copies[j].wait_recv()
            self.sent[j] = (self.own_rows(self.order[j]) + self.pair_in[j]).astype(BF)
            self.copies[j].start()

    def to_inner(self):
        self.pair_copies[7].wait_recv()
        total = self.own_rows(self.spot) + self.pair_in[7]
        for j in range(7):
            self.copies[j].wait_recv()
            total = total + self.got[j].astype(F32)
        self.unit_out[...] = total.reshape(self.unit_out.shape)
        for j in range(7):
            pl.when(self.unit_at[j] != 7)(self.unit_copies[j].start)

    def to_gather(self):
        @pl.when(self.unit != 7)
        def _():
            total = self.unit_out[self.own]
            for j in range(7):
                self.unit_copies[j].wait_recv()
                total = total + self.unit_in[j]
            self.gathered[self.core, self.spot, self.own] = (total * self.scale).astype(BF)
            for copy in self.gather:
                copy.start()

    def to_back(self):
        for j in range(7):
            pl.when(self.unit_from[j] != 7)(self.gather[j].wait_recv)
        for copy in self.back:
            copy.start()
        self.last[0].start()

    def to_pair(self):
        for j in range(7):
            self.back[j].wait_recv()
            self.last[j + 1].start()

    def store(self, out, half, lanes):
        width = self.gathered.shape[4]
        filled = 9 * (out.shape[1] // 4)
        for g in range(8):
            rows = min(CHUNK, filled - g * CHUNK)
            block = self.gathered[half, g].astype(F32).reshape(CHUNK, width)
            out[pl.ds(pl.multiple_of(half * filled + g * CHUNK, 16), rows), lanes] = block[:rows]

    def finish_pair(self):
        for copy in self.last:
            copy.wait()

    def finish(self):
        for copy in self.pair_copies + self.copies + self.back:
            copy.wait_send()
        for j in range(7):
            pl.when(self.unit_at[j] != 7)(self.unit_copies[j].wait_send)
            pl.when(self.unit != 7)(self.gather[j].wait_send)


def fused_kernel(
    scale,
    edge_tiles_in, edge_turns_in, corner_tiles_in, corner_turns_in, feat_in, cot_in, weight_in,
    output, grad_features, grad_weight,
    edge_tiles, edge_turns, corner_tiles, corner_turns,
    feat, cot, weight, rows_weight, out_weight,
    lines, sides, all_sides, cot_packed, cot_other, relay_a,
    padded, columns, cots, cot_columns, interior, pieces, all_pieces,
    packed, packed_other, relay_b, shifted, partial_out, hits, sums, turned,
    load_sems, side_sems, swap_a_sems, swap_b_sems, piece_sems,
    *streams,
):
    tiles = 128
    place = tile, ch, core, y, xl, z = coords()
    C2 = feat.shape[2]
    C = 2 * C2
    near, far = x_neighbours(tile, ch, xl)
    bufs = len(REDUCE_BUFS)
    sems = len(REDUCE_SEMS)
    first, second, third = [
        Reduce(
            scale,
            streams[i * (bufs + sems) : i * (bufs + sems) + bufs],
            streams[i * (bufs + sems) + bufs : (i + 1) * (bufs + sems)],
            place,
            False,
        )
        for i in range(3)
    ]
    greeted = [dev(wrap(tile + o, tiles), ch) for o in OFFSETS] + [near, far, first.pair]
    greeted = greeted + first.outer_peers + first.inner_peers
    ready = pltpu.get_barrier_semaphore()
    for where in greeted:
        pl.semaphore_signal(ready, inc=1, device_id=where, device_id_type=MESH)

    own_rows = pl.ds(pl.multiple_of(ch * C2, 64), C2)
    loads = [
        pltpu.make_async_copy(a, b, load_sems.at[i])
        for i, (a, b) in enumerate(
            (
                (feat_in, feat),
                (cot_in, cot),
                (edge_tiles_in, edge_tiles),
                (edge_turns_in, edge_turns),
                (corner_tiles_in, corner_tiles),
                (corner_turns_in, corner_turns),
                (weight_in, weight),
                (weight_in.at[:, own_rows], rows_weight),
            )
        )
    ]
    for load in loads[:6]:
        load.start()

    loads[0].wait()

    def take_columns(row, carry):
        x = feat[row].astype(F32)
        lines[0, pl.ds(row, 1)] = x[0:1]
        lines[1, pl.ds(row, 1)] = x[S - 1 : S]
        return carry

    lax.fori_loop(0, S, take_columns, 0, unroll=4)
    sides[0] = pack(feat[0])
    sides[1] = pack(lines[1].astype(BF))
    sides[2] = pack(feat[S - 1])
    sides[3] = pack(lines[0].astype(BF))
    loads[1].wait()

    def pack_cot(row, carry):
        for i in range(4):
            cot_packed[row, 16 * i : 16 * i + 16] = pack(cot[4 * row + i])
        return carry

    lax.fori_loop(0, S // 4, pack_cot, 0)
    pl.semaphore_wait(ready, len(greeted))
    swap_a = Swap(cot_packed, cot_other, relay_a, swap_a_sems, tile, ch, xl)
    swap_a.start()
    side_copies = near_copies(sides, all_sides, side_sems, tile, ch, tiles)
    for copy in side_copies:
        copy.start()
    for load in loads[6:]:
        load.start()

    zero = jnp.zeros((S, C), BF)
    for part in range(3):
        for row in (0, 1, S + 2, S + 3):
            cots[part, row] = zero
    cot_columns[...] = jnp.zeros_like(cot_columns)
    nothing = jnp.zeros((1, C2), F32)

    def fill(read, lanes):
        def shift(row, carry):
            x = read(row).astype(F32)
            spread_columns(cots, row + 2, lanes, x, nothing, nothing)
            cot_columns[0, pl.ds(row + 2, 1), lanes] = x[0:1]
            cot_columns[1, pl.ds(row + 2, 1), lanes] = x[S - 1 : S]
            return carry

        lax.fori_loop(0, S, shift, 0, unroll=8)

    def read_other(row):
        at = pl.multiple_of(lax.rem(row, 4) * 16, 16)
        return unpack(cot_other[row // 4, pl.ds(at, 16)])

    pl.when(ch == 0)(lambda: fill(lambda row: cot[row], slice(0, C2)))
    pl.when(ch == 1)(lambda: fill(lambda row: cot[row], slice(C2, C)))
    swap_a.relay()

    for i in range(2, 6):
        loads[i].wait()
    for copy in side_copies:
        copy.wait_recv()
    halos = []
    for border in range(4):
        source = source_slot(edge_tiles[border, tile], tile, tiles)
        slot = lookup(EDGE_TABLE, border, edge_turns[border, tile])
        rev = slot // 4
        x = unpack(all_sides[source, slot - 4 * rev])
        ii = iota2((S, 1), 0)
        hot = one_hot_rows(S, jnp.where(rev == 1, S - 1 - ii, ii), S)
        halos.append(jnp.dot(hot, x, preferred_element_type=F32))
    columns[0, 1 : S + 1] = halos[3]
    columns[1, 1 : S + 1] = halos[1]
    for corner in range(4):
        source = source_slot(corner_tiles[corner, tile], tile, tiles)
        slot = lookup(CORNER_TABLE, corner, corner_turns[corner, tile])
        cells = unpack(all_sides[source, jnp.where(slot < 2, 0, 2)]).astype(F32)
        start = (slot == 0) | (slot == 3)
        at = 0 if corner < 2 else S + 1
        columns[(0, 1, 1, 0)[corner], at : at + 1] = jnp.where(start, cells[0:1], cells[S - 1 : S])
    padded[1, 0] = halos[0].astype(BF)
    padded[1, S + 1] = halos[2].astype(BF)
    padded[1, 1 : S + 1] = feat[...]

    def shift_features(row, carry):
        x = padded[1, row].astype(F32)
        spread_columns(
            padded, row, slice(0, C2), x, columns[0, pl.ds(row, 1)], columns[1, pl.ds(row, 1)]
        )
        return carry

    lax.fori_loop(0, S + 2, shift_features, 0, unroll=17)
    for b in range(3):
        turned[b * C2 : (b + 1) * C2] = padded[b].reshape((S + 2) * S, C2).T
    filled = 9 * (C2 // 2)

    def weight_grad(parts, lanes):
        width = 128 * len(parts)
        for stream in parts:
            stream.grads[:, filled:] = jnp.zeros((2, 8 * CHUNK - filled, 128), F32)

        def products(order):
            for step, a in enumerate(order):
                full = cots[1, 2 - a : 2 - a + S + 2, :, lanes].reshape((S + 2) * S, width)
                result = jnp.dot(turned[...], full, preferred_element_type=F32)
                for i, stream in enumerate(parts):
                    for half in range(2):
                        low = max(half * filled, 3 * a * C2)
                        high = min((half + 1) * filled, 3 * (a + 1) * C2)
                        if low < high:
                            stream.grads[half, low - half * filled : high - half * filled] = result[
                                low - 3 * a * C2 : high - 3 * a * C2, 128 * i : 128 * (i + 1)
                            ]
                    if step < 2:
                        stream.start(step, order[0])

        pl.when(core == 1)(lambda: products((0, 1, 2)))
        pl.when(core == 0)(lambda: products((2, 1, 0)))

    lanes = [pl.ds(pl.multiple_of(at, 128), 128) for at in (256 * ch, 128 - 128 * ch, 256 - 128 * ch)]
    weight_grad([first], lanes[0])
    for copy in swap_a.second:
        copy.wait_recv()

    def place_other(lanes):
        def one_row(row, carry):
            cots[1, row + 2, :, lanes] = read_other(row)
            return carry

        lax.fori_loop(0, S, one_row, 0, unroll=8)

    pl.when(ch == 0)(lambda: place_other(slice(C2, C)))
    pl.when(ch == 1)(lambda: place_other(slice(0, C2)))
    first.to_outer()
    weight_grad([second, third], pl.ds(pl.multiple_of(128 - 128 * ch, 128), 256))
    second.to_outer()
    third.to_outer()
    pl.when(ch == 0)(lambda: fill(read_other, slice(C2, C)))
    pl.when(ch == 1)(lambda: fill(read_other, slice(0, C2)))

    def pack_padded(row, carry):
        packed[row // 5, lax.rem(row, 5)] = pack(padded[1, row])
        return carry

    lax.fori_loop(0, S + 2, pack_padded, 0, unroll=2)
    packed[6, 4] = pack(columns[0, 1 : S + 1].astype(BF))
    packed[7, 0] = pack(columns[1, 1 : S + 1].astype(BF))
    io = iota2((16, C2), 0)
    ends = jnp.zeros((16, C2), F32)
    for corner in range(4):
        at = 0 if corner < 2 else S + 1
        ends = jnp.where(io == corner, columns[(0, 1, 1, 0)[corner], at : at + 1], ends)
    packed[7, 1] = pack(jnp.concatenate([ends, ends], axis=0).astype(BF))
    for i in range(2, 5):
        packed[7, i] = jnp.zeros((16, C), BF)
    swap_b = Swap(packed, packed_other, relay_b, swap_b_sems, tile, ch, xl)
    swap_b.start()

    first.to_inner()
    loads[7].wait()
    half = (S + 2) // 2

    def feature_grad(block, carry):
        total = None
        for a in range(3):
            for b in range(3):
                window = cots[2 - b, pl.ds(block * half + 2 - a, half)].reshape(half * S, C)
                term = lax.dot_general(window, rows_weight[3 * a + b], NT, preferred_element_type=F32)
                total = term if total is None else total + term
        interior[pl.ds(block * half, half)] = total.reshape(half, S, C2)
        return carry

    lax.fori_loop(0, 2, feature_grad, 0)
    pieces[0] = pack(interior[0].astype(BF))
    pieces[2] = pack(interior[S + 1].astype(BF))
    tips = []
    for side in range(2):
        total = None
        for a in range(3):
            line = cot_columns[side, 2 - a : 2 - a + 40].astype(BF)
            term = lax.dot_general(line, rows_weight[3 * a + 2 * side], NT, preferred_element_type=F32)
            total = term if total is None else total + term
        cot_columns[side, 0:40, 0:C2] = total
        pieces[3 - 2 * side] = pack(cot_columns[side, 1 : S + 1, 0:C2].astype(BF))
        tips.append((total[0:1], total[S + 1 : S + 2]))
    io = iota2((16, C2), 0)
    ends = jnp.zeros((16, C2), F32)
    for corner, value in enumerate((tips[0][0], tips[1][0], tips[1][1], tips[0][1])):
        ends = jnp.where(io == corner, value, ends)
    pieces[4] = pack(jnp.concatenate([ends, ends], axis=0).astype(BF))
    loads[6].wait()

    def pick_weight(tap, carry):
        for part in range(2):
            input_half = ch if part == 0 else 1 - ch
            w = weight[tap, pl.ds(pl.multiple_of(input_half * C2, 64), C2)].astype(F32)
            out_weight[part, tap] = jnp.where(ch == 0, w[:, :C2], w[:, C2:]).astype(BF)
        return carry

    lax.fori_loop(0, 9, pick_weight, 0)
    second.to_inner()
    third.to_inner()
    piece_copies = near_copies(pieces, all_pieces, piece_sems, tile, ch, tiles)
    for copy in piece_copies:
        copy.start()

    first.to_gather()

    rows = S // 2

    def convolve_own(block, carry):
        total = None
        for a in range(3):
            for b in range(3):
                window = padded[b, pl.ds(block * rows + a, rows)].reshape(rows * S, C2)
                term = jnp.dot(window, out_weight[0, 3 * a + b], preferred_element_type=F32)
                total = term if total is None else total + term
        partial_out[pl.ds(block * rows, rows)] = total.reshape(rows, S, C2)
        return carry

    lax.fori_loop(0, 2, convolve_own, 0)
    second.to_gather()
    third.to_gather()
    swap_b.relay()

    for offset in OFFSETS:
        k = slot_of(-offset)
        source = wrap(tile - offset, tiles)
        for border in range(4):
            hit = edge_tiles[border, source] == tile
            slot = lookup(EDGE_TABLE, border, edge_turns[border, source])
            rev = slot // 4
            ii = iota2((S, 1), 0)
            target = jnp.where(rev == 1, S - 1 - ii, ii) + (slot - 4 * rev) * S
            hot = one_hot_rows(S, jnp.where(hit, target, -1), 4 * S)
            hits[0, k, border] = hot[:16]
            hits[1, k, border] = hot[16:]
        ii = iota2((16, 1), 0)
        target = jnp.full((16, 1), -1, jnp.int32)
        for corner in range(4):
            hit = corner_tiles[corner, source] == tile
            slot = lookup(CORNER_TABLE, corner, corner_turns[corner, source])
            cell = jnp.where(slot < 2, 0, 2 * S) + jnp.where((slot == 0) | (slot == 3), 0, S - 1)
            target = jnp.where((ii == corner) & hit, cell, target)
        hits[0, k, 4] = one_hot_rows(16, target, 4 * S)
        hits[1, k, 4] = jnp.zeros((16, 4 * S), BF)

    first.to_back()
    second.to_back()
    third.to_back()

    for copy in swap_b.second:
        copy.wait_recv()
    columns[0, 1 : S + 1] = unpack(packed_other[6, 4]).astype(F32)
    columns[1, 1 : S + 1] = unpack(packed_other[7, 0]).astype(F32)
    ends = unpack(packed_other[7, 1]).astype(F32)
    for corner in range(4):
        at = 0 if corner < 2 else S + 1
        columns[(0, 1, 1, 0)[corner], at : at + 1] = ends[corner : corner + 1]

    def shift_partner(row, carry):
        x = unpack(packed_other[row // 5, lax.rem(row, 5)]).astype(F32)
        spread_columns(
            shifted, row, slice(0, C2), x, columns[0, pl.ds(row, 1)], columns[1, pl.ds(row, 1)]
        )
        return carry

    lax.fori_loop(0, S + 2, shift_partner, 0, unroll=2)
    first.to_pair()
    for copy in piece_copies:
        copy.wait_recv()

    flat = all_pieces[...].reshape(8 * 5 * 16, C)
    parts = [
        lax.dot_general(hits[i].reshape(8 * 5 * 16, 4 * S), flat, TN, preferred_element_type=F32)
        for i in range(2)
    ]
    low = jnp.concatenate([parts[0][:, :128], parts[0][:, 256:320]], axis=1)
    high = jnp.concatenate([parts[1][:, 128:256], parts[1][:, 320:]], axis=1)
    sums[...] = (low + high).reshape(4, S, C2)
    def add_sides(row, carry):
        io = iota2((S, C2), 0)
        x = interior[row + 1]
        x = x + jnp.where(io == 0, sums[3, pl.ds(row, 1)], 0.0)
        x = x + jnp.where(io == S - 1, sums[1, pl.ds(row, 1)], 0.0)
        x = x + jnp.where(row == 0, sums[0], 0.0)
        x = x + jnp.where(row == S - 1, sums[2], 0.0)
        grad_features[0, row] = x.astype(BF)
        return carry

    lax.fori_loop(0, S, add_sides, 0, unroll=2)

    def convolve_other(block, carry):
        total = partial_out[pl.ds(block * rows, rows)].reshape(rows * S, C2)
        for a in range(3):
            for b in range(3):
                window = shifted[b, pl.ds(block * rows + a, rows)].reshape(rows * S, C2)
                total = total + jnp.dot(window, out_weight[1, 3 * a + b], preferred_element_type=F32)
        output[0, pl.ds(block * rows, rows)] = total.reshape(rows, S, C2).astype(BF)
        return carry

    lax.fori_loop(0, 2, convolve_other, 0)
    second.to_pair()
    third.to_pair()
    for stream, spot in zip((first, second, third), lanes):
        stream.store(grad_weight, core, spot)
    for stream, spot in zip((first, second, third), lanes):
        stream.finish_pair()
        stream.store(grad_weight, 1 - core, spot)
    swap_a.finish_sends()
    swap_b.finish_sends()
    for copy in side_copies + piece_copies:
        copy.wait_send()
    for stream in (first, second, third):
        stream.finish()


def publish_kernel(a, b, c, a_out, b_out, c_out, sems):
    copies = [
        pltpu.make_async_copy(src, dst, sems.at[i])
        for i, (src, dst) in enumerate(((c, c_out), (a, a_out), (b, b_out)))
    ]
    for copy in copies:
        copy.start()
    for copy in copies:
        copy.wait()


VSPEC = pl.BlockSpec(memory_space=VM)
ANY = pl.BlockSpec(memory_space=pltpu.HBM)
DMA = pltpu.SemaphoreType.DMA
SM = pltpu.SMEM
REDUCE_BUFS = [
    ((2, 8 * CHUNK), F32),
    ((8, CHUNK), F32),
    ((7, CHUNK), BF),
    ((7, CHUNK), BF),
    ((7, UNIT), F32),
    ((7, UNIT), F32),
    ((2, 8, 7, UNIT), BF),
]
REDUCE_SEMS = [(2, 8), (2, 7), (2, 7), (2, 7), (2, 7), (2, 8)]


def reduce_scratch(width):
    return [VM(lead + (width,), kind) for lead, kind in REDUCE_BUFS] + [DMA(lead) for lead in REDUCE_SEMS]


def body(features, weight, cotangent, edge_tiles, edge_turns, corner_tiles, corner_turns):
    C2 = features.shape[3]
    C = 2 * C2
    shape = jax.ShapeDtypeStruct
    table = SM((4, 128), jnp.int32)
    output, grad_features, grad_weight = pl.pallas_call(
        lambda *refs: fused_kernel(1.0 / math.sqrt(128 * ROWS), *refs),
        name="fused",
        out_shape=(
            shape((1, S, S, C2), BF),
            shape((1, S, S, C2), BF),
            shape((9 * C2, C), F32),
        ),
        in_specs=[ANY] * 7,
        out_specs=(VSPEC,) * 3,
        scratch_shapes=[
            table, table, table, table,
            VM((S, S, C2), BF),
            VM((S, S, C2), BF),
            VM((9, C, C), BF),
            VM((9, C2, C), BF),
            VM((2, 9, C2, C2), BF),
            VM((2, S, C2), F32),
            VM((4, 16, C), BF),
            VM((8, 4, 16, C), BF),
            VM((8, 64, C), BF),
            VM((8, 64, C), BF),
            VM((2, 4, 64, C), BF),
            VM((3, S + 2, S, C2), BF),
            VM((2, 40, C2), F32),
            VM((3, S + 4, S, C), BF),
            VM((2, 48, C), F32),
            VM((S + 2, S, C2), F32),
            VM((5, 16, C), BF),
            VM((8, 5, 16, C), BF),
            VM((8, 5, 16, C), BF),
            VM((8, 5, 16, C), BF),
            VM((2, 4, 5, 16, C), BF),
            VM((3, S + 2, S, C2), BF),
            VM((S, S, C2), F32),
            VM((2, 8, 5, 16, 4 * S), BF),
            VM((4, S, C2), F32),
            VM((3 * C2, (S + 2) * S), BF),
            DMA((8,)),
            DMA((2, 8)),
            DMA((4, 8)),
            DMA((4, 8)),
            DMA((2, 8)),
        ]
        + reduce_scratch(128) * 3,
        compiler_params=pltpu.CompilerParams(
            vmem_limit_bytes=44 * 1024 * 1024, collective_id=0, has_side_effects=True
        ),
    )(
        *[pltpu.with_memory_space_constraint(x.T, pltpu.HBM) for x in (edge_tiles, edge_turns, corner_tiles, corner_turns)],
        *[pltpu.with_memory_space_constraint(x, pltpu.HBM) for x in (features[0], cotangent[0], weight.reshape(9, C, C))],
    )

    output, grad_features, grad_weight = pl.pallas_call(
        publish_kernel,
        name="publish",
        out_shape=(shape((1, S, S, C2), BF), shape((1, S, S, C2), BF), shape((9 * C2, C), F32)),
        in_specs=[pl.BlockSpec(memory_space=pl.ANY)] * 3,
        out_specs=(ANY,) * 3,
        scratch_shapes=[DMA((3,))],
        compiler_params=pltpu.CompilerParams(vmem_limit_bytes=1024 * 1024),
    )(output, grad_features, grad_weight)
    return (output, grad_features, grad_weight.reshape(3, 3, C2, C))


def solution(mesh):
    return jax.shard_map(
        body,
        mesh=mesh,
        in_specs=(
            P("tile", None, None, "ch"),
            P(),
            P("tile", None, None, "ch"),
            P(),
            P(),
            P(),
            P(),
        ),
        out_specs=(
            P("tile", None, None, "ch"),
            P("tile", None, None, "ch"),
            P(None, None, "ch", None),
        ),
        check_vma=False,
    )
```

```python
import math

import jax
import jax.numpy as jnp
import numpy as np
from jax import lax
from jax.experimental import pallas as pl
from jax.experimental.pallas import tpu as pltpu
from jax.sharding import PartitionSpec as P

MESH = pl.DeviceIdType.MESH
SPAN = 4
OFFSETS = [-4, -3, -2, -1, 1, 2, 3, 4]
S = 32
ROWS = S * S
UNIT = 16
VM = pltpu.VMEM
BF = jnp.bfloat16
F32 = jnp.float32


def turn_tables():
    labels = [[3 * row + col for col in range(3)] for row in range(3)]

    def turn_once(block):
        return [[block[col][2 - row] for col in range(3)] for row in range(3)]

    def sides_of(block):
        return [
            list(block[0]),
            [block[row][2] for row in range(3)],
            list(block[2]),
            [block[row][0] for row in range(3)],
        ]

    def corners_of(block):
        return [block[0][0], block[0][2], block[2][2], block[2][0]]

    base_sides = sides_of(labels)
    base_corners = corners_of(labels)
    edge_table = np.zeros((4, 4), np.int32)
    corner_table = np.zeros((4, 4), np.int32)
    for border in range(4):
        turned = labels
        for quarter in range(4):
            wanted = sides_of(turned)[(border + 2) % 4]
            for side_index in range(4):
                if base_sides[side_index] == wanted:
                    edge_table[border, quarter] = side_index
                if base_sides[side_index][::-1] == wanted:
                    edge_table[border, quarter] = side_index + 4
            corner_cell = corners_of(turned)[(border + 2) % 4]
            for corner_index in range(4):
                if base_corners[corner_index] == corner_cell:
                    corner_table[border, quarter] = corner_index
            turned = turn_once(turned)
    return (edge_table, corner_table)


EDGE_TABLE, CORNER_TABLE = turn_tables()


def lookup(table, border, turn):
    row = [int(v) for v in table[border]]
    value = jnp.int32(row[0])
    for quarter in range(1, 4):
        value = jnp.where(turn == quarter, jnp.int32(row[quarter]), value)
    return value


def slot_of(offset):
    return offset + SPAN if offset < 0 else offset + SPAN - 1


def wrap(index, size):
    return lax.rem(index + size, jnp.int32(size))


def coords():
    tile = lax.axis_index("tile")
    ch = lax.axis_index("ch")
    core = lax.rem(tile, 2)
    y = lax.rem(tile // 2, 4)
    xl = lax.rem(tile // 8, 2)
    z = tile // 16
    return tile, ch, core, y, xl, z


def dev(tile, ch):
    return {"tile": tile, "ch": ch}


def x_neighbours(tile, ch, xl):
    beside = tile + 8 - 16 * xl
    return dev(beside, ch), dev(beside, 1 - ch)


def remote(src, dst, send, recv, where):
    return pltpu.make_async_remote_copy(
        src_ref=src, dst_ref=dst, send_sem=send, recv_sem=recv, device_id=where, device_id_type=MESH
    )


class Swap:
    def __init__(self, src, dst, relay, sems, tile, ch, xl):
        self.n = relay.shape[1]
        near, far = x_neighbours(tile, ch, xl)
        self.first, self.second = [], []
        for i in range(self.n):
            for path in range(2):
                hop1, hop2 = (near, far) if path == 0 else (far, near)
                j = path * self.n + i
                self.first.append(remote(src.at[j], relay.at[path, i], sems.at[0, j], sems.at[1, j], hop1))
                self.second.append(remote(relay.at[path, i], dst.at[j], sems.at[2, j], sems.at[3, j], hop2))

    def start(self):
        for copy in self.first:
            copy.start()

    def relay(self, start=0, stop=None):
        for one, two in zip(self.first[start:stop], self.second[start:stop]):
            one.wait_recv()
            two.start()

    def finish_sends(self):
        for one, two in zip(self.first, self.second):
            one.wait_send()
            two.wait_send()


def near_copies(src, dst, sems, tile, ch, tiles):
    copies = []
    for offset in OFFSETS:
        k = slot_of(-offset)
        copies.append(
            remote(src, dst.at[k], sems.at[0, k], sems.at[1, k], dev(wrap(tile + offset, tiles), ch))
        )
    return copies


def iota2(shape, dim):
    return lax.broadcasted_iota(jnp.int32, shape, dim)


def source_slot(target, tile, tiles):
    away = wrap(target - tile, tiles)
    return jnp.clip(jnp.where(away > tiles // 2, away - tiles + SPAN, away + SPAN - 1), 0, 2 * SPAN - 1)


def spread_columns(buf, row, lanes, x, left, right):
    io = iota2(x.shape, 0)
    buf[1, row, :, lanes] = x.astype(BF)
    buf[0, row, :, lanes] = jnp.where(io == 0, left, pltpu.roll(x, 1, 0)).astype(BF)
    buf[2, row, :, lanes] = jnp.where(io == S - 1, right, pltpu.roll(x, S - 1, 0)).astype(BF)


def pack(x):
    n = x.shape[0] // 2
    return jnp.concatenate([x[:n, :128], x[n:, :128], x[:n, 128:], x[n:, 128:]], axis=1)


def unpack(x):
    low = jnp.concatenate([x[:, :128], x[:, 256:320]], axis=1)
    high = jnp.concatenate([x[:, 128:256], x[:, 320:]], axis=1)
    return jnp.concatenate([low, high], axis=0)


def one_hot_rows(rows, target, width):
    return jnp.where(iota2((rows, width), 1) == target, 1.0, 0.0).astype(BF)


TN = (((0,), (0,)), ((), ()))
NT = (((1,), (1,)), ((), ()))
CHUNK = 7 * UNIT


class Reduce:
    def __init__(self, scale, bufs, sems, place):
        self.grads, self.pair_in, self.sent, self.got, self.unit_out, self.unit_in, self.gathered = bufs
        self.scale = scale
        tile, ch, core, y, xl, z = place
        self.core = core
        self.pair = dev(tile + 1 - 2 * core, ch)
        across = (2 * y + xl, lambda g: dev(tile + 2 * (g // 2 - y) + 8 * (lax.rem(g, 2) - xl), ch))
        along = (z, lambda g: dev(tile + 16 * (g - z), ch))
        (spot, outer), (unit, inner) = across, along
        self.spot, self.unit = spot, unit
        self.order = [lax.rem(spot + 1 + j, 8) for j in range(7)] + [spot]
        self.unit_at = [lax.rem(unit + 1 + j, 8) for j in range(7)]
        self.unit_from = [lax.rem(unit + 7 - j, 8) for j in range(7)]
        self.outer_peers = [outer(g) for g in self.order[:7]]
        self.inner_peers = [inner(g) for g in self.unit_at]
        pair_sems, outer_sems, inner_sems, gather_sems, back_sems, last_sems = sems

        def copy(src, dst, pool, j, where):
            return remote(src, dst, pool.at[0, j], pool.at[1, j], where)

        def rows(half, g):
            return self.grads.at[half, pl.ds(pl.multiple_of(g * CHUNK, CHUNK), CHUNK)]

        self.own = jnp.minimum(unit, 6)
        mine = self.gathered.at[core, spot]
        cell = mine.at[self.own]
        seven = range(7)
        self.pair_copies = [
            copy(rows(1 - core, g), self.pair_in.at[j], pair_sems, j, self.pair)
            for j, g in enumerate(self.order)
        ]
        self.copies = [
            copy(self.sent.at[j], self.got.at[j], outer_sems, j, self.outer_peers[j]) for j in seven
        ]
        self.unit_copies = [
            copy(
                self.unit_out.at[jnp.minimum(self.unit_at[j], 6)], self.unit_in.at[j],
                inner_sems, j, self.inner_peers[j],
            )
            for j in seven
        ]
        self.gather = [copy(cell, cell, gather_sems, j, self.inner_peers[j]) for j in seven]
        near, _ = x_neighbours(tile, ch, xl)
        column = [dev(tile + 2 * (lax.rem(y + 1 + j, 4) - y), ch) for j in range(3)]
        beside = self.gathered.at[core, 2 * y + 1 - xl]
        self.back = [copy(mine, mine, back_sems, 0, near)]
        self.back += [copy(mine, mine, back_sems, 1 + j, column[j]) for j in range(3)]
        self.back += [copy(beside, beside, back_sems, 4 + j, column[j]) for j in range(3)]
        got = [2 * y + 1 - xl]
        for other in (xl, 1 - xl):
            got += [2 * lax.rem(y + 3 - j, 4) + other for j in range(3)]
        self.last = []
        for j, g in enumerate([spot] + got):
            block = self.gathered.at[core, g]
            self.last.append(copy(block, block, last_sems, j, self.pair))

    def own_rows(self, g):
        return self.grads[self.core, pl.ds(pl.multiple_of(g * CHUNK, CHUNK), CHUNK)]

    def start(self, step, begin):
        for g, copy in zip(self.order, self.pair_copies):
            early = g <= 4 if begin == 0 else g >= 3
            pl.when(early if step == 0 else jnp.logical_not(early))(copy.start)

    def to_outer(self):
        for j in range(7):
            self.pair_copies[j].wait_recv()
            self.sent[j] = (self.own_rows(self.order[j]) + self.pair_in[j]).astype(BF)
            self.copies[j].start()

    def to_inner(self):
        self.pair_copies[7].wait_recv()
        total = self.own_rows(self.spot) + self.pair_in[7]
        for j in range(7):
            self.copies[j].wait_recv()
            total = total + self.got[j].astype(F32)
        self.unit_out[...] = total.reshape(self.unit_out.shape)
        for j in range(7):
            pl.when(self.unit_at[j] != 7)(self.unit_copies[j].start)

    def to_gather(self):
        @pl.when(self.unit != 7)
        def _():
            total = self.unit_out[self.own]
            for j in range(7):
                self.unit_copies[j].wait_recv()
                total = total + self.unit_in[j]
            self.gathered[self.core, self.spot, self.own] = (total * self.scale).astype(BF)
            for copy in self.gather:
                copy.start()

    def to_back(self):
        for j in range(7):
            pl.when(self.unit_from[j] != 7)(self.gather[j].wait_recv)
        for copy in self.back[:4]:
            copy.start()
        self.last[0].start()

    def pass_back(self):
        self.back[0].wait_recv()
        for copy in self.back[4:]:
            copy.start()
        self.last[1].start()

    def to_pair(self):
        for j in range(1, 7):
            self.back[j].wait_recv()
            self.last[j + 1].start()

    def store(self, out, half, lanes):
        width = self.gathered.shape[4]
        filled = 9 * (out.shape[1] // 4)
        for g in range(8):
            rows = min(CHUNK, filled - g * CHUNK)
            block = self.gathered[half, g].astype(F32).reshape(CHUNK, width)
            out[pl.ds(pl.multiple_of(half * filled + g * CHUNK, 16), rows), lanes] = block[:rows]

    def finish_pair(self):
        for copy in self.last:
            copy.wait()

    def finish(self):
        for copy in self.pair_copies + self.copies + self.back:
            copy.wait_send()
        for j in range(7):
            pl.when(self.unit_at[j] != 7)(self.unit_copies[j].wait_send)
            pl.when(self.unit != 7)(self.gather[j].wait_send)


def fused_kernel(
    scale,
    edge_tiles_in, edge_turns_in, corner_tiles_in, corner_turns_in, feat_in, cot_in, weight_in,
    output, grad_features, grad_weight,
    edge_tiles, edge_turns, corner_tiles, corner_turns,
    feat, cot, weight, rows_weight, out_weight,
    lines, sides, all_sides, cot_packed, cot_other, relay_a,
    padded, columns, cots, cot_columns, interior, pieces, all_pieces,
    packed, packed_other, relay_b, shifted, partial_out, hits, sums, turned,
    load_sems, side_sems, swap_a_sems, swap_b_sems, piece_sems,
    *streams,
):
    tiles = 128
    place = tile, ch, core, y, xl, z = coords()
    C2 = feat.shape[2]
    C = 2 * C2
    near, far = x_neighbours(tile, ch, xl)
    bufs = len(REDUCE_BUFS)
    sems = len(REDUCE_SEMS)
    first, second, third = [
        Reduce(
            scale,
            streams[i * (bufs + sems) : i * (bufs + sems) + bufs],
            streams[i * (bufs + sems) + bufs : (i + 1) * (bufs + sems)],
            place,
        )
        for i in range(3)
    ]
    greeted = [dev(wrap(tile + o, tiles), ch) for o in OFFSETS] + [near, far, first.pair]
    greeted = greeted + first.outer_peers + first.inner_peers
    ready = pltpu.get_barrier_semaphore()
    for where in greeted:
        pl.semaphore_signal(ready, inc=1, device_id=where, device_id_type=MESH)

    own_rows = pl.ds(pl.multiple_of(ch * C2, 64), C2)
    loads = [
        pltpu.make_async_copy(a, b, load_sems.at[i])
        for i, (a, b) in enumerate(
            (
                (feat_in, feat),
                (cot_in, cot),
                (edge_tiles_in, edge_tiles),
                (edge_turns_in, edge_turns),
                (corner_tiles_in, corner_tiles),
                (corner_turns_in, corner_turns),
                (weight_in, weight),
                (weight_in.at[:, own_rows], rows_weight),
            )
        )
    ]
    for load in loads[:6]:
        load.start()

    loads[0].wait()

    def take_columns(row, carry):
        x = feat[row].astype(F32)
        lines[0, pl.ds(row, 1)] = x[0:1]
        lines[1, pl.ds(row, 1)] = x[S - 1 : S]
        return carry

    lax.fori_loop(0, S, take_columns, 0, unroll=4)
    sides[0] = pack(feat[0])
    sides[1] = pack(lines[1].astype(BF))
    sides[2] = pack(feat[S - 1])
    sides[3] = pack(lines[0].astype(BF))
    loads[1].wait()

    def pack_cot(row, carry):
        for i in range(4):
            cot_packed[row, 16 * i : 16 * i + 16] = pack(cot[4 * row + i])
        return carry

    lax.fori_loop(0, S // 4, pack_cot, 0)
    pl.semaphore_wait(ready, len(greeted))
    swap_a = Swap(cot_packed, cot_other, relay_a, swap_a_sems, tile, ch, xl)
    swap_a.start()
    side_copies = near_copies(sides, all_sides, side_sems, tile, ch, tiles)
    for copy in side_copies:
        copy.start()
    for load in loads[6:]:
        load.start()

    zero = jnp.zeros((S, C), BF)
    for part in range(3):
        for row in (0, 1, S + 2, S + 3):
            cots[part, row] = zero
    cot_columns[...] = jnp.zeros_like(cot_columns)
    nothing = jnp.zeros((1, C2), F32)

    def fill(read, lanes):
        def shift(row, carry):
            x = read(row).astype(F32)
            spread_columns(cots, row + 2, lanes, x, nothing, nothing)
            cot_columns[0, pl.ds(row + 2, 1), lanes] = x[0:1]
            cot_columns[1, pl.ds(row + 2, 1), lanes] = x[S - 1 : S]
            return carry

        lax.fori_loop(0, S, shift, 0, unroll=8)

    def read_other(row):
        at = pl.multiple_of(lax.rem(row, 4) * 16, 16)
        return unpack(cot_other[row // 4, pl.ds(at, 16)])

    pl.when(ch == 0)(lambda: fill(lambda row: cot[row], slice(0, C2)))
    pl.when(ch == 1)(lambda: fill(lambda row: cot[row], slice(C2, C)))
    swap_a.relay()

    for i in range(2, 6):
        loads[i].wait()
    for copy in side_copies:
        copy.wait_recv()
    halos = []
    for border in range(4):
        source = source_slot(edge_tiles[border, tile], tile, tiles)
        slot = lookup(EDGE_TABLE, border, edge_turns[border, tile])
        rev = slot // 4
        x = unpack(all_sides[source, slot - 4 * rev])
        ii = iota2((S, 1), 0)
        hot = one_hot_rows(S, jnp.where(rev == 1, S - 1 - ii, ii), S)
        halos.append(jnp.dot(hot, x, preferred_element_type=F32))
    columns[0, 1 : S + 1] = halos[3]
    columns[1, 1 : S + 1] = halos[1]
    for corner in range(4):
        source = source_slot(corner_tiles[corner, tile], tile, tiles)
        slot = lookup(CORNER_TABLE, corner, corner_turns[corner, tile])
        cells = unpack(all_sides[source, jnp.where(slot < 2, 0, 2)]).astype(F32)
        start = (slot == 0) | (slot == 3)
        at = 0 if corner < 2 else S + 1
        columns[(0, 1, 1, 0)[corner], at : at + 1] = jnp.where(start, cells[0:1], cells[S - 1 : S])
    padded[1, 0] = halos[0].astype(BF)
    padded[1, S + 1] = halos[2].astype(BF)
    padded[1, 1 : S + 1] = feat[...]

    def shift_features(row, carry):
        x = padded[1, row].astype(F32)
        spread_columns(
            padded, row, slice(0, C2), x, columns[0, pl.ds(row, 1)], columns[1, pl.ds(row, 1)]
        )
        return carry

    lax.fori_loop(0, S + 2, shift_features, 0, unroll=17)
    for b in range(3):
        turned[b * C2 : (b + 1) * C2] = padded[b].reshape((S + 2) * S, C2).T
    filled = 9 * (C2 // 2)

    def weight_grad(parts, lanes):
        width = 128 * len(parts)
        for stream in parts:
            stream.grads[:, filled:] = jnp.zeros((2, 8 * CHUNK - filled, 128), F32)

        def products(order):
            for step, a in enumerate(order):
                full = cots[1, 2 - a : 2 - a + S + 2, :, lanes].reshape((S + 2) * S, width)
                result = jnp.dot(turned[...], full, preferred_element_type=F32)
                for i, stream in enumerate(parts):
                    for half in range(2):
                        low = max(half * filled, 3 * a * C2)
                        high = min((half + 1) * filled, 3 * (a + 1) * C2)
                        if low < high:
                            stream.grads[half, low - half * filled : high - half * filled] = result[
                                low - 3 * a * C2 : high - 3 * a * C2, 128 * i : 128 * (i + 1)
                            ]
                    if step < 2:
                        stream.start(step, order[0])

        pl.when(core == 1)(lambda: products((0, 1, 2)))
        pl.when(core == 0)(lambda: products((2, 1, 0)))

    lanes = [pl.ds(pl.multiple_of(at, 128), 128) for at in (256 * ch, 128 - 128 * ch, 256 - 128 * ch)]
    weight_grad([first], lanes[0])
    for copy in swap_a.second:
        copy.wait_recv()

    def place_other(lanes):
        def one_row(row, carry):
            cots[1, row + 2, :, lanes] = read_other(row)
            return carry

        lax.fori_loop(0, S, one_row, 0, unroll=8)

    pl.when(ch == 0)(lambda: place_other(slice(C2, C)))
    pl.when(ch == 1)(lambda: place_other(slice(0, C2)))
    first.to_outer()
    weight_grad([second, third], pl.ds(pl.multiple_of(128 - 128 * ch, 128), 256))
    second.to_outer()
    third.to_outer()

    def pack_padded(row, carry):
        packed[row // 5, lax.rem(row, 5)] = pack(padded[1, row])
        return carry

    lax.fori_loop(0, S + 2, pack_padded, 0, unroll=2)
    packed[6, 4] = pack(columns[0, 1 : S + 1].astype(BF))
    packed[7, 0] = pack(columns[1, 1 : S + 1].astype(BF))
    io = iota2((16, C2), 0)
    ends = jnp.zeros((16, C2), F32)
    for corner in range(4):
        at = 0 if corner < 2 else S + 1
        ends = jnp.where(io == corner, columns[(0, 1, 1, 0)[corner], at : at + 1], ends)
    packed[7, 1] = pack(jnp.concatenate([ends, ends], axis=0).astype(BF))
    for i in range(2, 5):
        packed[7, i] = jnp.zeros((16, C), BF)
    swap_b = Swap(packed, packed_other, relay_b, swap_b_sems, tile, ch, xl)
    swap_b.start()

    pl.when(ch == 0)(lambda: fill(read_other, slice(C2, C)))
    pl.when(ch == 1)(lambda: fill(read_other, slice(0, C2)))

    first.to_inner()
    loads[7].wait()
    half = (S + 2) // 2

    def feature_grad(block, carry):
        total = None
        for a in range(3):
            for b in range(3):
                window = cots[2 - b, pl.ds(block * half + 2 - a, half)].reshape(half * S, C)
                term = lax.dot_general(window, rows_weight[3 * a + b], NT, preferred_element_type=F32)
                total = term if total is None else total + term
        interior[pl.ds(block * half, half)] = total.reshape(half, S, C2)
        return carry

    lax.fori_loop(0, 2, feature_grad, 0)
    pieces[0] = pack(interior[0].astype(BF))
    pieces[2] = pack(interior[S + 1].astype(BF))
    tips = []
    for side in range(2):
        total = None
        for a in range(3):
            line = cot_columns[side, 2 - a : 2 - a + 40].astype(BF)
            term = lax.dot_general(line, rows_weight[3 * a + 2 * side], NT, preferred_element_type=F32)
            total = term if total is None else total + term
        cot_columns[side, 0:40, 0:C2] = total
        pieces[3 - 2 * side] = pack(cot_columns[side, 1 : S + 1, 0:C2].astype(BF))
        tips.append((total[0:1], total[S + 1 : S + 2]))
    io = iota2((16, C2), 0)
    ends = jnp.zeros((16, C2), F32)
    for corner, value in enumerate((tips[0][0], tips[1][0], tips[1][1], tips[0][1])):
        ends = jnp.where(io == corner, value, ends)
    pieces[4] = pack(jnp.concatenate([ends, ends], axis=0).astype(BF))
    loads[6].wait()

    def pick_weight(tap, carry):
        for part in range(2):
            input_half = ch if part == 0 else 1 - ch
            w = weight[tap, pl.ds(pl.multiple_of(input_half * C2, 64), C2)].astype(F32)
            out_weight[part, tap] = jnp.where(ch == 0, w[:, :C2], w[:, C2:]).astype(BF)
        return carry

    lax.fori_loop(0, 9, pick_weight, 0)
    second.to_inner()
    third.to_inner()
    piece_copies = near_copies(pieces, all_pieces, piece_sems, tile, ch, tiles)
    for copy in piece_copies:
        copy.start()

    first.to_gather()

    rows = S // 2

    def convolve_own(block, carry):
        total = None
        for a in range(3):
            for b in range(3):
                window = padded[b, pl.ds(block * rows + a, rows)].reshape(rows * S, C2)
                term = jnp.dot(window, out_weight[0, 3 * a + b], preferred_element_type=F32)
                total = term if total is None else total + term
        partial_out[pl.ds(block * rows, rows)] = total.reshape(rows, S, C2)
        return carry

    lax.fori_loop(0, 2, convolve_own, 0)
    swap_b.relay(0, 4)
    second.to_gather()
    swap_b.relay(4)
    third.to_gather()

    for offset in OFFSETS:
        k = slot_of(-offset)
        source = wrap(tile - offset, tiles)
        for border in range(4):
            hit = edge_tiles[border, source] == tile
            slot = lookup(EDGE_TABLE, border, edge_turns[border, source])
            rev = slot // 4
            ii = iota2((S, 1), 0)
            target = jnp.where(rev == 1, S - 1 - ii, ii) + (slot - 4 * rev) * S
            hot = one_hot_rows(S, jnp.where(hit, target, -1), 4 * S)
            hits[0, k, border] = hot[:16]
            hits[1, k, border] = hot[16:]
        ii = iota2((16, 1), 0)
        target = jnp.full((16, 1), -1, jnp.int32)
        for corner in range(4):
            hit = corner_tiles[corner, source] == tile
            slot = lookup(CORNER_TABLE, corner, corner_turns[corner, source])
            cell = jnp.where(slot < 2, 0, 2 * S) + jnp.where((slot == 0) | (slot == 3), 0, S - 1)
            target = jnp.where((ii == corner) & hit, cell, target)
        hits[0, k, 4] = one_hot_rows(16, target, 4 * S)
        hits[1, k, 4] = jnp.zeros((16, 4 * S), BF)

    first.to_back()
    second.to_back()
    third.to_back()
    first.pass_back()
    second.pass_back()
    third.pass_back()

    for copy in swap_b.second:
        copy.wait_recv()
    columns[0, 1 : S + 1] = unpack(packed_other[6, 4]).astype(F32)
    columns[1, 1 : S + 1] = unpack(packed_other[7, 0]).astype(F32)
    ends = unpack(packed_other[7, 1]).astype(F32)
    for corner in range(4):
        at = 0 if corner < 2 else S + 1
        columns[(0, 1, 1, 0)[corner], at : at + 1] = ends[corner : corner + 1]

    def shift_partner(row, carry):
        x = unpack(packed_other[row // 5, lax.rem(row, 5)]).astype(F32)
        spread_columns(
            shifted, row, slice(0, C2), x, columns[0, pl.ds(row, 1)], columns[1, pl.ds(row, 1)]
        )
        return carry

    lax.fori_loop(0, S + 2, shift_partner, 0, unroll=2)
    for copy in piece_copies:
        copy.wait_recv()

    flat = all_pieces[...].reshape(8 * 5 * 16, C)
    parts = [
        lax.dot_general(hits[i].reshape(8 * 5 * 16, 4 * S), flat, TN, preferred_element_type=F32)
        for i in range(2)
    ]
    low = jnp.concatenate([parts[0][:, :128], parts[0][:, 256:320]], axis=1)
    high = jnp.concatenate([parts[1][:, 128:256], parts[1][:, 320:]], axis=1)
    sums[...] = (low + high).reshape(4, S, C2)
    def add_sides(row, carry):
        io = iota2((S, C2), 0)
        x = interior[row + 1]
        x = x + jnp.where(io == 0, sums[3, pl.ds(row, 1)], 0.0)
        x = x + jnp.where(io == S - 1, sums[1, pl.ds(row, 1)], 0.0)
        x = x + jnp.where(row == 0, sums[0], 0.0)
        x = x + jnp.where(row == S - 1, sums[2], 0.0)
        grad_features[0, row] = x.astype(BF)
        return carry

    lax.fori_loop(0, S, add_sides, 0, unroll=2)

    def convolve_other(block, carry):
        total = partial_out[pl.ds(block * rows, rows)].reshape(rows * S, C2)
        for a in range(3):
            for b in range(3):
                window = shifted[b, pl.ds(block * rows + a, rows)].reshape(rows * S, C2)
                total = total + jnp.dot(window, out_weight[1, 3 * a + b], preferred_element_type=F32)
        output[0, pl.ds(block * rows, rows)] = total.reshape(rows, S, C2).astype(BF)
        return carry

    lax.fori_loop(0, 2, convolve_other, 0)
    first.to_pair()
    second.to_pair()
    third.to_pair()
    for stream, spot in zip((first, second, third), lanes):
        stream.store(grad_weight, core, spot)
    for stream, spot in zip((first, second, third), lanes):
        stream.finish_pair()
        stream.store(grad_weight, 1 - core, spot)
    swap_a.finish_sends()
    swap_b.finish_sends()
    for copy in side_copies + piece_copies:
        copy.wait_send()
    for stream in (first, second, third):
        stream.finish()


def publish_kernel(a, b, c, a_out, b_out, c_out, sems):
    copies = [
        pltpu.make_async_copy(src, dst, sems.at[i])
        for i, (src, dst) in enumerate(((c, c_out), (a, a_out), (b, b_out)))
    ]
    for copy in copies:
        copy.start()
    for copy in copies:
        copy.wait()


VSPEC = pl.BlockSpec(memory_space=VM)
ANY = pl.BlockSpec(memory_space=pltpu.HBM)
DMA = pltpu.SemaphoreType.DMA
SM = pltpu.SMEM
REDUCE_BUFS = [
    ((2, 8 * CHUNK), F32),
    ((8, CHUNK), F32),
    ((7, CHUNK), BF),
    ((7, CHUNK), BF),
    ((7, UNIT), F32),
    ((7, UNIT), F32),
    ((2, 8, 7, UNIT), BF),
]
REDUCE_SEMS = [(2, 8), (2, 7), (2, 7), (2, 7), (2, 7), (2, 8)]


def reduce_scratch(width):
    return [VM(lead + (width,), kind) for lead, kind in REDUCE_BUFS] + [DMA(lead) for lead in REDUCE_SEMS]


def body(features, weight, cotangent, edge_tiles, edge_turns, corner_tiles, corner_turns):
    C2 = features.shape[3]
    C = 2 * C2
    shape = jax.ShapeDtypeStruct
    table = SM((4, 128), jnp.int32)
    output, grad_features, grad_weight = pl.pallas_call(
        lambda *refs: fused_kernel(1.0 / math.sqrt(128 * ROWS), *refs),
        name="fused",
        out_shape=(
            shape((1, S, S, C2), BF),
            shape((1, S, S, C2), BF),
            shape((9 * C2, C), F32),
        ),
        in_specs=[ANY] * 7,
        out_specs=(VSPEC,) * 3,
        scratch_shapes=[
            table, table, table, table,
            VM((S, S, C2), BF),
            VM((S, S, C2), BF),
            VM((9, C, C), BF),
            VM((9, C2, C), BF),
            VM((2, 9, C2, C2), BF),
            VM((2, S, C2), F32),
            VM((4, 16, C), BF),
            VM((8, 4, 16, C), BF),
            VM((8, 64, C), BF),
            VM((8, 64, C), BF),
            VM((2, 4, 64, C), BF),
            VM((3, S + 2, S, C2), BF),
            VM((2, 40, C2), F32),
            VM((3, S + 4, S, C), BF),
            VM((2, 48, C), F32),
            VM((S + 2, S, C2), F32),
            VM((5, 16, C), BF),
            VM((8, 5, 16, C), BF),
            VM((8, 5, 16, C), BF),
            VM((8, 5, 16, C), BF),
            VM((2, 4, 5, 16, C), BF),
            VM((3, S + 2, S, C2), BF),
            VM((S, S, C2), F32),
            VM((2, 8, 5, 16, 4 * S), BF),
            VM((4, S, C2), F32),
            VM((3 * C2, (S + 2) * S), BF),
            DMA((8,)),
            DMA((2, 8)),
            DMA((4, 8)),
            DMA((4, 8)),
            DMA((2, 8)),
        ]
        + reduce_scratch(128) * 3,
        compiler_params=pltpu.CompilerParams(
            vmem_limit_bytes=44 * 1024 * 1024, collective_id=0, has_side_effects=True
        ),
    )(
        *[pltpu.with_memory_space_constraint(x.T, pltpu.HBM) for x in (edge_tiles, edge_turns, corner_tiles, corner_turns)],
        *[pltpu.with_memory_space_constraint(x, pltpu.HBM) for x in (features[0], cotangent[0], weight.reshape(9, C, C))],
    )

    output, grad_features, grad_weight = pl.pallas_call(
        publish_kernel,
        name="publish",
        out_shape=(shape((1, S, S, C2), BF), shape((1, S, S, C2), BF), shape((9 * C2, C), F32)),
        in_specs=[pl.BlockSpec(memory_space=pl.ANY)] * 3,
        out_specs=(ANY,) * 3,
        scratch_shapes=[DMA((3,))],
        compiler_params=pltpu.CompilerParams(vmem_limit_bytes=1024 * 1024),
    )(output, grad_features, grad_weight)
    return (output, grad_features, grad_weight.reshape(3, 3, C2, C))


def solution(mesh):
    return jax.shard_map(
        body,
        mesh=mesh,
        in_specs=(
            P("tile", None, None, "ch"),
            P(),
            P("tile", None, None, "ch"),
            P(),
            P(),
            P(),
            P(),
        ),
        out_specs=(
            P("tile", None, None, "ch"),
            P("tile", None, None, "ch"),
            P(None, None, "ch", None),
        ),
        check_vma=False,
    )
```

```python
import math

import jax
import jax.numpy as jnp
import numpy as np
from jax import lax
from jax.experimental import pallas as pl
from jax.experimental.pallas import tpu as pltpu
from jax.sharding import PartitionSpec as P

MESH = pl.DeviceIdType.MESH
SPAN = 4
OFFSETS = [-4, -3, -2, -1, 1, 2, 3, 4]
S = 32
ROWS = S * S
UNIT = 16
VM = pltpu.VMEM
BF = jnp.bfloat16
F32 = jnp.float32


def turn_tables():
    labels = [[3 * row + col for col in range(3)] for row in range(3)]

    def turn_once(block):
        return [[block[col][2 - row] for col in range(3)] for row in range(3)]

    def sides_of(block):
        return [
            list(block[0]),
            [block[row][2] for row in range(3)],
            list(block[2]),
            [block[row][0] for row in range(3)],
        ]

    def corners_of(block):
        return [block[0][0], block[0][2], block[2][2], block[2][0]]

    base_sides = sides_of(labels)
    base_corners = corners_of(labels)
    edge_table = np.zeros((4, 4), np.int32)
    corner_table = np.zeros((4, 4), np.int32)
    for border in range(4):
        turned = labels
        for quarter in range(4):
            wanted = sides_of(turned)[(border + 2) % 4]
            for side_index in range(4):
                if base_sides[side_index] == wanted:
                    edge_table[border, quarter] = side_index
                if base_sides[side_index][::-1] == wanted:
                    edge_table[border, quarter] = side_index + 4
            corner_cell = corners_of(turned)[(border + 2) % 4]
            for corner_index in range(4):
                if base_corners[corner_index] == corner_cell:
                    corner_table[border, quarter] = corner_index
            turned = turn_once(turned)
    return (edge_table, corner_table)


EDGE_TABLE, CORNER_TABLE = turn_tables()


def lookup(table, border, turn):
    row = [int(v) for v in table[border]]
    value = jnp.int32(row[0])
    for quarter in range(1, 4):
        value = jnp.where(turn == quarter, jnp.int32(row[quarter]), value)
    return value


def slot_of(offset):
    return offset + SPAN if offset < 0 else offset + SPAN - 1


def wrap(index, size):
    return lax.rem(index + size, jnp.int32(size))


def coords():
    tile = lax.axis_index("tile")
    ch = lax.axis_index("ch")
    core = lax.rem(tile, 2)
    y = lax.rem(tile // 2, 4)
    xl = lax.rem(tile // 8, 2)
    z = tile // 16
    return tile, ch, core, y, xl, z


def dev(tile, ch):
    return {"tile": tile, "ch": ch}


def x_neighbours(tile, ch, xl):
    beside = tile + 8 - 16 * xl
    return dev(beside, ch), dev(beside, 1 - ch)


def remote(src, dst, send, recv, where):
    return pltpu.make_async_remote_copy(
        src_ref=src, dst_ref=dst, send_sem=send, recv_sem=recv, device_id=where, device_id_type=MESH
    )


class Swap:
    def __init__(self, src, dst, relay, sems, tile, ch, xl):
        self.n = relay.shape[1]
        near, far = x_neighbours(tile, ch, xl)
        self.first, self.second = [], []
        for i in range(self.n):
            for path in range(2):
                hop1, hop2 = (near, far) if path == 0 else (far, near)
                j = path * self.n + i
                self.first.append(remote(src.at[j], relay.at[path, i], sems.at[0, j], sems.at[1, j], hop1))
                self.second.append(remote(relay.at[path, i], dst.at[j], sems.at[2, j], sems.at[3, j], hop2))

    def start(self):
        for copy in self.first:
            copy.start()

    def relay(self, start=0, stop=None):
        for one, two in zip(self.first[start:stop], self.second[start:stop]):
            one.wait_recv()
            two.start()

    def finish_sends(self):
        for one, two in zip(self.first, self.second):
            one.wait_send()
            two.wait_send()


def near_copies(src, dst, sems, tile, ch, tiles):
    copies = []
    for offset in OFFSETS:
        k = slot_of(-offset)
        copies.append(
            remote(src, dst.at[k], sems.at[0, k], sems.at[1, k], dev(wrap(tile + offset, tiles), ch))
        )
    return copies


def iota2(shape, dim):
    return lax.broadcasted_iota(jnp.int32, shape, dim)


def source_slot(target, tile, tiles):
    away = wrap(target - tile, tiles)
    return jnp.clip(jnp.where(away > tiles // 2, away - tiles + SPAN, away + SPAN - 1), 0, 2 * SPAN - 1)


def spread_columns(buf, row, lanes, x, left, right):
    io = iota2(x.shape, 0)
    buf[1, row, :, lanes] = x.astype(BF)
    buf[0, row, :, lanes] = jnp.where(io == 0, left, pltpu.roll(x, 1, 0)).astype(BF)
    buf[2, row, :, lanes] = jnp.where(io == S - 1, right, pltpu.roll(x, S - 1, 0)).astype(BF)


def pack(x):
    n = x.shape[0] // 2
    return jnp.concatenate([x[:n, :128], x[n:, :128], x[:n, 128:], x[n:, 128:]], axis=1)


def unpack(x):
    low = jnp.concatenate([x[:, :128], x[:, 256:320]], axis=1)
    high = jnp.concatenate([x[:, 128:256], x[:, 320:]], axis=1)
    return jnp.concatenate([low, high], axis=0)


def one_hot_rows(rows, target, width):
    return jnp.where(iota2((rows, width), 1) == target, 1.0, 0.0).astype(BF)


TN = (((0,), (0,)), ((), ()))
NT = (((1,), (1,)), ((), ()))
CHUNK = 7 * UNIT


class Reduce:
    def __init__(self, scale, bufs, sems, place):
        self.grads, self.pair_in, self.sent, self.got, self.unit_out, self.unit_in, self.gathered = bufs
        self.scale = scale
        tile, ch, core, y, xl, z = place
        self.core = core
        self.pair = dev(tile + 1 - 2 * core, ch)
        across = (2 * y + xl, lambda g: dev(tile + 2 * (g // 2 - y) + 8 * (lax.rem(g, 2) - xl), ch))
        along = (z, lambda g: dev(tile + 16 * (g - z), ch))
        (spot, outer), (unit, inner) = across, along
        self.spot, self.unit = spot, unit
        self.order = [lax.rem(spot + 1 + j, 8) for j in range(7)] + [spot]
        self.unit_at = [lax.rem(unit + 1 + j, 8) for j in range(7)]
        self.unit_from = [lax.rem(unit + 7 - j, 8) for j in range(7)]
        self.outer_peers = [outer(g) for g in self.order[:7]]
        self.inner_peers = [inner(g) for g in self.unit_at]
        pair_sems, outer_sems, inner_sems, gather_sems, back_sems, last_sems = sems

        def copy(src, dst, pool, j, where):
            return remote(src, dst, pool.at[0, j], pool.at[1, j], where)

        def rows(half, g):
            return self.grads.at[half, pl.ds(pl.multiple_of(g * CHUNK, CHUNK), CHUNK)]

        self.own = jnp.minimum(unit, 6)
        mine = self.gathered.at[core, spot]
        cell = mine.at[self.own]
        seven = range(7)
        def pair_copy(g):
            return copy(rows(1 - core, g), self.pair_in.at[g], pair_sems, g, self.pair)

        self.pair_starts = [pair_copy(g) for g in range(8)]
        self.pair_copies = [pair_copy(g) for g in self.order]
        self.copies = [
            copy(self.sent.at[j], self.got.at[j], outer_sems, j, self.outer_peers[j]) for j in seven
        ]
        self.unit_copies = [
            copy(
                self.unit_out.at[jnp.minimum(self.unit_at[j], 6)], self.unit_in.at[j],
                inner_sems, j, self.inner_peers[j],
            )
            for j in seven
        ]
        self.gather = [copy(cell, cell, gather_sems, j, self.inner_peers[j]) for j in seven]
        near, _ = x_neighbours(tile, ch, xl)
        column = [dev(tile + 2 * (lax.rem(y + 1 + j, 4) - y), ch) for j in range(3)]
        beside = self.gathered.at[core, 2 * y + 1 - xl]
        self.back = [copy(mine, mine, back_sems, 0, near)]
        self.back += [copy(mine, mine, back_sems, 1 + j, column[j]) for j in range(3)]
        self.back += [copy(beside, beside, back_sems, 4 + j, column[j]) for j in range(3)]
        got = [2 * y + 1 - xl]
        for other in (xl, 1 - xl):
            got += [2 * lax.rem(y + 3 - j, 4) + other for j in range(3)]
        self.last = []
        for j, g in enumerate([spot] + got):
            block = self.gathered.at[core, g]
            self.last.append(copy(block, block, last_sems, j, self.pair))

    def own_rows(self, g):
        return self.grads[self.core, pl.ds(pl.multiple_of(g * CHUNK, CHUNK), CHUNK)]

    def start(self, step, begin):
        for g, copy in enumerate(self.pair_starts):
            early = g <= 4 if begin == 0 else g >= 3
            if early == (step == 0):
                copy.start()

    def to_outer(self):
        for j in range(7):
            self.pair_copies[j].wait_recv()
            self.sent[j] = (self.own_rows(self.order[j]) + self.pair_in[self.order[j]]).astype(BF)
            self.copies[j].start()

    def to_inner(self):
        self.pair_copies[7].wait_recv()
        total = self.own_rows(self.spot) + self.pair_in[self.spot]
        for j in range(7):
            self.copies[j].wait_recv()
            total = total + self.got[j].astype(F32)
        self.unit_out[...] = total.reshape(self.unit_out.shape)
        for j in range(7):
            pl.when(self.unit_at[j] != 7)(self.unit_copies[j].start)

    def to_gather(self):
        @pl.when(self.unit != 7)
        def _():
            total = self.unit_out[self.own]
            for j in range(7):
                self.unit_copies[j].wait_recv()
                total = total + self.unit_in[j]
            self.gathered[self.core, self.spot, self.own] = (total * self.scale).astype(BF)
            for copy in self.gather:
                copy.start()

    def to_back(self):
        for j in range(7):
            pl.when(self.unit_from[j] != 7)(self.gather[j].wait_recv)
        for copy in self.back[:4]:
            copy.start()
        self.last[0].start()

    def pass_back(self):
        self.back[0].wait_recv()
        for copy in self.back[4:]:
            copy.start()
        self.last[1].start()

    def to_pair(self):
        for j in range(1, 7):
            self.back[j].wait_recv()
            self.last[j + 1].start()

    def store(self, out, half, lanes):
        width = self.gathered.shape[4]
        filled = 9 * (out.shape[1] // 4)
        for g in range(8):
            rows = min(CHUNK, filled - g * CHUNK)
            block = self.gathered[half, g].astype(F32).reshape(CHUNK, width)
            out[pl.ds(pl.multiple_of(half * filled + g * CHUNK, 16), rows), lanes] = block[:rows]

    def finish_pair(self):
        for copy in self.last:
            copy.wait()

    def finish(self):
        for copy in self.pair_copies + self.copies + self.back:
            copy.wait_send()
        for j in range(7):
            pl.when(self.unit_at[j] != 7)(self.unit_copies[j].wait_send)
            pl.when(self.unit != 7)(self.gather[j].wait_send)


def fused_kernel(
    scale,
    edge_tiles_in, edge_turns_in, corner_tiles_in, corner_turns_in, feat_in, cot_in, weight_in,
    output, grad_features, grad_weight,
    edge_tiles, edge_turns, corner_tiles, corner_turns,
    feat, cot, weight, rows_weight, out_weight,
    lines, sides, all_sides, cot_packed, cot_other, relay_a,
    padded, columns, cots, cot_columns, interior, pieces, all_pieces,
    packed, packed_other, relay_b, shifted, partial_out, hits, sums, turned,
    load_sems, side_sems, swap_a_sems, swap_b_sems, piece_sems,
    *streams,
):
    tiles = 128
    place = tile, ch, core, y, xl, z = coords()
    C2 = feat.shape[2]
    C = 2 * C2
    near, far = x_neighbours(tile, ch, xl)
    bufs = len(REDUCE_BUFS)
    sems = len(REDUCE_SEMS)
    first, second, third = [
        Reduce(
            scale,
            streams[i * (bufs + sems) : i * (bufs + sems) + bufs],
            streams[i * (bufs + sems) + bufs : (i + 1) * (bufs + sems)],
            place,
        )
        for i in range(3)
    ]
    greeted = [dev(wrap(tile + o, tiles), ch) for o in OFFSETS] + [near, far, first.pair]
    greeted = greeted + first.outer_peers + first.inner_peers
    ready = pltpu.get_barrier_semaphore()
    for where in greeted:
        pl.semaphore_signal(ready, inc=1, device_id=where, device_id_type=MESH)

    own_rows = pl.ds(pl.multiple_of(ch * C2, 64), C2)
    loads = [
        pltpu.make_async_copy(a, b, load_sems.at[i])
        for i, (a, b) in enumerate(
            (
                (feat_in, feat),
                (cot_in, cot),
                (edge_tiles_in, edge_tiles),
                (edge_turns_in, edge_turns),
                (corner_tiles_in, corner_tiles),
                (corner_turns_in, corner_turns),
                (weight_in, weight),
                (weight_in.at[:, own_rows], rows_weight),
            )
        )
    ]
    for load in loads[:6]:
        load.start()

    loads[0].wait()

    def take_columns(row, carry):
        x = feat[row].astype(F32)
        lines[0, pl.ds(row, 1)] = x[0:1]
        lines[1, pl.ds(row, 1)] = x[S - 1 : S]
        return carry

    lax.fori_loop(0, S, take_columns, 0, unroll=4)
    sides[0] = pack(feat[0])
    sides[1] = pack(lines[1].astype(BF))
    sides[2] = pack(feat[S - 1])
    sides[3] = pack(lines[0].astype(BF))
    loads[1].wait()

    def pack_cot(row, carry):
        for i in range(4):
            cot_packed[row, 16 * i : 16 * i + 16] = pack(cot[4 * row + i])
        return carry

    lax.fori_loop(0, S // 4, pack_cot, 0)
    pl.semaphore_wait(ready, len(greeted))
    swap_a = Swap(cot_packed, cot_other, relay_a, swap_a_sems, tile, ch, xl)
    swap_a.start()
    side_copies = near_copies(sides, all_sides, side_sems, tile, ch, tiles)
    for copy in side_copies:
        copy.start()
    for load in loads[6:]:
        load.start()

    zero = jnp.zeros((S, C), BF)
    for part in range(3):
        for row in (0, 1, S + 2, S + 3):
            cots[part, row] = zero
    cot_columns[...] = jnp.zeros_like(cot_columns)
    nothing = jnp.zeros((1, C2), F32)

    def fill(read, lanes):
        def shift(row, carry):
            x = read(row).astype(F32)
            spread_columns(cots, row + 2, lanes, x, nothing, nothing)
            cot_columns[0, pl.ds(row + 2, 1), lanes] = x[0:1]
            cot_columns[1, pl.ds(row + 2, 1), lanes] = x[S - 1 : S]
            return carry

        lax.fori_loop(0, S, shift, 0, unroll=8)

    def read_other(row):
        at = pl.multiple_of(lax.rem(row, 4) * 16, 16)
        return unpack(cot_other[row // 4, pl.ds(at, 16)])

    pl.when(ch == 0)(lambda: fill(lambda row: cot[row], slice(0, C2)))
    pl.when(ch == 1)(lambda: fill(lambda row: cot[row], slice(C2, C)))
    swap_a.relay()

    for i in range(2, 6):
        loads[i].wait()
    for copy in side_copies:
        copy.wait_recv()
    halos = []
    for border in range(4):
        source = source_slot(edge_tiles[border, tile], tile, tiles)
        slot = lookup(EDGE_TABLE, border, edge_turns[border, tile])
        rev = slot // 4
        x = unpack(all_sides[source, slot - 4 * rev])
        ii = iota2((S, 1), 0)
        hot = one_hot_rows(S, jnp.where(rev == 1, S - 1 - ii, ii), S)
        halos.append(jnp.dot(hot, x, preferred_element_type=F32))
    columns[0, 1 : S + 1] = halos[3]
    columns[1, 1 : S + 1] = halos[1]
    for corner in range(4):
        source = source_slot(corner_tiles[corner, tile], tile, tiles)
        slot = lookup(CORNER_TABLE, corner, corner_turns[corner, tile])
        cells = unpack(all_sides[source, jnp.where(slot < 2, 0, 2)]).astype(F32)
        start = (slot == 0) | (slot == 3)
        at = 0 if corner < 2 else S + 1
        columns[(0, 1, 1, 0)[corner], at : at + 1] = jnp.where(start, cells[0:1], cells[S - 1 : S])
    padded[1, 0] = halos[0].astype(BF)
    padded[1, S + 1] = halos[2].astype(BF)
    padded[1, 1 : S + 1] = feat[...]

    def shift_features(row, carry):
        x = padded[1, row].astype(F32)
        spread_columns(
            padded, row, slice(0, C2), x, columns[0, pl.ds(row, 1)], columns[1, pl.ds(row, 1)]
        )
        return carry

    lax.fori_loop(0, S + 2, shift_features, 0, unroll=17)
    for b in range(3):
        turned[b * C2 : (b + 1) * C2] = padded[b].reshape((S + 2) * S, C2).T
    filled = 9 * (C2 // 2)

    def weight_grad(parts, lanes):
        width = 128 * len(parts)
        for stream in parts:
            stream.grads[:, filled:] = jnp.zeros((2, 8 * CHUNK - filled, 128), F32)

        def products(order):
            for step, a in enumerate(order):
                full = cots[1, 2 - a : 2 - a + S + 2, :, lanes].reshape((S + 2) * S, width)
                result = jnp.dot(turned[...], full, preferred_element_type=F32)
                for i, stream in enumerate(parts):
                    for half in range(2):
                        low = max(half * filled, 3 * a * C2)
                        high = min((half + 1) * filled, 3 * (a + 1) * C2)
                        if low < high:
                            stream.grads[half, low - half * filled : high - half * filled] = result[
                                low - 3 * a * C2 : high - 3 * a * C2, 128 * i : 128 * (i + 1)
                            ]
                    if step < 2:
                        stream.start(step, order[0])

        pl.when(core == 1)(lambda: products((0, 1, 2)))
        pl.when(core == 0)(lambda: products((2, 1, 0)))

    lanes = [pl.ds(pl.multiple_of(at, 128), 128) for at in (256 * ch, 128 - 128 * ch, 256 - 128 * ch)]
    weight_grad([first], lanes[0])
    for copy in swap_a.second:
        copy.wait_recv()

    def place_other(lanes):
        def one_row(row, carry):
            cots[1, row + 2, :, lanes] = read_other(row)
            return carry

        lax.fori_loop(0, S, one_row, 0, unroll=8)

    pl.when(ch == 0)(lambda: place_other(slice(C2, C)))
    pl.when(ch == 1)(lambda: place_other(slice(0, C2)))
    first.to_outer()
    weight_grad([second, third], pl.ds(pl.multiple_of(128 - 128 * ch, 128), 256))
    second.to_outer()
    third.to_outer()

    def pack_padded(row, carry):
        packed[row // 5, lax.rem(row, 5)] = pack(padded[1, row])
        return carry

    lax.fori_loop(0, S + 2, pack_padded, 0, unroll=2)
    packed[6, 4] = pack(columns[0, 1 : S + 1].astype(BF))
    packed[7, 0] = pack(columns[1, 1 : S + 1].astype(BF))
    io = iota2((16, C2), 0)
    ends = jnp.zeros((16, C2), F32)
    for corner in range(4):
        at = 0 if corner < 2 else S + 1
        ends = jnp.where(io == corner, columns[(0, 1, 1, 0)[corner], at : at + 1], ends)
    packed[7, 1] = pack(jnp.concatenate([ends, ends], axis=0).astype(BF))
    for i in range(2, 5):
        packed[7, i] = jnp.zeros((16, C), BF)
    swap_b = Swap(packed, packed_other, relay_b, swap_b_sems, tile, ch, xl)
    swap_b.start()

    pl.when(ch == 0)(lambda: fill(read_other, slice(C2, C)))
    pl.when(ch == 1)(lambda: fill(read_other, slice(0, C2)))

    first.to_inner()
    loads[7].wait()
    half = (S + 2) // 2

    def feature_grad(block, carry):
        total = None
        for a in range(3):
            for b in range(3):
                window = cots[2 - b, pl.ds(block * half + 2 - a, half)].reshape(half * S, C)
                term = lax.dot_general(window, rows_weight[3 * a + b], NT, preferred_element_type=F32)
                total = term if total is None else total + term
        interior[pl.ds(block * half, half)] = total.reshape(half, S, C2)
        return carry

    lax.fori_loop(0, 2, feature_grad, 0)
    pieces[0] = pack(interior[0].astype(BF))
    pieces[2] = pack(interior[S + 1].astype(BF))
    tips = []
    for side in range(2):
        total = None
        for a in range(3):
            line = cot_columns[side, 2 - a : 2 - a + 40].astype(BF)
            term = lax.dot_general(line, rows_weight[3 * a + 2 * side], NT, preferred_element_type=F32)
            total = term if total is None else total + term
        cot_columns[side, 0:40, 0:C2] = total
        pieces[3 - 2 * side] = pack(cot_columns[side, 1 : S + 1, 0:C2].astype(BF))
        tips.append((total[0:1], total[S + 1 : S + 2]))
    io = iota2((16, C2), 0)
    ends = jnp.zeros((16, C2), F32)
    for corner, value in enumerate((tips[0][0], tips[1][0], tips[1][1], tips[0][1])):
        ends = jnp.where(io == corner, value, ends)
    pieces[4] = pack(jnp.concatenate([ends, ends], axis=0).astype(BF))
    second.to_inner()
    third.to_inner()
    piece_copies = near_copies(pieces, all_pieces, piece_sems, tile, ch, tiles)
    for copy in piece_copies:
        copy.start()

    first.to_gather()
    loads[6].wait()

    def pick_weight(tap, carry):
        for part in range(2):
            input_half = ch if part == 0 else 1 - ch
            w = weight[tap, pl.ds(pl.multiple_of(input_half * C2, 64), C2)].astype(F32)
            out_weight[part, tap] = jnp.where(ch == 0, w[:, :C2], w[:, C2:]).astype(BF)
        return carry

    lax.fori_loop(0, 9, pick_weight, 0)
    swap_b.relay(0, 4)

    rows = S // 2

    def convolve_own(block, carry):
        total = None
        for a in range(3):
            for b in range(3):
                window = padded[b, pl.ds(block * rows + a, rows)].reshape(rows * S, C2)
                term = jnp.dot(window, out_weight[0, 3 * a + b], preferred_element_type=F32)
                total = term if total is None else total + term
        partial_out[pl.ds(block * rows, rows)] = total.reshape(rows, S, C2)
        return carry

    lax.fori_loop(0, 2, convolve_own, 0)
    swap_b.relay(4, 6)
    second.to_gather()
    swap_b.relay(6)
    third.to_gather()

    for offset in OFFSETS:
        k = slot_of(-offset)
        source = wrap(tile - offset, tiles)
        for border in range(4):
            hit = edge_tiles[border, source] == tile
            slot = lookup(EDGE_TABLE, border, edge_turns[border, source])
            rev = slot // 4
            ii = iota2((S, 1), 0)
            target = jnp.where(rev == 1, S - 1 - ii, ii) + (slot - 4 * rev) * S
            hot = one_hot_rows(S, jnp.where(hit, target, -1), 4 * S)
            hits[0, k, border] = hot[:16]
            hits[1, k, border] = hot[16:]
        ii = iota2((16, 1), 0)
        target = jnp.full((16, 1), -1, jnp.int32)
        for corner in range(4):
            hit = corner_tiles[corner, source] == tile
            slot = lookup(CORNER_TABLE, corner, corner_turns[corner, source])
            cell = jnp.where(slot < 2, 0, 2 * S) + jnp.where((slot == 0) | (slot == 3), 0, S - 1)
            target = jnp.where((ii == corner) & hit, cell, target)
        hits[0, k, 4] = one_hot_rows(16, target, 4 * S)
        hits[1, k, 4] = jnp.zeros((16, 4 * S), BF)

    first.to_back()
    second.to_back()
    third.to_back()
    first.pass_back()
    second.pass_back()
    third.pass_back()

    for copy in swap_b.second:
        copy.wait_recv()
    columns[0, 1 : S + 1] = unpack(packed_other[6, 4]).astype(F32)
    columns[1, 1 : S + 1] = unpack(packed_other[7, 0]).astype(F32)
    ends = unpack(packed_other[7, 1]).astype(F32)
    for corner in range(4):
        at = 0 if corner < 2 else S + 1
        columns[(0, 1, 1, 0)[corner], at : at + 1] = ends[corner : corner + 1]

    def shift_partner(row, carry):
        x = unpack(packed_other[row // 5, lax.rem(row, 5)]).astype(F32)
        spread_columns(
            shifted, row, slice(0, C2), x, columns[0, pl.ds(row, 1)], columns[1, pl.ds(row, 1)]
        )
        return carry

    lax.fori_loop(0, S + 2, shift_partner, 0, unroll=2)
    for copy in piece_copies:
        copy.wait_recv()

    flat = all_pieces[...].reshape(8 * 5 * 16, C)
    parts = [
        lax.dot_general(hits[i].reshape(8 * 5 * 16, 4 * S), flat, TN, preferred_element_type=F32)
        for i in range(2)
    ]
    low = jnp.concatenate([parts[0][:, :128], parts[0][:, 256:320]], axis=1)
    high = jnp.concatenate([parts[1][:, 128:256], parts[1][:, 320:]], axis=1)
    sums[...] = (low + high).reshape(4, S, C2)
    def add_sides(row, carry):
        io = iota2((S, C2), 0)
        x = interior[row + 1]
        x = x + jnp.where(io == 0, sums[3, pl.ds(row, 1)], 0.0)
        x = x + jnp.where(io == S - 1, sums[1, pl.ds(row, 1)], 0.0)
        x = x + jnp.where(row == 0, sums[0], 0.0)
        x = x + jnp.where(row == S - 1, sums[2], 0.0)
        grad_features[0, row] = x.astype(BF)
        return carry

    lax.fori_loop(0, S, add_sides, 0, unroll=2)

    def convolve_other(block, carry):
        total = partial_out[pl.ds(block * rows, rows)].reshape(rows * S, C2)
        for a in range(3):
            for b in range(3):
                window = shifted[b, pl.ds(block * rows + a, rows)].reshape(rows * S, C2)
                total = total + jnp.dot(window, out_weight[1, 3 * a + b], preferred_element_type=F32)
        output[0, pl.ds(block * rows, rows)] = total.reshape(rows, S, C2).astype(BF)
        return carry

    lax.fori_loop(0, 2, convolve_other, 0)
    first.to_pair()
    second.to_pair()
    third.to_pair()
    for stream, spot in zip((first, second, third), lanes):
        stream.store(grad_weight, core, spot)
    for stream, spot in zip((first, second, third), lanes):
        stream.finish_pair()
        stream.store(grad_weight, 1 - core, spot)
    swap_a.finish_sends()
    swap_b.finish_sends()
    for copy in side_copies + piece_copies:
        copy.wait_send()
    for stream in (first, second, third):
        stream.finish()


def publish_kernel(a, b, c, a_out, b_out, c_out, sems):
    copies = [
        pltpu.make_async_copy(src, dst, sems.at[i])
        for i, (src, dst) in enumerate(
            [(c.at[pl.ds(k * 432, 432)], c_out.at[pl.ds(k * 432, 432)]) for k in range(4)]
            + [(a, a_out), (b, b_out)]
        )
    ]
    for copy in copies:
        copy.start()
    for copy in copies:
        copy.wait()


VSPEC = pl.BlockSpec(memory_space=VM)
ANY = pl.BlockSpec(memory_space=pltpu.HBM)
DMA = pltpu.SemaphoreType.DMA
SM = pltpu.SMEM
REDUCE_BUFS = [
    ((2, 8 * CHUNK), F32),
    ((8, CHUNK), F32),
    ((7, CHUNK), BF),
    ((7, CHUNK), BF),
    ((7, UNIT), F32),
    ((7, UNIT), F32),
    ((2, 8, 7, UNIT), BF),
]
REDUCE_SEMS = [(2, 8), (2, 7), (2, 7), (2, 7), (2, 7), (2, 8)]


def reduce_scratch(width):
    return [VM(lead + (width,), kind) for lead, kind in REDUCE_BUFS] + [DMA(lead) for lead in REDUCE_SEMS]


def body(features, weight, cotangent, edge_tiles, edge_turns, corner_tiles, corner_turns):
    C2 = features.shape[3]
    C = 2 * C2
    shape = jax.ShapeDtypeStruct
    table = SM((4, 128), jnp.int32)
    output, grad_features, grad_weight = pl.pallas_call(
        lambda *refs: fused_kernel(1.0 / math.sqrt(128 * ROWS), *refs),
        name="fused",
        out_shape=(
            shape((1, S, S, C2), BF),
            shape((1, S, S, C2), BF),
            shape((9 * C2, C), F32),
        ),
        in_specs=[ANY] * 7,
        out_specs=(VSPEC,) * 3,
        scratch_shapes=[
            table, table, table, table,
            VM((S, S, C2), BF),
            VM((S, S, C2), BF),
            VM((9, C, C), BF),
            VM((9, C2, C), BF),
            VM((2, 9, C2, C2), BF),
            VM((2, S, C2), F32),
            VM((4, 16, C), BF),
            VM((8, 4, 16, C), BF),
            VM((8, 64, C), BF),
            VM((8, 64, C), BF),
            VM((2, 4, 64, C), BF),
            VM((3, S + 2, S, C2), BF),
            VM((2, 40, C2), F32),
            VM((3, S + 4, S, C), BF),
            VM((2, 48, C), F32),
            VM((S + 2, S, C2), F32),
            VM((5, 16, C), BF),
            VM((8, 5, 16, C), BF),
            VM((8, 5, 16, C), BF),
            VM((8, 5, 16, C), BF),
            VM((2, 4, 5, 16, C), BF),
            VM((3, S + 2, S, C2), BF),
            VM((S, S, C2), F32),
            VM((2, 8, 5, 16, 4 * S), BF),
            VM((4, S, C2), F32),
            VM((3 * C2, (S + 2) * S), BF),
            DMA((8,)),
            DMA((2, 8)),
            DMA((4, 8)),
            DMA((4, 8)),
            DMA((2, 8)),
        ]
        + reduce_scratch(128) * 3,
        compiler_params=pltpu.CompilerParams(
            vmem_limit_bytes=44 * 1024 * 1024, collective_id=0, has_side_effects=True
        ),
    )(
        *[pltpu.with_memory_space_constraint(x.T, pltpu.HBM) for x in (edge_tiles, edge_turns, corner_tiles, corner_turns)],
        *[pltpu.with_memory_space_constraint(x, pltpu.HBM) for x in (features[0], cotangent[0], weight.reshape(9, C, C))],
    )

    output, grad_features, grad_weight = pl.pallas_call(
        publish_kernel,
        name="publish",
        out_shape=(shape((1, S, S, C2), BF), shape((1, S, S, C2), BF), shape((9 * C2, C), F32)),
        in_specs=[pl.BlockSpec(memory_space=pl.ANY)] * 3,
        out_specs=(ANY,) * 3,
        scratch_shapes=[DMA((6,))],
        compiler_params=pltpu.CompilerParams(vmem_limit_bytes=1024 * 1024),
    )(output, grad_features, grad_weight)
    return (output, grad_features, grad_weight.reshape(3, 3, C2, C))


def solution(mesh):
    return jax.shard_map(
        body,
        mesh=mesh,
        in_specs=(
            P("tile", None, None, "ch"),
            P(),
            P("tile", None, None, "ch"),
            P(),
            P(),
            P(),
            P(),
        ),
        out_specs=(
            P("tile", None, None, "ch"),
            P("tile", None, None, "ch"),
            P(None, None, "ch", None),
        ),
        check_vma=False,
    )
```

```python
import math

import jax
import jax.numpy as jnp
import numpy as np
from jax import lax
from jax.experimental import pallas as pl
from jax.experimental.pallas import tpu as pltpu
from jax.sharding import PartitionSpec as P

MESH = pl.DeviceIdType.MESH
SPAN = 4
OFFSETS = [-4, -3, -2, -1, 1, 2, 3, 4]
S = 32
ROWS = S * S
UNIT = 16
VM = pltpu.VMEM
BF = jnp.bfloat16
F32 = jnp.float32


def turn_tables():
    labels = [[3 * row + col for col in range(3)] for row in range(3)]

    def turn_once(block):
        return [[block[col][2 - row] for col in range(3)] for row in range(3)]

    def sides_of(block):
        return [
            list(block[0]),
            [block[row][2] for row in range(3)],
            list(block[2]),
            [block[row][0] for row in range(3)],
        ]

    def corners_of(block):
        return [block[0][0], block[0][2], block[2][2], block[2][0]]

    base_sides = sides_of(labels)
    base_corners = corners_of(labels)
    edge_table = np.zeros((4, 4), np.int32)
    corner_table = np.zeros((4, 4), np.int32)
    for border in range(4):
        turned = labels
        for quarter in range(4):
            wanted = sides_of(turned)[(border + 2) % 4]
            for side_index in range(4):
                if base_sides[side_index] == wanted:
                    edge_table[border, quarter] = side_index
                if base_sides[side_index][::-1] == wanted:
                    edge_table[border, quarter] = side_index + 4
            corner_cell = corners_of(turned)[(border + 2) % 4]
            for corner_index in range(4):
                if base_corners[corner_index] == corner_cell:
                    corner_table[border, quarter] = corner_index
            turned = turn_once(turned)
    return (edge_table, corner_table)


EDGE_TABLE, CORNER_TABLE = turn_tables()


def lookup(table, border, turn):
    row = [int(v) for v in table[border]]
    value = jnp.int32(row[0])
    for quarter in range(1, 4):
        value = jnp.where(turn == quarter, jnp.int32(row[quarter]), value)
    return value


def slot_of(offset):
    return offset + SPAN if offset < 0 else offset + SPAN - 1


def wrap(index, size):
    return lax.rem(index + size, jnp.int32(size))


def coords():
    tile = lax.axis_index("tile")
    ch = lax.axis_index("ch")
    core = lax.rem(tile, 2)
    y = lax.rem(tile // 2, 4)
    xl = lax.rem(tile // 8, 2)
    z = tile // 16
    return tile, ch, core, y, xl, z


def dev(tile, ch):
    return {"tile": tile, "ch": ch}


def x_neighbours(tile, ch, xl):
    beside = tile + 8 - 16 * xl
    return dev(beside, ch), dev(beside, 1 - ch)


def remote(src, dst, send, recv, where):
    return pltpu.make_async_remote_copy(
        src_ref=src, dst_ref=dst, send_sem=send, recv_sem=recv, device_id=where, device_id_type=MESH
    )


class Swap:
    def __init__(self, src, dst, relay, sems, tile, ch, xl):
        self.n = relay.shape[1]
        near, far = x_neighbours(tile, ch, xl)
        self.first, self.second = [], []
        for i in range(self.n):
            for path in range(2):
                hop1, hop2 = (near, far) if path == 0 else (far, near)
                j = path * self.n + i
                self.first.append(remote(src.at[j], relay.at[path, i], sems.at[0, j], sems.at[1, j], hop1))
                self.second.append(remote(relay.at[path, i], dst.at[j], sems.at[2, j], sems.at[3, j], hop2))

    def start(self):
        for copy in self.first:
            copy.start()

    def relay(self, start=0, stop=None):
        for one, two in zip(self.first[start:stop], self.second[start:stop]):
            one.wait_recv()
            two.start()

    def finish_sends(self):
        for one, two in zip(self.first, self.second):
            one.wait_send()
            two.wait_send()


def near_copies(src, dst, sems, tile, ch, tiles):
    copies = []
    for offset in OFFSETS:
        k = slot_of(-offset)
        copies.append(
            remote(src, dst.at[k], sems.at[0, k], sems.at[1, k], dev(wrap(tile + offset, tiles), ch))
        )
    return copies


def iota2(shape, dim):
    return lax.broadcasted_iota(jnp.int32, shape, dim)


def source_slot(target, tile, tiles):
    away = wrap(target - tile, tiles)
    return jnp.clip(jnp.where(away > tiles // 2, away - tiles + SPAN, away + SPAN - 1), 0, 2 * SPAN - 1)


def spread_columns(buf, row, lanes, x, left, right):
    io = iota2(x.shape, 0)
    buf[1, row, :, lanes] = x.astype(BF)
    buf[0, row, :, lanes] = jnp.where(io == 0, left, pltpu.roll(x, 1, 0)).astype(BF)
    buf[2, row, :, lanes] = jnp.where(io == S - 1, right, pltpu.roll(x, S - 1, 0)).astype(BF)


def pack(x):
    n = x.shape[0] // 2
    return jnp.concatenate([x[:n, :128], x[n:, :128], x[:n, 128:], x[n:, 128:]], axis=1)


def unpack(x):
    low = jnp.concatenate([x[:, :128], x[:, 256:320]], axis=1)
    high = jnp.concatenate([x[:, 128:256], x[:, 320:]], axis=1)
    return jnp.concatenate([low, high], axis=0)


def one_hot_rows(rows, target, width):
    return jnp.where(iota2((rows, width), 1) == target, 1.0, 0.0).astype(BF)


TN = (((0,), (0,)), ((), ()))
NT = (((1,), (1,)), ((), ()))
CHUNK = 7 * UNIT


class Reduce:
    def __init__(self, scale, bufs, sems, place):
        self.grads, self.pair_in, self.sent, self.got, self.unit_out, self.unit_in, self.gathered = bufs
        self.scale = scale
        tile, ch, core, y, xl, z = place
        self.core = core
        self.pair = dev(tile + 1 - 2 * core, ch)
        across = (2 * y + xl, lambda g: dev(tile + 2 * (g // 2 - y) + 8 * (lax.rem(g, 2) - xl), ch))
        along = (z, lambda g: dev(tile + 16 * (g - z), ch))
        (spot, outer), (unit, inner) = across, along
        self.spot, self.unit = spot, unit
        self.order = [lax.rem(spot + 1 + j, 8) for j in range(7)] + [spot]
        self.unit_at = [lax.rem(unit + 1 + j, 8) for j in range(7)]
        self.unit_from = [lax.rem(unit + 7 - j, 8) for j in range(7)]
        self.outer_peers = [outer(g) for g in self.order[:7]]
        self.inner_peers = [inner(g) for g in self.unit_at]
        pair_sems, outer_sems, inner_sems, gather_sems, back_sems, last_sems = sems

        def copy(src, dst, pool, j, where):
            return remote(src, dst, pool.at[0, j], pool.at[1, j], where)

        def rows(half, g):
            return self.grads.at[half, pl.ds(pl.multiple_of(g * CHUNK, CHUNK), CHUNK)]

        self.own = jnp.minimum(unit, 6)
        mine = self.gathered.at[core, spot]
        cell = mine.at[self.own]
        seven = range(7)
        def pair_copy(g):
            return copy(rows(1 - core, g), self.pair_in.at[g], pair_sems, g, self.pair)

        self.pair_starts = [pair_copy(g) for g in range(8)]
        self.pair_copies = [pair_copy(g) for g in self.order]
        self.copies = [
            copy(self.sent.at[j], self.got.at[j], outer_sems, j, self.outer_peers[j]) for j in seven
        ]
        self.unit_copies = [
            copy(
                self.unit_out.at[jnp.minimum(self.unit_at[j], 6)], self.unit_in.at[j],
                inner_sems, j, self.inner_peers[j],
            )
            for j in seven
        ]
        self.gather = [copy(cell, cell, gather_sems, j, self.inner_peers[j]) for j in seven]
        near, _ = x_neighbours(tile, ch, xl)
        column = [dev(tile + 2 * (lax.rem(y + 1 + j, 4) - y), ch) for j in range(3)]
        beside = self.gathered.at[core, 2 * y + 1 - xl]
        self.back = [copy(mine, mine, back_sems, 0, near)]
        self.back += [copy(mine, mine, back_sems, 1 + j, column[j]) for j in range(3)]
        self.back += [copy(beside, beside, back_sems, 4 + j, column[j]) for j in range(3)]
        got = [2 * y + 1 - xl]
        for other in (xl, 1 - xl):
            got += [2 * lax.rem(y + 3 - j, 4) + other for j in range(3)]
        self.last = []
        for j, g in enumerate([spot] + got):
            block = self.gathered.at[core, g]
            self.last.append(copy(block, block, last_sems, j, self.pair))

    def own_rows(self, g):
        return self.grads[self.core, pl.ds(pl.multiple_of(g * CHUNK, CHUNK), CHUNK)]

    def start(self, step, begin):
        for g, copy in enumerate(self.pair_starts):
            early = g <= 4 if begin == 0 else g >= 3
            if early == (step == 0):
                copy.start()

    def to_outer(self):
        for j in range(7):
            self.pair_copies[j].wait_recv()
            self.sent[j] = (self.own_rows(self.order[j]) + self.pair_in[self.order[j]]).astype(BF)
            self.copies[j].start()

    def to_inner(self):
        self.pair_copies[7].wait_recv()
        total = self.own_rows(self.spot) + self.pair_in[self.spot]
        for j in range(7):
            self.copies[j].wait_recv()
            total = total + self.got[j].astype(F32)
        self.unit_out[...] = total.reshape(self.unit_out.shape)
        for j in range(7):
            pl.when(self.unit_at[j] != 7)(self.unit_copies[j].start)

    def to_gather(self):
        @pl.when(self.unit != 7)
        def _():
            total = self.unit_out[self.own]
            for j in range(7):
                self.unit_copies[j].wait_recv()
                total = total + self.unit_in[j]
            self.gathered[self.core, self.spot, self.own] = (total * self.scale).astype(BF)
            for copy in self.gather:
                copy.start()

    def to_back(self):
        for j in range(7):
            pl.when(self.unit_from[j] != 7)(self.gather[j].wait_recv)
        for copy in self.back[:4]:
            copy.start()
        self.last[0].start()

    def pass_back(self):
        self.back[0].wait_recv()
        for copy in self.back[4:]:
            copy.start()
        self.last[1].start()

    def to_pair(self):
        for j in range(1, 7):
            self.back[j].wait_recv()
            self.last[j + 1].start()

    def store(self, out, half, lanes):
        width = self.gathered.shape[4]
        filled = 9 * (out.shape[1] // 4)
        for g in range(8):
            rows = min(CHUNK, filled - g * CHUNK)
            block = self.gathered[half, g].astype(F32).reshape(CHUNK, width)
            out[pl.ds(pl.multiple_of(half * filled + g * CHUNK, 16), rows), lanes] = block[:rows]

    def finish_pair(self):
        for copy in self.last:
            copy.wait()

    def finish(self):
        for copy in self.pair_copies + self.copies + self.back:
            copy.wait_send()
        for j in range(7):
            pl.when(self.unit_at[j] != 7)(self.unit_copies[j].wait_send)
            pl.when(self.unit != 7)(self.gather[j].wait_send)


def fused_kernel(
    scale,
    edge_tiles_in, edge_turns_in, corner_tiles_in, corner_turns_in, feat_in, cot_in, weight_in,
    output, grad_features, grad_weight,
    edge_tiles, edge_turns, corner_tiles, corner_turns,
    feat, cot, weight, rows_weight, out_weight,
    lines, sides, all_sides, cot_packed, cot_other, relay_a,
    padded, columns, cots, cot_columns, interior, pieces, all_pieces,
    packed, packed_other, relay_b, shifted, partial_out, hits, sums, turned,
    load_sems, side_sems, swap_a_sems, swap_b_sems, piece_sems,
    *streams,
):
    tiles = 128
    place = tile, ch, core, y, xl, z = coords()
    C2 = feat.shape[2]
    C = 2 * C2
    near, far = x_neighbours(tile, ch, xl)
    bufs = len(REDUCE_BUFS)
    sems = len(REDUCE_SEMS)
    first, second, third = [
        Reduce(
            scale,
            streams[i * (bufs + sems) : i * (bufs + sems) + bufs],
            streams[i * (bufs + sems) + bufs : (i + 1) * (bufs + sems)],
            place,
        )
        for i in range(3)
    ]
    greeted = [dev(wrap(tile + o, tiles), ch) for o in OFFSETS] + [near, far, first.pair]
    greeted = greeted + first.outer_peers + first.inner_peers
    ready = pltpu.get_barrier_semaphore()
    for where in greeted:
        pl.semaphore_signal(ready, inc=1, device_id=where, device_id_type=MESH)

    own_rows = pl.ds(pl.multiple_of(ch * C2, 64), C2)
    loads = [
        pltpu.make_async_copy(a, b, load_sems.at[i])
        for i, (a, b) in enumerate(
            (
                (feat_in, feat),
                (cot_in, cot),
                (edge_tiles_in, edge_tiles),
                (edge_turns_in, edge_turns),
                (corner_tiles_in, corner_tiles),
                (corner_turns_in, corner_turns),
                (weight_in, weight),
                (weight_in.at[:, own_rows], rows_weight),
            )
        )
    ]
    for load in loads[:6]:
        load.start()

    loads[0].wait()

    def take_columns(row, carry):
        x = feat[row].astype(F32)
        lines[0, pl.ds(row, 1)] = x[0:1]
        lines[1, pl.ds(row, 1)] = x[S - 1 : S]
        return carry

    lax.fori_loop(0, S, take_columns, 0, unroll=4)
    sides[0] = pack(feat[0])
    sides[1] = pack(lines[1].astype(BF))
    sides[2] = pack(feat[S - 1])
    sides[3] = pack(lines[0].astype(BF))
    loads[1].wait()

    def pack_cot(row, carry):
        for i in range(4):
            cot_packed[row, 16 * i : 16 * i + 16] = pack(cot[4 * row + i])
        return carry

    lax.fori_loop(0, S // 4, pack_cot, 0)
    pl.semaphore_wait(ready, len(greeted))
    swap_a = Swap(cot_packed, cot_other, relay_a, swap_a_sems, tile, ch, xl)
    swap_a.start()
    side_copies = near_copies(sides, all_sides, side_sems, tile, ch, tiles)
    for copy in side_copies:
        copy.start()
    for load in loads[6:]:
        load.start()

    zero = jnp.zeros((S, C), BF)
    for part in range(3):
        for row in (0, 1, S + 2, S + 3):
            cots[part, row] = zero
    cot_columns[...] = jnp.zeros_like(cot_columns)
    nothing = jnp.zeros((1, C2), F32)

    def fill(read, lanes):
        def shift(row, carry):
            x = read(row).astype(F32)
            spread_columns(cots, row + 2, lanes, x, nothing, nothing)
            cot_columns[0, pl.ds(row + 2, 1), lanes] = x[0:1]
            cot_columns[1, pl.ds(row + 2, 1), lanes] = x[S - 1 : S]
            return carry

        lax.fori_loop(0, S, shift, 0, unroll=8)

    def read_other(row):
        at = pl.multiple_of(lax.rem(row, 4) * 16, 16)
        return unpack(cot_other[row // 4, pl.ds(at, 16)])

    pl.when(ch == 0)(lambda: fill(lambda row: cot[row], slice(0, C2)))
    pl.when(ch == 1)(lambda: fill(lambda row: cot[row], slice(C2, C)))
    swap_a.relay()

    for i in range(2, 6):
        loads[i].wait()
    for copy in side_copies:
        copy.wait_recv()
    halos = []
    for border in range(4):
        source = source_slot(edge_tiles[border, tile], tile, tiles)
        slot = lookup(EDGE_TABLE, border, edge_turns[border, tile])
        rev = slot // 4
        x = unpack(all_sides[source, slot - 4 * rev])
        ii = iota2((S, 1), 0)
        hot = one_hot_rows(S, jnp.where(rev == 1, S - 1 - ii, ii), S)
        halos.append(jnp.dot(hot, x, preferred_element_type=F32))
    columns[0, 1 : S + 1] = halos[3]
    columns[1, 1 : S + 1] = halos[1]
    for corner in range(4):
        source = source_slot(corner_tiles[corner, tile], tile, tiles)
        slot = lookup(CORNER_TABLE, corner, corner_turns[corner, tile])
        cells = unpack(all_sides[source, jnp.where(slot < 2, 0, 2)]).astype(F32)
        start = (slot == 0) | (slot == 3)
        at = 0 if corner < 2 else S + 1
        columns[(0, 1, 1, 0)[corner], at : at + 1] = jnp.where(start, cells[0:1], cells[S - 1 : S])
    padded[1, 0] = halos[0].astype(BF)
    padded[1, S + 1] = halos[2].astype(BF)
    padded[1, 1 : S + 1] = feat[...]

    def shift_features(row, carry):
        x = padded[1, row].astype(F32)
        spread_columns(
            padded, row, slice(0, C2), x, columns[0, pl.ds(row, 1)], columns[1, pl.ds(row, 1)]
        )
        return carry

    lax.fori_loop(0, S + 2, shift_features, 0, unroll=17)
    for b in range(3):
        turned[b * C2 : (b + 1) * C2] = padded[b].reshape((S + 2) * S, C2).T
    filled = 9 * (C2 // 2)

    def weight_grad(parts, lanes):
        width = 128 * len(parts)
        for stream in parts:
            stream.grads[:, filled:] = jnp.zeros((2, 8 * CHUNK - filled, 128), F32)

        def products(order):
            for step, a in enumerate(order):
                full = cots[1, 2 - a : 2 - a + S + 2, :, lanes].reshape((S + 2) * S, width)
                result = jnp.dot(turned[...], full, preferred_element_type=F32)
                for i, stream in enumerate(parts):
                    for half in range(2):
                        low = max(half * filled, 3 * a * C2)
                        high = min((half + 1) * filled, 3 * (a + 1) * C2)
                        if low < high:
                            stream.grads[half, low - half * filled : high - half * filled] = result[
                                low - 3 * a * C2 : high - 3 * a * C2, 128 * i : 128 * (i + 1)
                            ]
                    if step < 2:
                        stream.start(step, order[0])

        pl.when(core == 1)(lambda: products((0, 1, 2)))
        pl.when(core == 0)(lambda: products((2, 1, 0)))

    lanes = [pl.ds(pl.multiple_of(at, 128), 128) for at in (256 * ch, 128 - 128 * ch, 256 - 128 * ch)]
    weight_grad([first], lanes[0])
    for copy in swap_a.second:
        copy.wait_recv()

    def place_other(lanes):
        def one_row(row, carry):
            cots[1, row + 2, :, lanes] = read_other(row)
            return carry

        lax.fori_loop(0, S, one_row, 0, unroll=8)

    pl.when(ch == 0)(lambda: place_other(slice(C2, C)))
    pl.when(ch == 1)(lambda: place_other(slice(0, C2)))
    first.to_outer()
    weight_grad([second, third], pl.ds(pl.multiple_of(128 - 128 * ch, 128), 256))
    second.to_outer()
    third.to_outer()

    def pack_padded(row, carry):
        packed[row // 5, lax.rem(row, 5)] = pack(padded[1, row])
        return carry

    lax.fori_loop(0, S + 2, pack_padded, 0, unroll=2)
    packed[6, 4] = pack(columns[0, 1 : S + 1].astype(BF))
    packed[7, 0] = pack(columns[1, 1 : S + 1].astype(BF))
    io = iota2((16, C2), 0)
    ends = jnp.zeros((16, C2), F32)
    for corner in range(4):
        at = 0 if corner < 2 else S + 1
        ends = jnp.where(io == corner, columns[(0, 1, 1, 0)[corner], at : at + 1], ends)
    packed[7, 1] = pack(jnp.concatenate([ends, ends], axis=0).astype(BF))
    for i in range(2, 5):
        packed[7, i] = jnp.zeros((16, C), BF)
    swap_b = Swap(packed, packed_other, relay_b, swap_b_sems, tile, ch, xl)
    swap_b.start()

    pl.when(ch == 0)(lambda: fill(read_other, slice(C2, C)))
    pl.when(ch == 1)(lambda: fill(read_other, slice(0, C2)))

    first.to_inner()
    loads[7].wait()
    half = (S + 2) // 2

    def feature_grad(block, carry):
        total = None
        for a in range(3):
            for b in range(3):
                window = cots[2 - b, pl.ds(block * half + 2 - a, half)].reshape(half * S, C)
                term = lax.dot_general(window, rows_weight[3 * a + b], NT, preferred_element_type=F32)
                total = term if total is None else total + term
        interior[pl.ds(block * half, half)] = total.reshape(half, S, C2)
        return carry

    lax.fori_loop(0, 2, feature_grad, 0)
    pieces[0] = pack(interior[0].astype(BF))
    pieces[2] = pack(interior[S + 1].astype(BF))
    tips = []
    for side in range(2):
        total = None
        for a in range(3):
            line = cot_columns[side, 2 - a : 2 - a + 40].astype(BF)
            term = lax.dot_general(line, rows_weight[3 * a + 2 * side], NT, preferred_element_type=F32)
            total = term if total is None else total + term
        cot_columns[side, 0:40, 0:C2] = total
        pieces[3 - 2 * side] = pack(cot_columns[side, 1 : S + 1, 0:C2].astype(BF))
        tips.append((total[0:1], total[S + 1 : S + 2]))
    io = iota2((16, C2), 0)
    ends = jnp.zeros((16, C2), F32)
    for corner, value in enumerate((tips[0][0], tips[1][0], tips[1][1], tips[0][1])):
        ends = jnp.where(io == corner, value, ends)
    pieces[4] = pack(jnp.concatenate([ends, ends], axis=0).astype(BF))
    loads[6].wait()

    def pick_weight(tap, carry):
        for part in range(2):
            input_half = ch if part == 0 else 1 - ch
            w = weight[tap, pl.ds(pl.multiple_of(input_half * C2, 64), C2)].astype(F32)
            out_weight[part, tap] = jnp.where(ch == 0, w[:, :C2], w[:, C2:]).astype(BF)
        return carry

    lax.fori_loop(0, 9, pick_weight, 0)
    second.to_inner()
    third.to_inner()
    piece_copies = near_copies(pieces, all_pieces, piece_sems, tile, ch, tiles)
    for copy in piece_copies:
        copy.start()

    first.to_gather()
    swap_b.relay(0, 4)

    rows = S // 2

    def convolve_own(block, carry):
        total = None
        for a in range(3):
            for b in range(3):
                window = padded[b, pl.ds(block * rows + a, rows)].reshape(rows * S, C2)
                term = jnp.dot(window, out_weight[0, 3 * a + b], preferred_element_type=F32)
                total = term if total is None else total + term
        partial_out[pl.ds(block * rows, rows)] = total.reshape(rows, S, C2)
        return carry

    lax.fori_loop(0, 2, convolve_own, 0)
    swap_b.relay(4, 6)
    second.to_gather()
    swap_b.relay(6)
    third.to_gather()

    for offset in OFFSETS:
        k = slot_of(-offset)
        source = wrap(tile - offset, tiles)
        for border in range(4):
            hit = edge_tiles[border, source] == tile
            slot = lookup(EDGE_TABLE, border, edge_turns[border, source])
            rev = slot // 4
            ii = iota2((S, 1), 0)
            target = jnp.where(rev == 1, S - 1 - ii, ii) + (slot - 4 * rev) * S
            hot = one_hot_rows(S, jnp.where(hit, target, -1), 4 * S)
            hits[0, k, border] = hot[:16]
            hits[1, k, border] = hot[16:]
        ii = iota2((16, 1), 0)
        target = jnp.full((16, 1), -1, jnp.int32)
        for corner in range(4):
            hit = corner_tiles[corner, source] == tile
            slot = lookup(CORNER_TABLE, corner, corner_turns[corner, source])
            cell = jnp.where(slot < 2, 0, 2 * S) + jnp.where((slot == 0) | (slot == 3), 0, S - 1)
            target = jnp.where((ii == corner) & hit, cell, target)
        hits[0, k, 4] = one_hot_rows(16, target, 4 * S)
        hits[1, k, 4] = jnp.zeros((16, 4 * S), BF)

    first.to_back()
    second.to_back()
    third.to_back()
    first.pass_back()
    second.pass_back()
    third.pass_back()

    for copy in swap_b.second:
        copy.wait_recv()
    columns[0, 1 : S + 1] = unpack(packed_other[6, 4]).astype(F32)
    columns[1, 1 : S + 1] = unpack(packed_other[7, 0]).astype(F32)
    ends = unpack(packed_other[7, 1]).astype(F32)
    for corner in range(4):
        at = 0 if corner < 2 else S + 1
        columns[(0, 1, 1, 0)[corner], at : at + 1] = ends[corner : corner + 1]

    def shift_partner(row, carry):
        x = unpack(packed_other[row // 5, lax.rem(row, 5)]).astype(F32)
        spread_columns(
            shifted, row, slice(0, C2), x, columns[0, pl.ds(row, 1)], columns[1, pl.ds(row, 1)]
        )
        return carry

    lax.fori_loop(0, S + 2, shift_partner, 0, unroll=2)
    for copy in piece_copies:
        copy.wait_recv()

    flat = all_pieces[...].reshape(8 * 5 * 16, C)
    parts = [
        lax.dot_general(hits[i].reshape(8 * 5 * 16, 4 * S), flat, TN, preferred_element_type=F32)
        for i in range(2)
    ]
    low = jnp.concatenate([parts[0][:, :128], parts[0][:, 256:320]], axis=1)
    high = jnp.concatenate([parts[1][:, 128:256], parts[1][:, 320:]], axis=1)
    sums[...] = (low + high).reshape(4, S, C2)
    def add_sides(row, carry):
        io = iota2((S, C2), 0)
        x = interior[row + 1]
        x = x + jnp.where(io == 0, sums[3, pl.ds(row, 1)], 0.0)
        x = x + jnp.where(io == S - 1, sums[1, pl.ds(row, 1)], 0.0)
        x = x + jnp.where(row == 0, sums[0], 0.0)
        x = x + jnp.where(row == S - 1, sums[2], 0.0)
        grad_features[0, row] = x.astype(BF)
        return carry

    lax.fori_loop(0, S, add_sides, 0, unroll=2)

    def convolve_other(block, carry):
        total = partial_out[pl.ds(block * rows, rows)].reshape(rows * S, C2)
        for a in range(3):
            for b in range(3):
                window = shifted[b, pl.ds(block * rows + a, rows)].reshape(rows * S, C2)
                total = total + jnp.dot(window, out_weight[1, 3 * a + b], preferred_element_type=F32)
        output[0, pl.ds(block * rows, rows)] = total.reshape(rows, S, C2).astype(BF)
        return carry

    lax.fori_loop(0, 2, convolve_other, 0)
    first.to_pair()
    second.to_pair()
    third.to_pair()
    for stream, spot in zip((first, second, third), lanes):
        stream.store(grad_weight, core, spot)
    for stream, spot in zip((first, second, third), lanes):
        stream.finish_pair()
        stream.store(grad_weight, 1 - core, spot)
    swap_a.finish_sends()
    swap_b.finish_sends()
    for copy in side_copies + piece_copies:
        copy.wait_send()
    for stream in (first, second, third):
        stream.finish()


def publish_kernel(a, b, c, a_out, b_out, c_out, sems):
    copies = [
        pltpu.make_async_copy(src, dst, sems.at[i])
        for i, (src, dst) in enumerate(
            [(c.at[pl.ds(k * 432, 432)], c_out.at[pl.ds(k * 432, 432)]) for k in range(4)]
            + [(a, a_out), (b, b_out)]
        )
    ]
    for copy in copies:
        copy.start()
    for copy in copies:
        copy.wait()


VSPEC = pl.BlockSpec(memory_space=VM)
ANY = pl.BlockSpec(memory_space=pltpu.HBM)
DMA = pltpu.SemaphoreType.DMA
SM = pltpu.SMEM
REDUCE_BUFS = [
    ((2, 8 * CHUNK), F32),
    ((8, CHUNK), F32),
    ((7, CHUNK), BF),
    ((7, CHUNK), BF),
    ((7, UNIT), F32),
    ((7, UNIT), F32),
    ((2, 8, 7, UNIT), BF),
]
REDUCE_SEMS = [(2, 8), (2, 7), (2, 7), (2, 7), (2, 7), (2, 8)]


def reduce_scratch(width):
    return [VM(lead + (width,), kind) for lead, kind in REDUCE_BUFS] + [DMA(lead) for lead in REDUCE_SEMS]


def body(features, weight, cotangent, edge_tiles, edge_turns, corner_tiles, corner_turns):
    C2 = features.shape[3]
    C = 2 * C2
    shape = jax.ShapeDtypeStruct
    table = SM((4, 128), jnp.int32)
    output, grad_features, grad_weight = pl.pallas_call(
        lambda *refs: fused_kernel(1.0 / math.sqrt(128 * ROWS), *refs),
        name="fused",
        out_shape=(
            shape((1, S, S, C2), BF),
            shape((1, S, S, C2), BF),
            shape((9 * C2, C), F32),
        ),
        in_specs=[ANY] * 7,
        out_specs=(VSPEC,) * 3,
        scratch_shapes=[
            table, table, table, table,
            VM((S, S, C2), BF),
            VM((S, S, C2), BF),
            VM((9, C, C), BF),
            VM((9, C2, C), BF),
            VM((2, 9, C2, C2), BF),
            VM((2, S, C2), F32),
            VM((4, 16, C), BF),
            VM((8, 4, 16, C), BF),
            VM((8, 64, C), BF),
            VM((8, 64, C), BF),
            VM((2, 4, 64, C), BF),
            VM((3, S + 2, S, C2), BF),
            VM((2, 40, C2), F32),
            VM((3, S + 4, S, C), BF),
            VM((2, 48, C), F32),
            VM((S + 2, S, C2), F32),
            VM((5, 16, C), BF),
            VM((8, 5, 16, C), BF),
            VM((8, 5, 16, C), BF),
            VM((8, 5, 16, C), BF),
            VM((2, 4, 5, 16, C), BF),
            VM((3, S + 2, S, C2), BF),
            VM((S, S, C2), F32),
            VM((2, 8, 5, 16, 4 * S), BF),
            VM((4, S, C2), F32),
            VM((3 * C2, (S + 2) * S), BF),
            DMA((8,)),
            DMA((2, 8)),
            DMA((4, 8)),
            DMA((4, 8)),
            DMA((2, 8)),
        ]
        + reduce_scratch(128) * 3,
        compiler_params=pltpu.CompilerParams(
            vmem_limit_bytes=44 * 1024 * 1024, collective_id=0, has_side_effects=True
        ),
    )(
        *[pltpu.with_memory_space_constraint(x.T, pltpu.HBM) for x in (edge_tiles, edge_turns, corner_tiles, corner_turns)],
        *[pltpu.with_memory_space_constraint(x, pltpu.HBM) for x in (features[0], cotangent[0], weight.reshape(9, C, C))],
    )

    output, grad_features, grad_weight = pl.pallas_call(
        publish_kernel,
        name="publish",
        out_shape=(shape((1, S, S, C2), BF), shape((1, S, S, C2), BF), shape((9 * C2, C), F32)),
        in_specs=[pl.BlockSpec(memory_space=pl.ANY)] * 3,
        out_specs=(ANY,) * 3,
        scratch_shapes=[DMA((6,))],
        compiler_params=pltpu.CompilerParams(vmem_limit_bytes=1024 * 1024),
    )(output, grad_features, grad_weight)
    return (output, grad_features, grad_weight.reshape(3, 3, C2, C))


def solution(mesh):
    return jax.shard_map(
        body,
        mesh=mesh,
        in_specs=(
            P("tile", None, None, "ch"),
            P(),
            P("tile", None, None, "ch"),
            P(),
            P(),
            P(),
            P(),
        ),
        out_specs=(
            P("tile", None, None, "ch"),
            P("tile", None, None, "ch"),
            P(None, None, "ch", None),
        ),
        check_vma=False,
    )
```
